128 devices in a mesh: grp: 8 (over y_lo, z), tok: 16 (over y_hi, x, core).
Axes of the slice: x: 4, y: 4 (y_hi: 2, y_lo: 2; y = y_hi * 2 + y_lo), z: 4, core: 2. Of those that a mesh axis runs over, the one named last changes fastest.
Arguments:
- hidden: bfloat16 [8, 2048, 4608], P('grp', 'tok'), may hold values from -40 to 40
- input_gain: float32 [4608], replicated, may hold values from 0.25 to 1.75
- w_query: bfloat16 [4608, 4096], P(None, 'tok'), may hold values from -4 to 4
- w_key: bfloat16 [4608, 2048], P(None, 'tok'), may hold values from -4 to 4
- w_value: bfloat16 [4608, 2048], P(None, 'tok'), may hold values from -0.09375 to 0.09375
- w_out: bfloat16 [4096, 4608], P('tok'), may hold values from -0.09375 to 0.09375
- post_gain: float32 [4608], replicated, may hold values from 0.25 to 1.75
- cache_keys: bfloat16 [64, 256, 2048], P('grp', None, 'tok'), may hold values from -6 to 46
- cache_values: bfloat16 [64, 256, 2048], P('grp', None, 'tok'), may hold values from -6 to 6
- page_table: int32 [8, 8], replicated, may hold values from 0 to 63, as said below
- stretch_request: int32 [8, 8], P('grp'), may hold values from 0 to 2, never falling along the last dimension, each value on 1 to 4 neighbouring positions
- recompute_ids: int32 [8, 204], P('grp'), may hold values from 0 to 2047, as said below
- query_counts: int32 [8, 3], P('grp'), may hold values from 1 to 1024, 1844 in all within a row
Outputs:
- output: bfloat16 [8, 2048, 4608], P('grp', 'tok')
The draws below stay inside these ranges and needn't reach their ends.
Inputs may be any that keep to these rules, and one draw needn't show every extreme that they name: `page_table`: row g lists the pages of group g's 8 stretch slots; page p is held by group p // 8; every page appears once, and the slots of a group take exactly one page from each group. `stretch_request`: each request of a group holds one or more consecutive slots, request numbers never fall along the slots, and one request holds (8 + 1) // 2 slots, none more. `recompute_ids`: each row holds 204 distinct cached tokens of the group (slot times 256 plus the token within the stretch) in rising order. `query_counts`: the counts of a group sum to 1844.
All inputs are finite; a program needn't handle non-finite values.
Results may differ from the reference program's by a relative error of at most 0.01.
Values may be sent and summed in bfloat16 or wider, within the bound.
A program may use at most 128 MiB of HBM per device.

```python
import math
import jax
import jax.numpy as jnp
import numpy as np
from jax import lax

D = 4608
HEADS = 32
KV_HEADS = 16
HEAD = 128
STRETCH = 256
REQ_G = 3
CH_G = 8
PAGES = 64
NEW_G = 2048
SEL_G = 204
Q_G = 1844
N_GRP = 8
N_TOK = 16


def shared_pattern(key):
    return jnp.clip(jax.random.normal(jax.random.fold_in(key, 9091), (D,), jnp.float32), -3.0, 3.0)


def head_marker(total_heads):
    return (jnp.arange(total_heads * HEAD) % HEAD == HEAD // 2 - 1).astype(jnp.float32)


def drawn_weight(key, salt, total_heads, lowest, highest):
    key_base, key_strength = jax.random.split(jax.random.fold_in(key, salt))
    base = jnp.clip(jax.random.normal(key_base, (D, total_heads * HEAD), jnp.float32), -6.0, 6.0) * D ** (-0.5)
    strength = jax.random.uniform(key_strength, (total_heads,), jnp.float32, lowest, highest)
    per_column = jnp.repeat(strength, HEAD) * head_marker(total_heads)
    return (base + shared_pattern(key)[:, None] * per_column[None, :] / D).astype(jnp.bfloat16)


def draw_hidden(key, part):
    key_base, key_rows, key_cols, key_amp = jax.random.split(jax.random.fold_in(key, 101), 4)
    shape_all = (N_GRP, NEW_G, D)
    entries = jnp.clip(jax.random.normal(key_base, shape_all, jnp.float32), -4.0, 4.0)
    row_scale = jnp.exp(jax.random.uniform(key_rows, (N_GRP, NEW_G, 1), jnp.float32, math.log(0.2), math.log(2.0)))
    col_scale = jnp.exp(jax.random.uniform(key_cols, (D,), jnp.float32, math.log(0.3), math.log(3.0)))
    amplitude = jax.random.uniform(key_amp, (N_GRP, NEW_G, 1), jnp.float32, 1.0, 2.0)
    mixed = entries * col_scale[None, None, :] + amplitude * shared_pattern(key)[None, None, :]
    return (mixed * row_scale).astype(jnp.bfloat16)


def draw_w_query(key, part):
    return drawn_weight(key, 202, HEADS, 35.0, 55.0)


def draw_w_key(key, part):
    return drawn_weight(key, 303, KV_HEADS, 25.0, 50.0)


def draw_cache_keys(key, part):
    key_base, key_lift = jax.random.split(jax.random.fold_in(key, 404))
    shape_all = (PAGES, STRETCH, KV_HEADS * HEAD)
    entries = jnp.clip(jax.random.normal(key_base, shape_all, jnp.float32), -6.0, 6.0)
    lift = jax.random.uniform(key_lift, shape_all, jnp.float32, 15.0, 40.0)
    return (entries + lift * head_marker(KV_HEADS)[None, None, :]).astype(jnp.bfloat16)


def draw_page_table(key, part):
    key_cols, key_rows, key_owner, key_local = jax.random.split(key, 4)
    col_perm = jax.random.permutation(key_cols, N_GRP)
    row_perm = jax.random.permutation(key_rows, N_GRP)
    owner_perm = jax.random.permutation(key_owner, N_GRP)
    owner = owner_perm[(col_perm[None, :] + row_perm[:, None]) % N_GRP]
    local_perm = jax.vmap(lambda single: jax.random.permutation(single, CH_G))(jax.random.split(key_local, N_GRP))
    group_ids = jnp.broadcast_to(jnp.arange(N_GRP)[:, None], (N_GRP, CH_G))
    local_page = local_perm[owner, group_ids]
    return (owner * CH_G + local_page).astype(jnp.int32)


def draw_recompute_ids(key, part):
    span = CH_G * STRETCH

    def free_row(single):
        picked = jax.random.permutation(single, span)[:SEL_G]
        return jnp.sort(picked.astype(jnp.int32))

    def bounded_row(single):
        middle = (jax.random.permutation(single, span - 2)[:SEL_G - 2] + 1).astype(jnp.int32)
        picked = jnp.concatenate([jnp.zeros((1,), jnp.int32), middle, jnp.full((1,), span - 1, jnp.int32)])
        return jnp.sort(picked)
    row_keys = jax.random.split(key, N_GRP)
    loose = jax.vmap(free_row)(row_keys)
    ended = jax.vmap(bounded_row)(row_keys)
    first_row = (jnp.arange(N_GRP) == 0)[:, None]
    return jnp.where(first_row, ended, loose).astype(jnp.int32)


def levels(rng, extent, shards, least, top_value):
    def one(position, parts):
        steps = jax.random.uniform(jax.random.fold_in(jax.random.fold_in(rng, 6), position), (parts,), jnp.float32, least / len(shards), top_value / len(shards))
        return jnp.repeat(jnp.exp(steps), extent[position] // parts).reshape((-1,) + (1,) * (len(extent) - position - 1))

    factor_of = one(*shards[0])
    for cut in shards[1:]:
        factor_of = factor_of * one(*cut)
    return factor_of


def length_profile(amount, total, reach, lean):
    weights = [(1 << 20) // math.isqrt(standing ** lean) + 1 for standing in range(2, amount + 1)]
    spare, given = total - reach - (amount - 1), [1] * (amount - 1)
    while spare > 0:
        movable = [i for i in range(amount - 1) if given[i] < reach]
        mass, left = sum([weights[i] for i in movable]), spare
        for i in movable:
            more = min(reach - given[i], max(1, left * weights[i] // mass), spare)
            given[i] = given[i] + more
            spare = spare - more
    return np.array([reach] + given)


def ragged(own_key, number_of, total, reach, skew):
    if number_of == 2:
        one = jax.random.randint(own_key, (), max(1, total - reach), min(reach, total - 1) + 1)
        return jnp.stack([one, total - one])
    tallies = jnp.asarray(length_profile(number_of, total, reach, skew), jnp.int32)
    pairs = (number_of - 1) // 2
    donor, sink = tallies[1:1 + 2 * pairs:2], tallies[2:2 + 2 * pairs:2]
    room = jnp.minimum(donor - 1, reach - sink)
    passed = jax.random.randint(jax.random.fold_in(own_key, 1), (pairs,), 0, 1 << 20) % (room + 1)
    tallies = tallies.at[1:1 + 2 * pairs:2].set(donor - passed).at[2:2 + 2 * pairs:2].set(sink + passed)
    return tallies[jax.random.permutation(jax.random.fold_in(own_key, 2), number_of)]


def noise(rng, shape, scale, reach, shards=(), kind=jnp.bfloat16):
    factor_of = levels(rng, shape, shards, -0.22, 0.18) if shards else 1.0
    array = jax.random.normal(rng, shape, jnp.float32) * scale * factor_of
    return jnp.minimum(jnp.maximum(array, -reach), reach).astype(kind)


def setup_inputs(seed: int = 0) -> dict:
    keys = jax.random.split(jax.random.key(seed), 14)
    return {
        "hidden": draw_hidden(jax.random.fold_in(keys[13], 71), 0),
        "input_gain": jnp.clip(1.0 + 0.15 * jax.random.normal(keys[1], (D,), jnp.float32), 0.25, 1.75),
        "w_query": draw_w_query(jax.random.fold_in(keys[13], 71), 0),
        "w_key": draw_w_key(jax.random.fold_in(keys[13], 71), 0),
        "w_value": noise(keys[4], (D, KV_HEADS * HEAD), D ** -0.5, 0.09375, ((1, 16),)),
        "w_out": noise(keys[5], (HEADS * HEAD, D), (HEADS * HEAD) ** -0.5, 0.09375, ((0, 16),)),
        "post_gain": jnp.clip(1.0 + 0.15 * jax.random.normal(keys[6], (D,), jnp.float32), 0.25, 1.75),
        "cache_keys": draw_cache_keys(jax.random.fold_in(keys[13], 71), 0),
        "cache_values": noise(keys[8], (PAGES, STRETCH, KV_HEADS * HEAD), 1.0, 6.0, ((0, 8), (2, 16))),
        "page_table": draw_page_table(jax.random.fold_in(keys[13], 71), 0),
        "stretch_request": jax.vmap(lambda own: jnp.searchsorted(jnp.cumsum(ragged(own, REQ_G, CH_G, (CH_G + 1) // 2, 1)), jnp.arange(CH_G), side="right"))(jax.random.split(keys[10], N_GRP)).reshape((N_GRP, CH_G)).astype(jnp.int32),
        "recompute_ids": draw_recompute_ids(jax.random.fold_in(keys[13], 71), 0),
        "query_counts": jax.vmap(lambda own: ragged(own, REQ_G, Q_G, NEW_G // 2, 2))(jax.random.split(keys[12], N_GRP)).reshape((N_GRP, REQ_G)).astype(jnp.int32),
    }


EPSILON = 1e-06
CAP_VALUE = 50.0
QUERY_SCALE = 1.0 / 12.0
ROPE_BASE = 10000.0

def rotate(tensor, positions):
    halfway = tensor.shape[-1] // 2
    ladder = jnp.arange(halfway).astype(jnp.float32)
    frequency = jnp.exp(ladder * (-2.0 * math.log(ROPE_BASE) / tensor.shape[-1]))
    angles = positions.astype(jnp.float32)[:, None] * frequency[None, :]
    cosine = jnp.cos(angles)[:, None, :]
    sine_values = jnp.sin(angles)[:, None, :]
    front_part = tensor[..., :halfway]
    back_part = tensor[..., halfway:]
    return jnp.concatenate([front_part * cosine - back_part * sine_values, back_part * cosine + front_part * sine_values], axis=-1)

def request_layout(stretch_owner, counts_row, selected, stretch_len, new_rows):
    slot_total = stretch_owner.shape[0]
    requests = counts_row.shape[0]
    request_ids = jnp.arange(requests, dtype=jnp.int32)
    slot_ids = jnp.arange(slot_total, dtype=jnp.int32)
    belongs = (stretch_owner[:, None] == request_ids[None, :]).astype(jnp.int32)
    first_slot = lax.optimization_barrier(jnp.sum((stretch_owner[None, :] < request_ids[:, None]).astype(jnp.int32), axis=1)).astype(jnp.int32)
    stretch_count = lax.optimization_barrier(jnp.sum(belongs, axis=0)).astype(jnp.int32)
    offsets = ((slot_ids - lax.optimization_barrier(jnp.sum(belongs * first_slot[None, :], axis=1)).astype(jnp.int32)) * stretch_len).astype(jnp.int32)
    inner_ids = jnp.arange(stretch_len, dtype=jnp.int32)
    cache_pos = (offsets[:, None] + inner_ids[None, :]).reshape(-1)
    cache_req = jnp.broadcast_to(stretch_owner[:, None], (slot_total, stretch_len)).reshape(-1)
    cache_ids = jnp.arange(slot_total * stretch_len, dtype=jnp.int32)
    chosen = lax.optimization_barrier(jnp.sum((selected[:, None] == cache_ids[None, :]).astype(jnp.int32), axis=0))
    cache_live = chosen == 0
    home_slot = ((selected // stretch_len)[:, None] == slot_ids[None, :]).astype(jnp.int32)
    select_req = lax.optimization_barrier(jnp.sum(home_slot * stretch_owner[None, :], axis=1)).astype(jnp.int32)
    select_pos = (lax.optimization_barrier(jnp.sum(home_slot * offsets[None, :], axis=1)) + selected % stretch_len).astype(jnp.int32)
    query_total = new_rows - selected.shape[0]
    query_ids = jnp.arange(query_total, dtype=jnp.int32)
    query_start = (jnp.cumsum(counts_row) - counts_row).astype(jnp.int32)
    query_req = lax.optimization_barrier(jnp.sum((query_ids[:, None] >= query_start[None, 1:]).astype(jnp.int32), axis=1)).astype(jnp.int32)
    mapping = (query_req[:, None] == request_ids[None, :]).astype(jnp.int32)
    query_pos = (lax.optimization_barrier(jnp.sum(mapping * (stretch_count * stretch_len - query_start)[None, :], axis=1)) + query_ids).astype(jnp.int32)
    row_req = jnp.concatenate([select_req, query_req])
    row_pos = jnp.concatenate([select_pos, query_pos])
    key_req = jnp.concatenate([cache_req, row_req])
    key_pos = jnp.concatenate([cache_pos, row_pos])
    key_live = jnp.concatenate([cache_live, jnp.ones((new_rows,), dtype=bool)])
    return (offsets, row_req, row_pos, key_req, key_pos, key_live)

def attend(queries, all_keys, all_values, row_req, row_pos, key_req, key_pos, key_live):
    scores = jnp.einsum('qcgd,kcd->cgqk', queries.astype(jnp.float32), all_keys.astype(jnp.float32))
    capped = CAP_VALUE * jnp.tanh(scores * (QUERY_SCALE / CAP_VALUE))
    visible = ((key_req[None, :] == row_req[:, None]) & (key_pos[None, :] <= row_pos[:, None]) & key_live[None, :]).astype(jnp.float32)
    weights = jnp.exp(capped) * visible[None, None]
    denominator = lax.optimization_barrier(jnp.sum(weights, axis=-1))
    rounded = weights.astype(jnp.bfloat16)
    weighted = jnp.einsum('cgqk,kcd->qcgd', rounded.astype(jnp.float32), all_values.astype(jnp.float32))
    result = weighted / jnp.transpose(denominator, (2, 0, 1))[..., None]
    return result.astype(jnp.bfloat16).reshape(queries.shape[0], -1)

def reference(hidden, input_gain, w_query, w_key, w_value, w_out, post_gain, cache_keys, cache_values, page_table, stretch_request, recompute_ids, query_counts):
    group_size = HEADS // KV_HEADS
    head_cols = HEADS * HEAD // N_TOK
    out_split = w_out.reshape(N_TOK, head_cols, D)
    block_rows = min(256, NEW_G)
    block_total = NEW_G // block_rows

    def one_group(operands):
        group_rows, group_pages, owners, selected, counts_row = operands
        widened = group_rows.astype(jnp.float32)
        normed = (widened * lax.rsqrt(lax.optimization_barrier(jnp.mean(widened * widened, axis=-1, keepdims=True)) + EPSILON) * input_gain.astype(jnp.float32)).astype(jnp.bfloat16)
        query_all = jnp.dot(normed, w_query, preferred_element_type=jnp.float32).reshape(NEW_G, HEADS, HEAD)
        key_new = jnp.dot(normed, w_key, preferred_element_type=jnp.float32).reshape(NEW_G, KV_HEADS, HEAD)
        value_new = jnp.dot(normed, w_value, preferred_element_type=jnp.float32).astype(jnp.bfloat16).reshape(NEW_G, KV_HEADS, HEAD)
        offsets, row_req, row_pos, key_req, key_pos, key_live = request_layout(owners, counts_row, selected, STRETCH, NEW_G)
        query_rot = rotate(query_all, row_pos).astype(jnp.bfloat16).reshape(NEW_G, KV_HEADS, group_size, HEAD)
        key_rot = rotate(key_new, row_pos).astype(jnp.bfloat16)
        shifts = jnp.broadcast_to(offsets[:, None], (CH_G, STRETCH)).reshape(-1)
        cached_k = cache_keys[group_pages].astype(jnp.float32).reshape(CH_G * STRETCH, KV_HEADS, HEAD)
        cached_k = rotate(cached_k, shifts).astype(jnp.bfloat16)
        cached_v = cache_values[group_pages].reshape(CH_G * STRETCH, KV_HEADS, HEAD)
        all_keys = jnp.concatenate([cached_k, key_rot], axis=0)
        all_values = jnp.concatenate([cached_v, value_new], axis=0)

        def one_block(bundle):
            return attend(bundle[0], all_keys, all_values, bundle[1], bundle[2], key_req, key_pos, key_live)
        attended = lax.map(one_block, (query_rot.reshape(block_total, block_rows, KV_HEADS, group_size, HEAD), row_req.reshape(block_total, block_rows), row_pos.reshape(block_total, block_rows)))
        pieces = attended.reshape(NEW_G, N_TOK, head_cols).transpose(1, 0, 2)

        def add_piece(running, bundle):
            partial_sum = jnp.dot(bundle[0], bundle[1], preferred_element_type=jnp.float32).astype(jnp.bfloat16)
            partial_sum = lax.optimization_barrier(partial_sum)
            return (running + partial_sum.astype(jnp.float32), None)
        summed, unused = lax.scan(add_piece, jnp.zeros((NEW_G, D), jnp.float32), (pieces, out_split))
        normal = summed * lax.rsqrt(lax.optimization_barrier(jnp.mean(summed * summed, axis=-1, keepdims=True)) + EPSILON) * post_gain.astype(jnp.float32)
        return (widened + normal).astype(jnp.bfloat16)
    return lax.map(one_group, (hidden, page_table, stretch_request, recompute_ids, query_counts))
```

```python
import math

import jax
import jax.numpy as jnp
from jax import lax
from jax.experimental import pallas as pl
from jax.experimental.pallas import tpu as pltpu
from jax.sharding import PartitionSpec as P

HEAD = 128
EPSILON = 1e-06
CAP_VALUE = 50.0
QUERY_SCALE = 1.0 / 12.0
ROPE_BASE = 10000.0
SPAN = 1 << 16
FAR = 1 << 30
BLOCK = 256


def angles_of(positions):
    halfway = HEAD // 2
    ladder = jnp.arange(halfway).astype(jnp.float32)
    frequency = jnp.exp(ladder * (-2.0 * math.log(ROPE_BASE) / HEAD))
    angles = positions.astype(jnp.float32)[:, None] * frequency[None, :]
    cosine = jnp.cos(angles)
    sine = jnp.sin(angles)
    return (
        jnp.concatenate([cosine, cosine], axis=1),
        jnp.concatenate([-sine, sine], axis=1),
    )


def turn(tensor, cosine, sine):
    halfway = HEAD // 2
    swapped = jnp.concatenate([tensor[..., halfway:], tensor[..., :halfway]], axis=-1)
    return tensor * cosine + swapped * sine


def normalize(matrix, gain):
    widened = matrix.astype(jnp.float32)
    return widened * lax.rsqrt(jnp.mean(widened * widened, axis=-1, keepdims=True) + EPSILON) * gain


def request_layout(owners, counts_row, selected, table_row, groups, stretch_len, new_rows):
    slots = owners.shape[0]
    requests = counts_row.shape[0]
    request_ids = jnp.arange(requests, dtype=jnp.int32)
    slot_ids = jnp.arange(slots, dtype=jnp.int32)
    belongs = (owners[:, None] == request_ids[None, :]).astype(jnp.int32)
    first_slot = jnp.sum((owners[None, :] < request_ids[:, None]).astype(jnp.int32), axis=1)
    stretch_count = jnp.sum(belongs, axis=0)
    offsets = (slot_ids - jnp.sum(belongs * first_slot[None, :], axis=1)) * stretch_len
    home = ((selected // stretch_len)[:, None] == slot_ids[None, :]).astype(jnp.int32)
    select_req = jnp.sum(home * owners[None, :], axis=1)
    select_pos = jnp.sum(home * offsets[None, :], axis=1) + selected % stretch_len
    query_ids = jnp.arange(new_rows - selected.shape[0], dtype=jnp.int32)
    query_start = jnp.cumsum(counts_row) - counts_row
    query_req = jnp.sum((query_ids[:, None] >= query_start[None, 1:]).astype(jnp.int32), axis=1)
    mapping = (query_req[:, None] == request_ids[None, :]).astype(jnp.int32)
    query_pos = (
        jnp.sum(mapping * (stretch_count * stretch_len - query_start)[None, :], axis=1) + query_ids
    )
    row_req = jnp.concatenate([select_req, query_req])
    row_pos = jnp.concatenate([select_pos, query_pos])
    source = table_row // groups[1]
    place = (source[None, :] == jnp.arange(groups[0], dtype=jnp.int32)[:, None]).astype(jnp.int32)
    slot_of = jnp.sum(place * slot_ids[None, :], axis=1)
    shift_of = jnp.sum(place * offsets[None, :], axis=1)
    owner_of = jnp.sum(place * owners[None, :], axis=1)
    inner = jnp.arange(stretch_len, dtype=jnp.int32)
    cached_id = slot_of[:, None] * stretch_len + inner[None, :]
    cached_code = owner_of[:, None] * SPAN + shift_of[:, None] + inner[None, :]
    dead = jnp.any(cached_id.reshape(-1)[:, None] == selected[None, :], axis=1)
    row_code = row_req * SPAN + row_pos
    key_code = jnp.concatenate([cached_code.reshape(-1), row_code])
    live = jnp.concatenate([~dead, jnp.ones((new_rows,), bool)])
    return shift_of, row_req, row_pos, row_code, key_code, live


def attention_kernel(
    active, q_ref, k_ref, v_ref, pk_ref, pv_ref, pcos_ref, psin_ref, rcode_ref, kcode_ref,
    live_ref, out_ref, keys, values, queries, total,
):
    rows = q_ref.shape[0]
    cached = pk_ref.shape[0]
    blocks = rows // BLOCK
    for s in range(cached // BLOCK):
        part = pl.ds(s * BLOCK, BLOCK)
        page = pk_ref[part, :].astype(jnp.float32)
        turned = page * pcos_ref[s : s + 1, :] + pltpu.roll(page, HEAD // 2, 1) * psin_ref[s : s + 1, :]
        keys[part, :] = turned.astype(jnp.bfloat16)
        alive = live_ref[part, :].astype(jnp.bfloat16)
        values[part, :HEAD] = pv_ref[part, :] * alive
        values[part, HEAD:] = jnp.broadcast_to(alive, (BLOCK, HEAD))
    keys[pl.ds(cached, rows), :] = k_ref[...]
    values[pl.ds(cached, rows), :HEAD] = v_ref[...]
    values[pl.ds(cached, rows), HEAD:] = jnp.ones((rows, HEAD), jnp.bfloat16)

    def row_block(rb, carry):
        here = pl.ds(pl.multiple_of(rb * BLOCK, BLOCK), BLOCK)
        queries[:BLOCK, :] = q_ref[here, :HEAD]
        queries[BLOCK:, :] = q_ref[here, HEAD:]
        total[...] = jnp.zeros_like(total)
        code = rcode_ref[here, :]
        base = (code // SPAN) * SPAN

        def key_block(kb, inner_carry):
            @pl.when(active[rb, kb] > 0)
            def _():
                there = pl.ds(pl.multiple_of(kb * BLOCK, BLOCK), BLOCK)
                scores = lax.dot_general(
                    queries[...], keys[there, :], (((1,), (1,)), ((), ())),
                    preferred_element_type=jnp.float32,
                )
                capped = jnp.tanh(scores * (QUERY_SCALE / CAP_VALUE))
                weights = jnp.exp2(capped * (CAP_VALUE * math.log2(math.e)))
                kcode = kcode_ref[pl.ds(kb, 1), 0, :]
                seen = (kcode <= code) & (kcode >= base)
                both = jnp.concatenate([seen, seen], axis=0)
                rounded = jnp.where(both, weights, 0.0).astype(jnp.bfloat16)
                total[...] += jnp.dot(rounded, values[there, :], preferred_element_type=jnp.float32)

            return inner_carry

        lax.fori_loop(0, kcode_ref.shape[0], key_block, 0)
        result = total[:, :HEAD] / total[:, HEAD:]
        out_ref[here, :HEAD] = result[:BLOCK].astype(jnp.bfloat16)
        out_ref[here, HEAD:] = result[BLOCK:].astype(jnp.bfloat16)
        return carry

    lax.fori_loop(0, blocks, row_block, 0)


def attention(q, k, v, page_k, page_v, pcos, psin, row_code, key_code, live):
    rows = q.shape[0]
    total_keys = key_code.shape[0]
    key_blocks = key_code.reshape(-1, BLOCK)
    row_blocks = row_code.reshape(-1, BLOCK)
    low = jnp.min(key_blocks, axis=1)
    high = jnp.max(key_blocks, axis=1)
    row_high = jnp.max(row_blocks, axis=1)
    row_low = (jnp.min(row_blocks, axis=1) // SPAN) * SPAN
    active = ((low[None, :] <= row_high[:, None]) & (high[None, :] >= row_low[:, None])).astype(
        jnp.int32
    )
    vmem = pl.BlockSpec(memory_space=pltpu.VMEM)
    return pl.pallas_call(
        attention_kernel,
        out_shape=jax.ShapeDtypeStruct((rows, q.shape[1]), jnp.bfloat16),
        in_specs=[pl.BlockSpec(memory_space=pltpu.SMEM)] + [vmem] * 10,
        out_specs=vmem,
        scratch_shapes=[
            pltpu.VMEM((total_keys, HEAD), jnp.bfloat16),
            pltpu.VMEM((total_keys, 2 * HEAD), jnp.bfloat16),
            pltpu.VMEM((2 * BLOCK, HEAD), jnp.bfloat16),
            pltpu.VMEM((2 * BLOCK, 2 * HEAD), jnp.float32),
        ],
        compiler_params=pltpu.CompilerParams(vmem_limit_bytes=40 << 20),
        name="attention",
    )(
        active, q, k, v, page_k, page_v, pcos, psin, row_code[:, None],
        jnp.where(live, key_code, FAR).reshape(-1, 1, BLOCK), live.astype(jnp.float32)[: page_k.shape[0], None],
    )


def on_device(
    hidden, input_gain, w_query, w_key, w_value, w_out, post_gain, cache_keys, cache_values,
    page_table, stretch_request, recompute_ids, query_counts,
):
    own_rows = hidden[0]
    tok_total = lax.axis_size("tok")
    groups = lax.axis_size("grp")
    new_rows = own_rows.shape[0] * tok_total
    pages, stretch_len = cache_keys.shape[:2]
    normed_own = normalize(own_rows, input_gain).astype(jnp.bfloat16)
    segment = lax.all_gather(normed_own, "tok", axis=0, tiled=True)
    group = lax.axis_index("grp")
    mine = page_table // pages == group
    local = jnp.sum(jnp.where(mine, page_table % pages, 0), axis=1)
    picks = (local[:, None] == jnp.arange(pages, dtype=jnp.int32)[None, :]).astype(jnp.bfloat16)
    both = jnp.concatenate([cache_keys, cache_values], axis=-1)
    send = jnp.einsum("gp,pkh->gkh", picks, both, preferred_element_type=jnp.float32).astype(
        jnp.bfloat16
    )
    got = lax.all_to_all(send, "grp", 0, 0, tiled=True)
    got = got.reshape(groups * stretch_len, 2 * HEAD)
    table_row = lax.dynamic_index_in_dim(page_table, group, 0, keepdims=False)
    shift_of, row_req, row_pos, row_code, key_code, live = request_layout(
        stretch_request[0], query_counts[0], recompute_ids[0], table_row, (groups, pages),
        stretch_len, new_rows,
    )
    pcos, psin = angles_of(shift_of)
    cosine, sine = angles_of(row_pos)
    q = jnp.dot(segment, w_query, preferred_element_type=jnp.float32)
    k = jnp.dot(segment, w_key, preferred_element_type=jnp.float32)
    v = jnp.dot(segment, w_value, preferred_element_type=jnp.float32)
    q = turn(q.reshape(new_rows, -1, HEAD), cosine[:, None], sine[:, None])
    q = q.astype(jnp.bfloat16).reshape(new_rows, -1)
    k = turn(k, cosine, sine).astype(jnp.bfloat16)
    attended = attention(
        q, k, v.astype(jnp.bfloat16), got[:, :HEAD], got[:, HEAD:], pcos, psin, row_code, key_code, live
    )
    summed = lax.psum_scatter(
        jnp.dot(attended, w_out, preferred_element_type=jnp.float32).astype(jnp.bfloat16),
        "tok",
        scatter_dimension=0,
        tiled=True,
    ).astype(jnp.float32)
    result = own_rows.astype(jnp.float32) + normalize(summed, post_gain)
    return result.astype(jnp.bfloat16)[None]


def solution(mesh):
    return jax.shard_map(
        on_device,
        mesh=mesh,
        in_specs=(
            P("grp", "tok", None), P(), P(None, "tok"), P(None, "tok"), P(None, "tok"),
            P("tok", None), P(), P("grp", None, "tok"), P("grp", None, "tok"), P(),
            P("grp", None), P("grp", None), P("grp", None),
        ),
        out_specs=P("grp", "tok", None),
        check_vma=False,
    )
```

```python
import math

import jax
import jax.numpy as jnp
from jax import lax
from jax.experimental import pallas as pl
from jax.experimental.pallas import tpu as pltpu
from jax.sharding import PartitionSpec as P

HEAD = 128
EPSILON = 1e-06
CAP_VALUE = 50.0
QUERY_SCALE = 1.0 / 12.0
ROPE_BASE = 10000.0
SPAN = 1 << 16
FAR = 1 << 30
BLOCK = 256


def angles_of(positions):
    halfway = HEAD // 2
    ladder = jnp.arange(halfway).astype(jnp.float32)
    frequency = jnp.exp(ladder * (-2.0 * math.log(ROPE_BASE) / HEAD))
    angles = positions.astype(jnp.float32)[:, None] * frequency[None, :]
    cosine = jnp.cos(angles)
    sine = jnp.sin(angles)
    return (
        jnp.concatenate([cosine, cosine], axis=1),
        jnp.concatenate([-sine, sine], axis=1),
    )


def turn(tensor, cosine, sine):
    halfway = HEAD // 2
    swapped = jnp.concatenate([tensor[..., halfway:], tensor[..., :halfway]], axis=-1)
    return tensor * cosine + swapped * sine


def normalize(matrix, gain):
    widened = matrix.astype(jnp.float32)
    return widened * lax.rsqrt(jnp.mean(widened * widened, axis=-1, keepdims=True) + EPSILON) * gain


def request_layout(owners, counts_row, selected, table_row, groups, stretch_len, new_rows):
    slots = owners.shape[0]
    requests = counts_row.shape[0]
    request_ids = jnp.arange(requests, dtype=jnp.int32)
    slot_ids = jnp.arange(slots, dtype=jnp.int32)
    belongs = (owners[:, None] == request_ids[None, :]).astype(jnp.int32)
    first_slot = jnp.sum((owners[None, :] < request_ids[:, None]).astype(jnp.int32), axis=1)
    stretch_count = jnp.sum(belongs, axis=0)
    offsets = (slot_ids - jnp.sum(belongs * first_slot[None, :], axis=1)) * stretch_len
    home = ((selected // stretch_len)[:, None] == slot_ids[None, :]).astype(jnp.int32)
    select_req = jnp.sum(home * owners[None, :], axis=1)
    select_pos = jnp.sum(home * offsets[None, :], axis=1) + selected % stretch_len
    query_ids = jnp.arange(new_rows - selected.shape[0], dtype=jnp.int32)
    query_start = jnp.cumsum(counts_row) - counts_row
    query_req = jnp.sum((query_ids[:, None] >= query_start[None, 1:]).astype(jnp.int32), axis=1)
    mapping = (query_req[:, None] == request_ids[None, :]).astype(jnp.int32)
    query_pos = (
        jnp.sum(mapping * (stretch_count * stretch_len - query_start)[None, :], axis=1) + query_ids
    )
    row_req = jnp.concatenate([select_req, query_req])
    row_pos = jnp.concatenate([select_pos, query_pos])
    source = table_row // groups[1]
    place = (source[None, :] == jnp.arange(groups[0], dtype=jnp.int32)[:, None]).astype(jnp.int32)
    slot_of = jnp.sum(place * slot_ids[None, :], axis=1)
    shift_of = jnp.sum(place * offsets[None, :], axis=1)
    owner_of = jnp.sum(place * owners[None, :], axis=1)
    inner = jnp.arange(stretch_len, dtype=jnp.int32)
    cached_id = slot_of[:, None] * stretch_len + inner[None, :]
    cached_code = owner_of[:, None] * SPAN + shift_of[:, None] + inner[None, :]
    dead = jnp.any(cached_id.reshape(-1)[:, None] == selected[None, :], axis=1)
    row_code = row_req * SPAN + row_pos
    key_code = jnp.concatenate([cached_code.reshape(-1), row_code])
    live = jnp.concatenate([~dead, jnp.ones((new_rows,), bool)])
    return shift_of, row_req, row_pos, row_code, key_code, live


def attention_kernel(
    active, q_ref, k_ref, v_ref, pk_ref, pv_ref, pcos_ref, psin_ref, rcode_ref, kcode_ref,
    live_ref, out_ref, keys, values, queries, total,
):
    rows = q_ref.shape[0]
    cached = pk_ref.shape[0]
    blocks = rows // BLOCK
    for s in range(cached // BLOCK):
        part = pl.ds(s * BLOCK, BLOCK)
        page = pk_ref[part, :].astype(jnp.float32)
        turned = page * pcos_ref[s : s + 1, :] + pltpu.roll(page, HEAD // 2, 1) * psin_ref[s : s + 1, :]
        keys[part, :] = turned.astype(jnp.bfloat16)
        alive = live_ref[part, :].astype(jnp.bfloat16)
        values[part, :HEAD] = pv_ref[part, :] * alive
        values[part, HEAD:] = jnp.broadcast_to(alive, (BLOCK, HEAD))
    keys[pl.ds(cached, rows), :] = k_ref[...]
    values[pl.ds(cached, rows), :HEAD] = v_ref[...]
    values[pl.ds(cached, rows), HEAD:] = jnp.ones((rows, HEAD), jnp.bfloat16)

    def row_block(rb, carry):
        here = pl.ds(pl.multiple_of(rb * BLOCK, BLOCK), BLOCK)
        queries[:BLOCK, :] = q_ref[here, :HEAD]
        queries[BLOCK:, :] = q_ref[here, HEAD:]
        total[...] = jnp.zeros_like(total)
        code = rcode_ref[here, :]
        base = (code // SPAN) * SPAN

        def key_block(kb, inner_carry):
            @pl.when(active[rb, kb] > 0)
            def _():
                there = pl.ds(pl.multiple_of(kb * BLOCK, BLOCK), BLOCK)
                scores = lax.dot_general(
                    queries[...], keys[there, :], (((1,), (1,)), ((), ())),
                    preferred_element_type=jnp.float32,
                )
                capped = jnp.tanh(scores * (QUERY_SCALE / CAP_VALUE))
                weights = jnp.exp2(capped * (CAP_VALUE * math.log2(math.e)))
                kcode = kcode_ref[pl.ds(kb, 1), 0, :]
                seen = (kcode <= code) & (kcode >= base)
                both = jnp.concatenate([seen, seen], axis=0)
                rounded = jnp.where(both, weights, 0.0).astype(jnp.bfloat16)
                total[...] += jnp.dot(rounded, values[there, :], preferred_element_type=jnp.float32)

            return inner_carry

        lax.fori_loop(0, kcode_ref.shape[0], key_block, 0)
        result = total[:, :HEAD] / total[:, HEAD:]
        out_ref[here, :HEAD] = result[:BLOCK].astype(jnp.bfloat16)
        out_ref[here, HEAD:] = result[BLOCK:].astype(jnp.bfloat16)
        return carry

    lax.fori_loop(0, blocks, row_block, 0)


def attention(q, k, v, page_k, page_v, pcos, psin, row_code, key_code, live):
    rows = q.shape[0]
    total_keys = key_code.shape[0]
    key_blocks = key_code.reshape(-1, BLOCK)
    row_blocks = row_code.reshape(-1, BLOCK)
    low = jnp.min(key_blocks, axis=1)
    high = jnp.max(key_blocks, axis=1)
    row_high = jnp.max(row_blocks, axis=1)
    row_low = (jnp.min(row_blocks, axis=1) // SPAN) * SPAN
    active = ((low[None, :] <= row_high[:, None]) & (high[None, :] >= row_low[:, None])).astype(
        jnp.int32
    )
    vmem = pl.BlockSpec(memory_space=pltpu.VMEM)
    return pl.pallas_call(
        attention_kernel,
        out_shape=jax.ShapeDtypeStruct((rows, q.shape[1]), jnp.bfloat16),
        in_specs=[pl.BlockSpec(memory_space=pltpu.SMEM)] + [vmem] * 10,
        out_specs=vmem,
        scratch_shapes=[
            pltpu.VMEM((total_keys, HEAD), jnp.bfloat16),
            pltpu.VMEM((total_keys, 2 * HEAD), jnp.bfloat16),
            pltpu.VMEM((2 * BLOCK, HEAD), jnp.bfloat16),
            pltpu.VMEM((2 * BLOCK, 2 * HEAD), jnp.float32),
        ],
        compiler_params=pltpu.CompilerParams(vmem_limit_bytes=40 << 20),
        name="attention",
    )(
        active, q, k, v, page_k, page_v, pcos, psin, row_code[:, None],
        jnp.where(live, key_code, FAR).reshape(-1, 1, BLOCK), live.astype(jnp.float32)[: page_k.shape[0], None],
    )


MESH = pl.DeviceIdType.MESH
RINGS = 4
AROUND = 4


def place():
    tok = lax.axis_index("tok")
    return lax.axis_index("grp"), tok // 8, (tok // 2) % AROUND, tok % 2


def device(group, half, spot, core):
    return (group, half * 8 + lax.rem(spot + 2 * AROUND, AROUND) * 2 + core)


def greet(partners):
    barrier = pltpu.get_barrier_semaphore()
    for partner in partners:
        pl.semaphore_signal(barrier, inc=1, device_id=partner, device_id_type=MESH)
    pl.semaphore_wait(barrier, len(partners))


def project_kernel(
    attn_ref, w0_ref, w1_ref, hid_ref, gain_ref, out_ref,
    other, product, own, pair_out, pair_in, ring_out, ring_in, result,
    other_send, other_recv, pair_send, pair_recv, ring_send, ring_recv,
):
    group, half, spot, core = place()
    rows = hid_ref.shape[0]
    width = hid_ref.shape[1] // RINGS
    chunk = 2 * rows
    across = device(group, 1 - half, spot, core)
    sibling = device(group, half, spot, 1 - core)
    greet([across, sibling, device(group, half, spot + 1, core), device(group, half, spot - 1, core)])

    def other_copy(j):
        owner = lax.rem(spot + (3, 1, 2, 0)[j], AROUND)
        start = pl.multiple_of(((1 - half) * AROUND + owner) * chunk, chunk)
        return pltpu.make_async_remote_copy(
            src_ref=attn_ref.at[pl.ds(start, chunk)], dst_ref=other.at[j],
            send_sem=other_send.at[j], recv_sem=other_recv.at[j],
            device_id=across, device_id_type=MESH,
        )

    def pair_copy(s, r):
        return pltpu.make_async_remote_copy(
            src_ref=pair_out.at[s, r], dst_ref=pair_in.at[s, r],
            send_sem=pair_send.at[s, r], recv_sem=pair_recv.at[s, r],
            device_id=sibling, device_id_type=MESH,
        )

    def ring_copy(s, r):
        return pltpu.make_async_remote_copy(
            src_ref=ring_out.at[s, r], dst_ref=ring_in.at[s, r],
            send_sem=ring_send.at[s, r], recv_sem=ring_recv.at[s, r],
            device_id=device(group, half, spot + 1 - 2 * (r // 2), core), device_id_type=MESH,
        )

    for j in range(4):
        other_copy(j).start()

    def partial(s, r):
        owner = lax.rem(spot + (2 * (r // 2) - 1) * (1 + s) + 2 * AROUND, AROUND)
        slot = (r // 2, 2, 1 - r // 2, 3)[s]
        start = pl.multiple_of((half * AROUND + owner) * chunk, chunk)
        columns = pl.ds(pl.multiple_of(r * width, width), width)
        product[...] = jnp.dot(
            attn_ref[pl.ds(start, chunk), :], w0_ref[:, columns], preferred_element_type=jnp.float32
        ) + jnp.dot(other[slot], w1_ref[:, columns], preferred_element_type=jnp.float32)
        theirs = pl.ds(pl.multiple_of((1 - core) * rows, rows), rows)
        pair_out[s, r] = product[theirs, :].astype(jnp.bfloat16)
        pair_copy(s, r).start()
        own[s, r] = product[pl.ds(pl.multiple_of(core * rows, rows), rows), :]

    def partials(s, first, last):
        def step(r, carry):
            partial(s, r)
            return carry

        lax.fori_loop(first, last, step, 0)

    def forward(s):
        def step(r, carry):
            pair_copy(s, r).wait_recv()
            running = own[s, r] + pair_in[s, r].astype(jnp.float32)
            if s > 0:
                ring_copy(s - 1, r).wait_recv()
                running = running + ring_in[s - 1, r].astype(jnp.float32)
            if s < 3:
                ring_out[s, r] = running.astype(jnp.bfloat16)
                ring_copy(s, r).start()
            else:
                result[:, pl.ds(pl.multiple_of(r * width, width), width)] = running
            return carry

        for r in (0, 2, 1, 3):
            step(r, 0)

    other_copy(0).wait_recv()
    partials(0, 0, 2)
    other_copy(1).wait_recv()
    partials(0, 2, 4)
    forward(0)
    other_copy(2).wait_recv()
    partials(1, 0, 4)
    partials(2, 0, 4)
    other_copy(3).wait_recv()
    partials(3, 0, 4)
    forward(1)
    forward(2)
    forward(3)
    for j in range(4):
        other_copy(j).wait_send()

    def drain(r, carry):
        for s in range(4):
            pair_copy(s, r).wait_send()
        for s in range(3):
            ring_copy(s, r).wait_send()
        return carry

    lax.fori_loop(0, RINGS, drain, 0)
    projected = result[...]
    scale = lax.rsqrt(jnp.mean(projected * projected, axis=-1, keepdims=True) + EPSILON)
    out_ref[...] = (
        hid_ref[...].astype(jnp.float32) + projected * scale * gain_ref[...]
    ).astype(jnp.bfloat16)


def project(attended, w_own, w_across, own_rows, post_gain):
    rows, features = own_rows.shape
    width = features // RINGS
    vmem = pl.BlockSpec(memory_space=pltpu.VMEM)
    dma = pltpu.SemaphoreType.DMA
    return pl.pallas_call(
        project_kernel,
        out_shape=jax.ShapeDtypeStruct((rows, features), jnp.bfloat16),
        in_specs=[vmem] * 5,
        out_specs=vmem,
        scratch_shapes=[
            pltpu.VMEM((4, 2 * rows, attended.shape[1]), jnp.bfloat16),
            pltpu.VMEM((2 * rows, width), jnp.float32),
            pltpu.VMEM((4, RINGS, rows, width), jnp.float32),
            pltpu.VMEM((4, RINGS, rows, width), jnp.bfloat16),
            pltpu.VMEM((4, RINGS, rows, width), jnp.bfloat16),
            pltpu.VMEM((3, RINGS, rows, width), jnp.bfloat16),
            pltpu.VMEM((3, RINGS, rows, width), jnp.bfloat16),
            pltpu.VMEM((rows, features), jnp.float32),
            dma((4,)), dma((4,)), dma((4, RINGS)), dma((4, RINGS)), dma((3, RINGS)), dma((3, RINGS)),
        ],
        compiler_params=pltpu.CompilerParams(
            collective_id=1, has_side_effects=True, vmem_limit_bytes=56 << 20
        ),
        name="project",
    )(attended, w_own, w_across, own_rows, post_gain[None, :])


def on_device(
    hidden, input_gain, w_query, w_key, w_value, w_out, post_gain, cache_keys, cache_values,
    page_table, stretch_request, recompute_ids, query_counts,
):
    own_rows = hidden[0]
    tok_total = lax.axis_size("tok")
    groups = lax.axis_size("grp")
    new_rows = own_rows.shape[0] * tok_total
    pages, stretch_len = cache_keys.shape[:2]
    normed_own = normalize(own_rows, input_gain).astype(jnp.bfloat16)
    there = [
        ((g + groups // 2) % groups) * tok_total + (t + tok_total // 2) % tok_total
        for g in range(groups)
        for t in range(tok_total)
    ]
    w_across = lax.ppermute(w_out, ("grp", "tok"), list(enumerate(there)))
    segment = lax.all_gather(normed_own, "tok", axis=0, tiled=True)
    group = lax.axis_index("grp")
    mine = page_table // pages == group
    local = jnp.sum(jnp.where(mine, page_table % pages, 0), axis=1)
    picks = (local[:, None] == jnp.arange(pages, dtype=jnp.int32)[None, :]).astype(jnp.bfloat16)
    both = jnp.concatenate([cache_keys, cache_values], axis=-1)
    send = jnp.einsum("gp,pkh->gkh", picks, both, preferred_element_type=jnp.float32).astype(
        jnp.bfloat16
    )
    got = lax.all_to_all(send, "grp", 0, 0, tiled=True)
    got = got.reshape(groups * stretch_len, 2 * HEAD)
    table_row = lax.dynamic_index_in_dim(page_table, group, 0, keepdims=False)
    shift_of, row_req, row_pos, row_code, key_code, live = request_layout(
        stretch_request[0], query_counts[0], recompute_ids[0], table_row, (groups, pages),
        stretch_len, new_rows,
    )
    pcos, psin = angles_of(shift_of)
    cosine, sine = angles_of(row_pos)
    q = jnp.dot(segment, w_query, preferred_element_type=jnp.float32)
    k = jnp.dot(segment, w_key, preferred_element_type=jnp.float32)
    v = jnp.dot(segment, w_value, preferred_element_type=jnp.float32)
    q = turn(q.reshape(new_rows, -1, HEAD), cosine[:, None], sine[:, None])
    q = q.astype(jnp.bfloat16).reshape(new_rows, -1)
    k = turn(k, cosine, sine).astype(jnp.bfloat16)
    attended = attention(
        q, k, v.astype(jnp.bfloat16), got[:, :HEAD], got[:, HEAD:], pcos, psin, row_code, key_code, live
    )
    output = project(attended, w_out, w_across, own_rows, post_gain)
    return output[None]


def solution(mesh):
    return jax.shard_map(
        on_device,
        mesh=mesh,
        in_specs=(
            P("grp", "tok", None), P(), P(None, "tok"), P(None, "tok"), P(None, "tok"),
            P("tok", None), P(), P("grp", None, "tok"), P("grp", None, "tok"), P(),
            P("grp", None), P("grp", None), P("grp", None),
        ),
        out_specs=P("grp", "tok", None),
        check_vma=False,
    )
```

```python
import math

import jax
import jax.numpy as jnp
from jax import lax
from jax.experimental import pallas as pl
from jax.experimental.pallas import tpu as pltpu
from jax.sharding import PartitionSpec as P

HEAD = 128
EPSILON = 1e-06
CAP_VALUE = 50.0
QUERY_SCALE = 1.0 / 12.0
ROPE_BASE = 10000.0
SPAN = 1 << 16
FAR = 1 << 30
BLOCK = 256


def angles_of(positions):
    halfway = HEAD // 2
    ladder = jnp.arange(halfway).astype(jnp.float32)
    frequency = jnp.exp(ladder * (-2.0 * math.log(ROPE_BASE) / HEAD))
    angles = positions.astype(jnp.float32)[:, None] * frequency[None, :]
    cosine = jnp.cos(angles)
    sine = jnp.sin(angles)
    return (
        jnp.concatenate([cosine, cosine], axis=1),
        jnp.concatenate([-sine, sine], axis=1),
    )


def request_layout(owners, counts_row, selected, table_row, groups, stretch_len, new_rows):
    slots = owners.shape[0]
    requests = counts_row.shape[0]
    request_ids = jnp.arange(requests, dtype=jnp.int32)
    slot_ids = jnp.arange(slots, dtype=jnp.int32)
    belongs = (owners[:, None] == request_ids[None, :]).astype(jnp.int32)
    first_slot = jnp.sum((owners[None, :] < request_ids[:, None]).astype(jnp.int32), axis=1)
    stretch_count = jnp.sum(belongs, axis=0)
    offsets = (slot_ids - jnp.sum(belongs * first_slot[None, :], axis=1)) * stretch_len
    home = ((selected // stretch_len)[:, None] == slot_ids[None, :]).astype(jnp.int32)
    select_req = jnp.sum(home * owners[None, :], axis=1)
    select_pos = jnp.sum(home * offsets[None, :], axis=1) + selected % stretch_len
    query_ids = jnp.arange(new_rows - selected.shape[0], dtype=jnp.int32)
    query_start = jnp.cumsum(counts_row) - counts_row
    query_req = jnp.sum((query_ids[:, None] >= query_start[None, 1:]).astype(jnp.int32), axis=1)
    mapping = (query_req[:, None] == request_ids[None, :]).astype(jnp.int32)
    query_pos = (
        jnp.sum(mapping * (stretch_count * stretch_len - query_start)[None, :], axis=1) + query_ids
    )
    row_req = jnp.concatenate([select_req, query_req])
    row_pos = jnp.concatenate([select_pos, query_pos])
    source = table_row // groups[1]
    place = (source[None, :] == jnp.arange(groups[0], dtype=jnp.int32)[:, None]).astype(jnp.int32)
    slot_of = jnp.sum(place * slot_ids[None, :], axis=1)
    shift_of = jnp.sum(place * offsets[None, :], axis=1)
    owner_of = jnp.sum(place * owners[None, :], axis=1)
    inner = jnp.arange(stretch_len, dtype=jnp.int32)
    cached_id = slot_of[:, None] * stretch_len + inner[None, :]
    cached_code = owner_of[:, None] * SPAN + shift_of[:, None] + inner[None, :]
    dead = jnp.any(cached_id.reshape(-1)[:, None] == selected[None, :], axis=1)
    row_code = row_req * SPAN + row_pos
    key_code = jnp.concatenate([cached_code.reshape(-1), row_code])
    live = jnp.concatenate([~dead, jnp.ones((new_rows,), bool)])
    return shift_of, row_req, row_pos, row_code, key_code, live


def attention_kernel(
    active, heads_ref, pk_ref, pv_ref, pcos_ref, psin_ref, rcode_ref, kcode_ref,
    live_ref, out_ref, keys, values, queries, total,
):
    rows = heads_ref.shape[1]
    cached = pk_ref.shape[0]
    blocks = rows // BLOCK
    for s in range(cached // BLOCK):
        part = pl.ds(s * BLOCK, BLOCK)
        page = pk_ref[part, :].astype(jnp.float32)
        turned = page * pcos_ref[s : s + 1, :] + pltpu.roll(page, HEAD // 2, 1) * psin_ref[s : s + 1, :]
        keys[part, :] = turned.astype(jnp.bfloat16)
        alive = live_ref[part, :].astype(jnp.bfloat16)
        values[part, :HEAD] = pv_ref[part, :] * alive
        values[part, HEAD:] = jnp.broadcast_to(alive, (BLOCK, HEAD))
    keys[pl.ds(cached, rows), :] = heads_ref[2]
    values[pl.ds(cached, rows), :HEAD] = heads_ref[3]
    values[pl.ds(cached, rows), HEAD:] = jnp.ones((rows, HEAD), jnp.bfloat16)

    def row_block(rb, carry):
        here = pl.ds(pl.multiple_of(rb * BLOCK, BLOCK), BLOCK)
        queries[:BLOCK, :] = heads_ref[0, here, :]
        queries[BLOCK:, :] = heads_ref[1, here, :]
        total[...] = jnp.zeros_like(total)
        code = rcode_ref[here, :]
        base = (code // SPAN) * SPAN

        def key_block(kb, inner_carry):
            @pl.when(active[rb, kb] > 0)
            def _():
                there = pl.ds(pl.multiple_of(kb * BLOCK, BLOCK), BLOCK)
                scores = lax.dot_general(
                    queries[...], keys[there, :], (((1,), (1,)), ((), ())),
                    preferred_element_type=jnp.float32,
                )
                capped = jnp.tanh(scores * (QUERY_SCALE / CAP_VALUE))
                weights = jnp.exp2(capped * (CAP_VALUE * math.log2(math.e)))
                kcode = kcode_ref[pl.ds(kb, 1), 0, :]
                seen = (kcode <= code) & (kcode >= base)
                both = jnp.concatenate([seen, seen], axis=0)
                rounded = jnp.where(both, weights, 0.0).astype(jnp.bfloat16)
                total[...] += jnp.dot(rounded, values[there, :], preferred_element_type=jnp.float32)

            return inner_carry

        lax.fori_loop(0, kcode_ref.shape[0], key_block, 0)
        result = total[:, :HEAD] / total[:, HEAD:]
        out_ref[here, :HEAD] = result[:BLOCK].astype(jnp.bfloat16)
        out_ref[here, HEAD:] = result[BLOCK:].astype(jnp.bfloat16)
        return carry

    lax.fori_loop(0, blocks, row_block, 0)


def attention(heads, page_k, page_v, pcos, psin, row_code, key_code, live):
    rows = heads.shape[1]
    total_keys = key_code.shape[0]
    key_blocks = key_code.reshape(-1, BLOCK)
    row_blocks = row_code.reshape(-1, BLOCK)
    low = jnp.min(key_blocks, axis=1)
    high = jnp.max(key_blocks, axis=1)
    row_high = jnp.max(row_blocks, axis=1)
    row_low = (jnp.min(row_blocks, axis=1) // SPAN) * SPAN
    active = ((low[None, :] <= row_high[:, None]) & (high[None, :] >= row_low[:, None])).astype(
        jnp.int32
    )
    vmem = pl.BlockSpec(memory_space=pltpu.VMEM)
    return pl.pallas_call(
        attention_kernel,
        out_shape=jax.ShapeDtypeStruct((rows, 2 * HEAD), jnp.bfloat16),
        in_specs=[pl.BlockSpec(memory_space=pltpu.SMEM)] + [vmem] * 8,
        out_specs=vmem,
        scratch_shapes=[
            pltpu.VMEM((total_keys, HEAD), jnp.bfloat16),
            pltpu.VMEM((total_keys, 2 * HEAD), jnp.bfloat16),
            pltpu.VMEM((2 * BLOCK, HEAD), jnp.bfloat16),
            pltpu.VMEM((2 * BLOCK, 2 * HEAD), jnp.float32),
        ],
        compiler_params=pltpu.CompilerParams(vmem_limit_bytes=40 << 20),
        name="attention",
    )(
        active, heads, page_k, page_v, pcos, psin, row_code[:, None],
        jnp.where(live, key_code, FAR).reshape(-1, 1, BLOCK), live.astype(jnp.float32)[: page_k.shape[0], None],
    )


MESH = pl.DeviceIdType.MESH
RINGS = 4
AROUND = 4


def place():
    tok = lax.axis_index("tok")
    return lax.axis_index("grp"), tok // 8, (tok // 2) % AROUND, tok % 2


def device(group, half, spot, core):
    return (group, half * 8 + lax.rem(spot + 2 * AROUND, AROUND) * 2 + core)


def greet(partners):
    barrier = pltpu.get_barrier_semaphore()
    for partner in partners:
        pl.semaphore_signal(barrier, inc=1, device_id=partner, device_id_type=MESH)
    pl.semaphore_wait(barrier, len(partners))


def project_kernel(
    attn_ref, w0_ref, w1_ref, hid_ref, gain_ref, out_ref,
    other, product, own, pair_out, pair_in, ring_out, ring_in, result,
    other_send, other_recv, pair_send, pair_recv, ring_send, ring_recv,
):
    group, half, spot, core = place()
    rows = hid_ref.shape[0]
    width = hid_ref.shape[1] // RINGS
    chunk = 2 * rows
    across = device(group, 1 - half, spot, core)
    sibling = device(group, half, spot, 1 - core)
    greet([across, sibling, device(group, half, spot + 1, core), device(group, half, spot - 1, core)])

    def other_copy(j):
        owner = lax.rem(spot + (3, 1, 2, 0)[j], AROUND)
        start = pl.multiple_of(((1 - half) * AROUND + owner) * chunk, chunk)
        return pltpu.make_async_remote_copy(
            src_ref=attn_ref.at[pl.ds(start, chunk)], dst_ref=other.at[j],
            send_sem=other_send.at[j], recv_sem=other_recv.at[j],
            device_id=across, device_id_type=MESH,
        )

    def pair_copy(s, r):
        return pltpu.make_async_remote_copy(
            src_ref=pair_out.at[s, r], dst_ref=pair_in.at[s, r],
            send_sem=pair_send.at[s, r], recv_sem=pair_recv.at[s, r],
            device_id=sibling, device_id_type=MESH,
        )

    def ring_copy(s, r):
        return pltpu.make_async_remote_copy(
            src_ref=ring_out.at[s, r], dst_ref=ring_in.at[s, r],
            send_sem=ring_send.at[s, r], recv_sem=ring_recv.at[s, r],
            device_id=device(group, half, spot + 1 - 2 * (r // 2), core), device_id_type=MESH,
        )

    for j in range(4):
        other_copy(j).start()

    def partial(s, r):
        owner = lax.rem(spot + (2 * (r // 2) - 1) * (1 + s) + 2 * AROUND, AROUND)
        slot = (r // 2, 2, 1 - r // 2, 3)[s]
        start = pl.multiple_of((half * AROUND + owner) * chunk, chunk)
        columns = pl.ds(pl.multiple_of(r * width, width), width)
        product[...] = jnp.dot(
            attn_ref[pl.ds(start, chunk), :], w0_ref[:, columns], preferred_element_type=jnp.float32
        ) + jnp.dot(other[slot], w1_ref[:, columns], preferred_element_type=jnp.float32)
        theirs = pl.ds(pl.multiple_of((1 - core) * rows, rows), rows)
        pair_out[s, r] = product[theirs, :].astype(jnp.bfloat16)
        pair_copy(s, r).start()
        own[s, r] = product[pl.ds(pl.multiple_of(core * rows, rows), rows), :]

    def partials(s, first, last):
        def step(r, carry):
            partial(s, r)
            return carry

        lax.fori_loop(first, last, step, 0)

    def forward(s):
        def step(r, carry):
            pair_copy(s, r).wait_recv()
            running = own[s, r] + pair_in[s, r].astype(jnp.float32)
            if s > 0:
                ring_copy(s - 1, r).wait_recv()
                running = running + ring_in[s - 1, r].astype(jnp.float32)
            if s < 3:
                ring_out[s, r] = running.astype(jnp.bfloat16)
                ring_copy(s, r).start()
            else:
                result[:, pl.ds(pl.multiple_of(r * width, width), width)] = running
            return carry

        for r in (0, 2, 1, 3):
            step(r, 0)

    other_copy(0).wait_recv()
    partials(0, 0, 2)
    other_copy(1).wait_recv()
    partials(0, 2, 4)
    forward(0)
    other_copy(2).wait_recv()
    partials(1, 0, 4)
    partials(2, 0, 4)
    other_copy(3).wait_recv()
    partials(3, 0, 4)
    forward(1)
    forward(2)
    forward(3)
    for j in range(4):
        other_copy(j).wait_send()

    def drain(r, carry):
        for s in range(4):
            pair_copy(s, r).wait_send()
        for s in range(3):
            ring_copy(s, r).wait_send()
        return carry

    lax.fori_loop(0, RINGS, drain, 0)
    projected = result[...]
    scale = lax.rsqrt(jnp.mean(projected * projected, axis=-1, keepdims=True) + EPSILON)
    out_ref[...] = (
        hid_ref[...].astype(jnp.float32) + projected * scale * gain_ref[...]
    ).astype(jnp.bfloat16)


def project(attended, w_own, w_across, own_rows, post_gain):
    rows, features = own_rows.shape
    width = features // RINGS
    vmem = pl.BlockSpec(memory_space=pltpu.VMEM)
    dma = pltpu.SemaphoreType.DMA
    return pl.pallas_call(
        project_kernel,
        out_shape=jax.ShapeDtypeStruct((rows, features), jnp.bfloat16),
        in_specs=[vmem] * 5,
        out_specs=vmem,
        scratch_shapes=[
            pltpu.VMEM((4, 2 * rows, attended.shape[1]), jnp.bfloat16),
            pltpu.VMEM((2 * rows, width), jnp.float32),
            pltpu.VMEM((4, RINGS, rows, width), jnp.float32),
            pltpu.VMEM((4, RINGS, rows, width), jnp.bfloat16),
            pltpu.VMEM((4, RINGS, rows, width), jnp.bfloat16),
            pltpu.VMEM((3, RINGS, rows, width), jnp.bfloat16),
            pltpu.VMEM((3, RINGS, rows, width), jnp.bfloat16),
            pltpu.VMEM((rows, features), jnp.float32),
            dma((4,)), dma((4,)), dma((4, RINGS)), dma((4, RINGS)), dma((3, RINGS)), dma((3, RINGS)),
        ],
        compiler_params=pltpu.CompilerParams(
            collective_id=1, has_side_effects=True, vmem_limit_bytes=56 << 20
        ),
        name="project",
    )(attended, w_own, w_across, own_rows, post_gain[None, :])


def project_in_kernel(
    hid_ref, gain_ref, wq_ref, wk_ref, wv_ref, cos_ref, sin_ref, wo_ref,
    heads_ref, wo_across_ref,
    normed, weights, ship,
    x_send, x_recv, f_send, f_recv, s_send, s_recv, y_send, y_recv, z_send, z_recv,
    g_send, g_recv, o_send, o_recv, e_send, e_recv,
):
    group, half, spot, core = place()
    rows, features = hid_ref.shape
    depth = group % AROUND
    lows = group // AROUND
    quarter = features // 4
    out_rows, out_columns = wo_ref.shape
    strip = out_columns // (2 * AROUND) // HEAD * HEAD
    direct = out_columns - AROUND * strip

    def around(value):
        return lax.rem(value + 2 * AROUND, AROUND)

    xs = [device(group, half, spot + 1, core), device(group, half, spot - 1, core)]
    zs = [
        device(lows * AROUND + around(depth + 1), half, spot, core),
        device(lows * AROUND + around(depth - 1), half, spot, core),
    ]
    near = device((1 - lows) * AROUND + depth, 1 - half, spot, core)
    across = device(group, 1 - half, spot, core)
    sibling = device(group, half, spot, 1 - core)
    greet(xs + zs + [near, across, sibling])

    def copy(src, dst, send, recv, to):
        return pltpu.make_async_remote_copy(
            src_ref=src, dst_ref=dst, send_sem=send, recv_sem=recv, device_id=to, device_id_type=MESH
        )

    mine = pl.multiple_of(core * rows, rows)
    twin = pl.multiple_of((1 - core) * rows, rows)

    def block(owner, start=0, size=rows, base=mine):
        return normed.at[owner, pl.ds(pl.multiple_of(base + start, size), size)]

    def x_copy(d, owner=spot):
        return copy(block(owner), block(owner), x_send.at[d], x_recv.at[d], xs[d])

    def f_copy(d, owner):
        piece = block(owner, d * (rows // 2), rows // 2)
        return copy(piece, piece, f_send.at[d], f_recv.at[d], xs[d])

    def s_copy(i, owner, base=mine):
        piece = block(owner, base=base)
        return copy(piece, piece, s_send.at[i], s_recv.at[i], sibling)

    def slab(q, p):
        return weights.at[q, pl.ds(p * quarter, quarter)]

    def y_copy(p, src=None):
        return copy(
            slab(depth, p) if src is None else src, slab(depth, p), y_send.at[p], y_recv.at[p], near
        )

    def y_start(p):
        part = pl.ds(p * quarter, quarter)
        sources = [
            wq_ref.at[part, pl.ds(0, HEAD)], wq_ref.at[part, pl.ds(HEAD, HEAD)],
            wk_ref.at[part], wv_ref.at[part],
        ]
        for z, src in enumerate(sources):
            @pl.when(depth == z)
            def _(src=src):
                y_copy(p, src).start()

    def z_copy(d, p, q=depth):
        return copy(slab(q, p), slab(q, p), z_send.at[d, p], z_recv.at[d, p], zs[d])

    def g_copy(d, j, q):
        p = (0, 1)[j] if d == 0 else (2, 3)[j]
        return copy(slab(q, p), slab(q, p), g_send.at[d, j], g_recv.at[d, j], zs[d])

    def o_piece(q, start=0, size=out_rows):
        columns = pl.ds(pl.multiple_of(direct + q * strip, HEAD), strip)
        return pl.ds(start, size), columns

    def o_copy(i, src, index, to):
        return copy(src.at[index], wo_across_ref.at[index], o_send.at[i], o_recv.at[i], to)

    def table(ref, owner):
        start = pl.multiple_of((half * AROUND + owner) * 2 * rows, 2 * rows)
        return ref[pl.ds(start, 2 * rows), :]

    def turned(u, cosine, sine):
        return u * cosine + pltpu.roll(u, HEAD // 2, 1) * sine

    def own_heads(owner):
        source = normed[owner]
        cosine, sine = table(cos_ref, owner), table(sin_ref, owner)
        to = pl.ds(pl.multiple_of((half * AROUND + owner) * 2 * rows, 2 * rows), 2 * rows)
        q = jnp.dot(source, wq_ref[...], preferred_element_type=jnp.float32)
        heads_ref[0, to] = turned(q[:, :HEAD], cosine, sine).astype(jnp.bfloat16)
        heads_ref[1, to] = turned(q[:, HEAD:], cosine, sine).astype(jnp.bfloat16)
        k = jnp.dot(source, wk_ref[...], preferred_element_type=jnp.float32)
        heads_ref[2, to] = turned(k, cosine, sine).astype(jnp.bfloat16)
        v = jnp.dot(source, wv_ref[...], preferred_element_type=jnp.float32)
        heads_ref[3, to] = v.astype(jnp.bfloat16)

    def e_copy(i, b, owner, q):
        to = pl.ds(pl.multiple_of((half * AROUND + owner) * 2 * rows, 2 * rows), 2 * rows)
        return copy(ship.at[i, b], heads_ref.at[q, to], e_send.at[i, b], e_recv.at[i, b], across)

    owners = [spot, around(spot - 1), around(spot + 1), around(spot + 2)]
    quarters = [depth, around(depth - 1), around(depth + 1), around(depth + 2)]

    def their_heads(i, b):
        owner, q = owners[b], quarters[i]
        u = jnp.dot(normed[owner], weights[q], preferred_element_type=jnp.float32)
        plain = (q == 3).astype(jnp.float32)
        cosine, sine = table(cos_ref, owner), table(sin_ref, owner)
        cosine = cosine + plain * (1.0 - cosine)
        sine = sine * (1.0 - plain)
        ship[i, b] = turned(u, cosine, sine).astype(jnp.bfloat16)
        e_copy(i, b, owner, q).start()

    y_start(0)
    y_start(2)
    wide = hid_ref[...].astype(jnp.float32)
    scale = lax.rsqrt(jnp.mean(wide * wide, axis=-1, keepdims=True) + EPSILON)
    normed[spot, pl.ds(mine, rows)] = (wide * scale * gain_ref[...]).astype(jnp.bfloat16)
    x_copy(0).start()
    x_copy(1).start()
    s_copy(0, spot).start()
    s_copy(0, spot, twin).wait_recv()
    own_heads(spot)
    y_copy(0).wait_recv()
    z_copy(0, 0).start()
    z_copy(1, 0).start()
    y_start(1)
    y_copy(2).wait_recv()
    z_copy(0, 2).start()
    z_copy(1, 2).start()
    y_start(3)
    y_copy(1).wait_recv()
    z_copy(0, 1).start()
    z_copy(1, 1).start()
    below, above = quarters[1], quarters[2]
    z_copy(0, 0, below).wait_recv()
    g_copy(0, 0, below).start()
    z_copy(1, 2, above).wait_recv()
    g_copy(1, 0, above).start()
    y_copy(3).wait_recv()
    z_copy(0, 3).start()
    z_copy(1, 3).start()
    strip_own = o_piece(depth)
    o_copy(0, wo_ref, strip_own, near).start()
    straight = (pl.ds(0, out_rows), pl.ds(0, direct))
    o_copy(1, wo_ref, straight, near).start()
    left, right, far = owners[1], owners[2], owners[3]
    x_copy(0, left).wait_recv()
    f_copy(0, left).start()
    s_copy(1, left).start()
    x_copy(1, right).wait_recv()
    f_copy(1, right).start()
    s_copy(2, right).start()
    their_heads(0, 0)
    s_copy(1, left, twin).wait_recv()
    their_heads(0, 1)
    own_heads(left)
    z_copy(0, 1, below).wait_recv()
    g_copy(0, 1, below).start()
    s_copy(2, right, twin).wait_recv()
    their_heads(0, 2)
    own_heads(right)
    z_copy(1, 3, above).wait_recv()
    g_copy(1, 1, above).start()
    o_copy(0, wo_ref, strip_own, near).wait_recv()
    o_copy(2, wo_across_ref, strip_own, zs[0]).start()
    o_copy(3, wo_across_ref, strip_own, zs[1]).start()
    z_copy(0, 2, below).wait_recv()
    z_copy(0, 3, below).wait_recv()
    for b in range(3):
        their_heads(1, b)
    z_copy(1, 0, above).wait_recv()
    z_copy(1, 1, above).wait_recv()
    for b in range(3):
        their_heads(2, b)
    f_copy(0, far).wait_recv()
    f_copy(1, far).wait_recv()
    s_copy(3, far).start()
    s_copy(3, far, twin).wait_recv()
    for i in range(3):
        their_heads(i, 3)
    own_heads(far)
    o_copy(2, wo_across_ref, o_piece(below), zs[0]).wait_recv()
    o_copy(4, wo_across_ref, o_piece(below, 0, out_rows // 2), zs[0]).start()
    o_copy(3, wo_across_ref, o_piece(above), zs[1]).wait_recv()
    o_copy(5, wo_across_ref, o_piece(above, out_rows // 2, out_rows // 2), zs[1]).start()
    for d in range(2):
        for j in range(2):
            g_copy(d, j, quarters[3]).wait_recv()
    for b in range(4):
        their_heads(3, b)
    o_copy(1, wo_ref, straight, near).wait_recv()
    o_copy(4, wo_across_ref, o_piece(quarters[3], 0, out_rows // 2), zs[0]).wait_recv()
    o_copy(5, wo_across_ref, o_piece(quarters[3], out_rows // 2, out_rows // 2), zs[1]).wait_recv()
    for i in range(4):
        for b in range(4):
            to = pl.ds(
                pl.multiple_of(((1 - half) * AROUND + owners[b]) * 2 * rows, 2 * rows), 2 * rows
            )
            copy(
                ship.at[i, b], heads_ref.at[quarters[i], to], e_send.at[i, b], e_recv.at[i, b], across
            ).wait()
    for d in range(2):
        x_copy(d).wait_send()
        f_copy(d, owners[1 + d]).wait_send()
        for p in range(4):
            z_copy(d, p).wait_send()
        for j in range(2):
            g_copy(d, j, quarters[1 + d]).wait_send()
    for i in range(4):
        s_copy(i, owners[i]).wait_send()
    for p in range(4):
        y_copy(p).wait_send()
    o_copy(0, wo_ref, strip_own, near).wait_send()
    o_copy(1, wo_ref, straight, near).wait_send()
    o_copy(2, wo_across_ref, strip_own, zs[0]).wait_send()
    o_copy(3, wo_across_ref, strip_own, zs[1]).wait_send()
    o_copy(4, wo_across_ref, o_piece(below, 0, out_rows // 2), zs[0]).wait_send()
    o_copy(5, wo_across_ref, o_piece(above, out_rows // 2, out_rows // 2), zs[1]).wait_send()


def project_in(own_rows, gain, w_query, w_key, w_value, cosine, sine, w_out):
    rows, features = own_rows.shape
    vmem = pl.BlockSpec(memory_space=pltpu.VMEM)
    hbm = pl.BlockSpec(memory_space=pl.ANY)
    dma = pltpu.SemaphoreType.DMA
    pairs = [(2,), (2,), (4,), (4,), (2, 4), (2, 2), (6,), (4, 4)]
    return pl.pallas_call(
        project_in_kernel,
        out_shape=(
            jax.ShapeDtypeStruct((4, cosine.shape[0], HEAD), jnp.bfloat16),
            jax.ShapeDtypeStruct(w_out.shape, jnp.bfloat16),
        ),
        in_specs=[vmem] * 7 + [hbm],
        out_specs=(vmem, hbm),
        scratch_shapes=[
            pltpu.VMEM((AROUND, 2 * rows, features), jnp.bfloat16),
            pltpu.VMEM((4, features, HEAD), jnp.bfloat16),
            pltpu.VMEM((4, 4, 2 * rows, HEAD), jnp.bfloat16),
        ] + [dma(shape) for shape in pairs for _ in range(2)],
        compiler_params=pltpu.CompilerParams(
            collective_id=2, has_side_effects=True, vmem_limit_bytes=48 << 20
        ),
        name="project_in",
    )(own_rows, gain[None, :], w_query, w_key, w_value, cosine, sine, w_out)


def on_device(
    hidden, input_gain, w_query, w_key, w_value, w_out, post_gain, cache_keys, cache_values,
    page_table, stretch_request, recompute_ids, query_counts,
):
    own_rows = hidden[0]
    tok_total = lax.axis_size("tok")
    groups = lax.axis_size("grp")
    new_rows = own_rows.shape[0] * tok_total
    pages, stretch_len = cache_keys.shape[:2]
    group = lax.axis_index("grp")
    mine = page_table // pages == group
    local = jnp.sum(jnp.where(mine, page_table % pages, 0), axis=1)
    picks = (local[:, None] == jnp.arange(pages, dtype=jnp.int32)[None, :]).astype(jnp.bfloat16)
    both = jnp.concatenate([cache_keys, cache_values], axis=-1)
    send = jnp.einsum("gp,pkh->gkh", picks, both, preferred_element_type=jnp.float32).astype(
        jnp.bfloat16
    )
    got = lax.all_to_all(send, "grp", 0, 0, tiled=True)
    got = got.reshape(groups * stretch_len, 2 * HEAD)
    table_row = lax.dynamic_index_in_dim(page_table, group, 0, keepdims=False)
    shift_of, row_req, row_pos, row_code, key_code, live = request_layout(
        stretch_request[0], query_counts[0], recompute_ids[0], table_row, (groups, pages),
        stretch_len, new_rows,
    )
    pcos, psin = angles_of(shift_of)
    cosine, sine = angles_of(row_pos)
    heads, w_across = project_in(own_rows, input_gain, w_query, w_key, w_value, cosine, sine, w_out)
    attended = attention(
        heads, got[:, :HEAD], got[:, HEAD:], pcos, psin, row_code, key_code, live
    )
    output = project(attended, w_out, w_across, own_rows, post_gain)
    return output[None]


def solution(mesh):
    return jax.shard_map(
        on_device,
        mesh=mesh,
        in_specs=(
            P("grp", "tok", None), P(), P(None, "tok"), P(None, "tok"), P(None, "tok"),
            P("tok", None), P(), P("grp", None, "tok"), P("grp", None, "tok"), P(),
            P("grp", None), P("grp", None), P("grp", None),
        ),
        out_specs=P("grp", "tok", None),
        check_vma=False,
    )
```

```python
import math

import jax
import jax.numpy as jnp
from jax import lax
from jax.experimental import pallas as pl
from jax.experimental.pallas import tpu as pltpu
from jax.sharding import PartitionSpec as P

HEAD = 128
EPSILON = 1e-06
CAP_VALUE = 50.0
QUERY_SCALE = 1.0 / 12.0
ROPE_BASE = 10000.0
SPAN = 1 << 16
FAR = 1 << 30
BLOCK = 256


def angles_of(positions):
    halfway = HEAD // 2
    ladder = jnp.arange(halfway).astype(jnp.float32)
    frequency = jnp.exp(ladder * (-2.0 * math.log(ROPE_BASE) / HEAD))
    angles = positions.astype(jnp.float32)[:, None] * frequency[None, :]
    cosine = jnp.cos(angles)
    sine = jnp.sin(angles)
    return (
        jnp.concatenate([cosine, cosine], axis=1),
        jnp.concatenate([-sine, sine], axis=1),
    )


def request_layout(owners, counts_row, selected, table_row, groups, stretch_len, new_rows):
    slots = owners.shape[0]
    requests = counts_row.shape[0]
    request_ids = jnp.arange(requests, dtype=jnp.int32)
    slot_ids = jnp.arange(slots, dtype=jnp.int32)
    belongs = (owners[:, None] == request_ids[None, :]).astype(jnp.int32)
    first_slot = jnp.sum((owners[None, :] < request_ids[:, None]).astype(jnp.int32), axis=1)
    stretch_count = jnp.sum(belongs, axis=0)
    offsets = (slot_ids - jnp.sum(belongs * first_slot[None, :], axis=1)) * stretch_len
    home = ((selected // stretch_len)[:, None] == slot_ids[None, :]).astype(jnp.int32)
    select_req = jnp.sum(home * owners[None, :], axis=1)
    select_pos = jnp.sum(home * offsets[None, :], axis=1) + selected % stretch_len
    query_ids = jnp.arange(new_rows - selected.shape[0], dtype=jnp.int32)
    query_start = jnp.cumsum(counts_row) - counts_row
    query_req = jnp.sum((query_ids[:, None] >= query_start[None, 1:]).astype(jnp.int32), axis=1)
    mapping = (query_req[:, None] == request_ids[None, :]).astype(jnp.int32)
    query_pos = (
        jnp.sum(mapping * (stretch_count * stretch_len - query_start)[None, :], axis=1) + query_ids
    )
    row_req = jnp.concatenate([select_req, query_req])
    row_pos = jnp.concatenate([select_pos, query_pos])
    source = table_row // groups[1]
    place = (source[None, :] == jnp.arange(groups[0], dtype=jnp.int32)[:, None]).astype(jnp.int32)
    slot_of = jnp.sum(place * slot_ids[None, :], axis=1)
    shift_of = jnp.sum(place * offsets[None, :], axis=1)
    owner_of = jnp.sum(place * owners[None, :], axis=1)
    inner = jnp.arange(stretch_len, dtype=jnp.int32)
    cached_id = slot_of[:, None] * stretch_len + inner[None, :]
    cached_code = owner_of[:, None] * SPAN + shift_of[:, None] + inner[None, :]
    dead = jnp.any(cached_id.reshape(-1)[:, None] == selected[None, :], axis=1)
    row_code = row_req * SPAN + row_pos
    key_code = jnp.concatenate([cached_code.reshape(-1), row_code])
    live = jnp.concatenate([~dead, jnp.ones((new_rows,), bool)])
    return shift_of, row_req, row_pos, row_code, key_code, live


def attention_kernel(
    active, heads_ref, pk_ref, pv_ref, pcos_ref, psin_ref, rcode_ref, kcode_ref,
    live_ref, out_ref, keys, values, queries, total,
):
    rows = heads_ref.shape[1]
    cached = pk_ref.shape[0]
    blocks = rows // BLOCK
    for s in range(cached // BLOCK):
        part = pl.ds(s * BLOCK, BLOCK)
        page = pk_ref[part, :].astype(jnp.float32)
        turned = page * pcos_ref[s : s + 1, :] + pltpu.roll(page, HEAD // 2, 1) * psin_ref[s : s + 1, :]
        keys[part, :] = turned.astype(jnp.bfloat16)
        alive = live_ref[part, :].astype(jnp.bfloat16)
        values[part, :HEAD] = pv_ref[part, :] * alive
        values[part, HEAD:] = jnp.broadcast_to(alive, (BLOCK, HEAD))
    keys[pl.ds(cached, rows), :] = heads_ref[2]
    values[pl.ds(cached, rows), :HEAD] = heads_ref[3]
    values[pl.ds(cached, rows), HEAD:] = jnp.ones((rows, HEAD), jnp.bfloat16)

    def row_block(rb, carry):
        here = pl.ds(pl.multiple_of(rb * BLOCK, BLOCK), BLOCK)
        queries[:BLOCK, :] = heads_ref[0, here, :]
        queries[BLOCK:, :] = heads_ref[1, here, :]
        total[...] = jnp.zeros_like(total)
        code = rcode_ref[here, :]
        base = (code // SPAN) * SPAN

        def key_block(kb, inner_carry):
            @pl.when(active[rb, kb] > 0)
            def _():
                there = pl.ds(pl.multiple_of(kb * BLOCK, BLOCK), BLOCK)
                scores = lax.dot_general(
                    queries[...], keys[there, :], (((1,), (1,)), ((), ())),
                    preferred_element_type=jnp.float32,
                )
                capped = jnp.tanh(scores * (QUERY_SCALE / CAP_VALUE))
                weights = jnp.exp2(capped * (CAP_VALUE * math.log2(math.e)))
                kcode = kcode_ref[pl.ds(kb, 1), 0, :]
                seen = (kcode <= code) & (kcode >= base)
                both = jnp.concatenate([seen, seen], axis=0)
                rounded = jnp.where(both, weights, 0.0).astype(jnp.bfloat16)
                total[...] += jnp.dot(rounded, values[there, :], preferred_element_type=jnp.float32)

            return inner_carry

        lax.fori_loop(0, kcode_ref.shape[0], key_block, 0)
        result = total[:, :HEAD] / total[:, HEAD:]
        out_ref[here, :HEAD] = result[:BLOCK].astype(jnp.bfloat16)
        out_ref[here, HEAD:] = result[BLOCK:].astype(jnp.bfloat16)
        return carry

    lax.fori_loop(0, blocks, row_block, 0)


def attention(heads, page_k, page_v, pcos, psin, row_code, key_code, live):
    rows = heads.shape[1]
    total_keys = key_code.shape[0]
    key_blocks = key_code.reshape(-1, BLOCK)
    row_blocks = row_code.reshape(-1, BLOCK)
    low = jnp.min(key_blocks, axis=1)
    high = jnp.max(key_blocks, axis=1)
    row_high = jnp.max(row_blocks, axis=1)
    row_low = (jnp.min(row_blocks, axis=1) // SPAN) * SPAN
    active = ((low[None, :] <= row_high[:, None]) & (high[None, :] >= row_low[:, None])).astype(
        jnp.int32
    )
    vmem = pl.BlockSpec(memory_space=pltpu.VMEM)
    return pl.pallas_call(
        attention_kernel,
        out_shape=jax.ShapeDtypeStruct((rows, 2 * HEAD), jnp.bfloat16),
        in_specs=[pl.BlockSpec(memory_space=pltpu.SMEM)] + [vmem] * 8,
        out_specs=vmem,
        scratch_shapes=[
            pltpu.VMEM((total_keys, HEAD), jnp.bfloat16),
            pltpu.VMEM((total_keys, 2 * HEAD), jnp.bfloat16),
            pltpu.VMEM((2 * BLOCK, HEAD), jnp.bfloat16),
            pltpu.VMEM((2 * BLOCK, 2 * HEAD), jnp.float32),
        ],
        compiler_params=pltpu.CompilerParams(vmem_limit_bytes=40 << 20),
        name="attention",
    )(
        active, heads, page_k, page_v, pcos, psin, row_code[:, None],
        jnp.where(live, key_code, FAR).reshape(-1, 1, BLOCK), live.astype(jnp.float32)[: page_k.shape[0], None],
    )


MESH = pl.DeviceIdType.MESH
RINGS = 4
AROUND = 4


def place():
    tok = lax.axis_index("tok")
    return lax.axis_index("grp"), tok // 8, (tok // 2) % AROUND, tok % 2


def device(group, half, spot, core):
    return (group, half * 8 + lax.rem(spot + 2 * AROUND, AROUND) * 2 + core)


def greet(partners):
    barrier = pltpu.get_barrier_semaphore()
    for partner in partners:
        pl.semaphore_signal(barrier, inc=1, device_id=partner, device_id_type=MESH)
    pl.semaphore_wait(barrier, len(partners))


def project_kernel(
    attn_ref, w0_ref, w1_ref, hid_ref, gain_ref, out_ref,
    other, product, own, pair_out, pair_in, ring_out, ring_in, result,
    other_send, other_recv, pair_send, pair_recv, ring_send, ring_recv,
):
    group, half, spot, core = place()
    rows = hid_ref.shape[0]
    width = hid_ref.shape[1] // RINGS
    chunk = 2 * rows
    across = device(group, 1 - half, spot, core)
    sibling = device(group, half, spot, 1 - core)
    greet([across, sibling, device(group, half, spot + 1, core), device(group, half, spot - 1, core)])

    def other_copy(j):
        owner = lax.rem(spot + (3, 1, 2, 0)[j], AROUND)
        start = pl.multiple_of(((1 - half) * AROUND + owner) * chunk, chunk)
        return pltpu.make_async_remote_copy(
            src_ref=attn_ref.at[pl.ds(start, chunk)], dst_ref=other.at[j],
            send_sem=other_send.at[j], recv_sem=other_recv.at[j],
            device_id=across, device_id_type=MESH,
        )

    def pair_copy(s, r):
        return pltpu.make_async_remote_copy(
            src_ref=pair_out.at[s, r], dst_ref=pair_in.at[s, r],
            send_sem=pair_send.at[s, r], recv_sem=pair_recv.at[s, r],
            device_id=sibling, device_id_type=MESH,
        )

    def ring_copy(s, r):
        return pltpu.make_async_remote_copy(
            src_ref=ring_out.at[s, r], dst_ref=ring_in.at[s, r],
            send_sem=ring_send.at[s, r], recv_sem=ring_recv.at[s, r],
            device_id=device(group, half, spot + 1 - 2 * (r // 2), core), device_id_type=MESH,
        )

    for j in range(4):
        other_copy(j).start()

    def partial(s, r):
        owner = lax.rem(spot + (2 * (r // 2) - 1) * (1 + s) + 2 * AROUND, AROUND)
        slot = (r // 2, 2, 1 - r // 2, 3)[s]
        start = pl.multiple_of((half * AROUND + owner) * chunk, chunk)
        columns = pl.ds(pl.multiple_of(r * width, width), width)
        product[...] = jnp.dot(
            attn_ref[pl.ds(start, chunk), :], w0_ref[:, columns], preferred_element_type=jnp.float32
        ) + jnp.dot(other[slot], w1_ref[:, columns], preferred_element_type=jnp.float32)
        theirs = pl.ds(pl.multiple_of((1 - core) * rows, rows), rows)
        pair_out[s, r] = product[theirs, :].astype(jnp.bfloat16)
        pair_copy(s, r).start()
        own[s, r] = product[pl.ds(pl.multiple_of(core * rows, rows), rows), :]

    def partials(s, first, last):
        def step(r, carry):
            partial(s, r)
            return carry

        lax.fori_loop(first, last, step, 0)

    def forward(s):
        def step(r, carry):
            pair_copy(s, r).wait_recv()
            running = own[s, r] + pair_in[s, r].astype(jnp.float32)
            if s > 0:
                ring_copy(s - 1, r).wait_recv()
                running = running + ring_in[s - 1, r].astype(jnp.float32)
            if s < 3:
                ring_out[s, r] = running.astype(jnp.bfloat16)
                ring_copy(s, r).start()
            else:
                result[:, pl.ds(pl.multiple_of(r * width, width), width)] = running
            return carry

        for r in (0, 2, 1, 3):
            step(r, 0)

    other_copy(0).wait_recv()
    partials(0, 0, 2)
    other_copy(1).wait_recv()
    partials(0, 2, 4)
    forward(0)
    other_copy(2).wait_recv()
    partials(1, 0, 4)
    partials(2, 0, 4)
    other_copy(3).wait_recv()
    partials(3, 0, 4)
    forward(1)
    forward(2)
    forward(3)
    for j in range(4):
        other_copy(j).wait_send()

    def drain(r, carry):
        for s in range(4):
            pair_copy(s, r).wait_send()
        for s in range(3):
            ring_copy(s, r).wait_send()
        return carry

    lax.fori_loop(0, RINGS, drain, 0)
    projected = result[...]
    scale = lax.rsqrt(jnp.mean(projected * projected, axis=-1, keepdims=True) + EPSILON)
    out_ref[...] = (
        hid_ref[...].astype(jnp.float32) + projected * scale * gain_ref[...]
    ).astype(jnp.bfloat16)


def project(attended, w_own, w_across, own_rows, post_gain):
    rows, features = own_rows.shape
    width = features // RINGS
    vmem = pl.BlockSpec(memory_space=pltpu.VMEM)
    dma = pltpu.SemaphoreType.DMA
    return pl.pallas_call(
        project_kernel,
        out_shape=jax.ShapeDtypeStruct((rows, features), jnp.bfloat16),
        in_specs=[vmem] * 5,
        out_specs=vmem,
        scratch_shapes=[
            pltpu.VMEM((4, 2 * rows, attended.shape[1]), jnp.bfloat16),
            pltpu.VMEM((2 * rows, width), jnp.float32),
            pltpu.VMEM((4, RINGS, rows, width), jnp.float32),
            pltpu.VMEM((4, RINGS, rows, width), jnp.bfloat16),
            pltpu.VMEM((4, RINGS, rows, width), jnp.bfloat16),
            pltpu.VMEM((3, RINGS, rows, width), jnp.bfloat16),
            pltpu.VMEM((3, RINGS, rows, width), jnp.bfloat16),
            pltpu.VMEM((rows, features), jnp.float32),
            dma((4,)), dma((4,)), dma((4, RINGS)), dma((4, RINGS)), dma((3, RINGS)), dma((3, RINGS)),
        ],
        compiler_params=pltpu.CompilerParams(
            collective_id=1, has_side_effects=True, vmem_limit_bytes=56 << 20
        ),
        name="project",
    )(attended, w_own, w_across, own_rows, post_gain[None, :])


def project_in_kernel(
    hid_ref, gain_ref, wq_ref, wk_ref, wv_ref, cos_ref, sin_ref, wo_ref,
    heads_ref, wo_across_ref,
    normed, weights, ship,
    x_send, x_recv, f_send, f_recv, s_send, s_recv, y_send, y_recv, w_send, w_recv, z_send, z_recv,
    g_send, g_recv, o_send, o_recv, e_send, e_recv,
):
    group, half, spot, core = place()
    rows, features = hid_ref.shape
    depth = group % AROUND
    lows = group // AROUND
    quarter = features // 4
    out_quarter = wo_ref.shape[0] // 4

    def around(value):
        return lax.rem(value + 2 * AROUND, AROUND)

    xs = [device(group, half, spot + 1, core), device(group, half, spot - 1, core)]
    zs = [
        device(lows * AROUND + around(depth + 1), half, spot, core),
        device(lows * AROUND + around(depth - 1), half, spot, core),
    ]
    near = device((1 - lows) * AROUND + depth, 1 - half, spot, core)
    across = device(group, 1 - half, spot, core)
    beside = device((1 - lows) * AROUND + depth, half, spot, core)
    sibling = device(group, half, spot, 1 - core)
    greet(xs + zs + [near, across, beside, sibling])

    def copy(src, dst, send, recv, to):
        return pltpu.make_async_remote_copy(
            src_ref=src, dst_ref=dst, send_sem=send, recv_sem=recv, device_id=to, device_id_type=MESH
        )

    mine = pl.multiple_of(core * rows, rows)
    twin = pl.multiple_of((1 - core) * rows, rows)

    def block(owner, start=0, size=rows, base=mine):
        return normed.at[owner, pl.ds(pl.multiple_of(base + start, size), size)]

    def x_copy(d, owner=spot):
        return copy(block(owner), block(owner), x_send.at[d], x_recv.at[d], xs[d])

    def f_copy(d, owner):
        piece = block(owner, d * (rows // 2), rows // 2)
        return copy(piece, piece, f_send.at[d], f_recv.at[d], xs[d])

    def s_copy(i, owner, base=mine):
        piece = block(owner, base=base)
        return copy(piece, piece, s_send.at[i], s_recv.at[i], sibling)

    mine_first, theirs_first = 2 * lows, 2 * (1 - lows)

    def slab(q, p):
        return weights.at[q, pl.ds(pl.multiple_of(p * quarter, quarter), quarter)]

    def y_start(j):
        part = pl.ds(pl.multiple_of((theirs_first + j) * quarter, quarter), quarter)
        sources = [
            wq_ref.at[part, pl.ds(0, HEAD)], wq_ref.at[part, pl.ds(HEAD, HEAD)],
            wk_ref.at[part], wv_ref.at[part],
        ]
        for z, src in enumerate(sources):
            @pl.when(depth == z)
            def _(src=src):
                copy(src, slab(depth, theirs_first + j), y_send.at[j], y_recv.at[j], near).start()

    def y_done(j):
        piece = slab(depth, mine_first + j)
        return copy(piece, piece, y_send.at[j], y_recv.at[j], near)

    def w_copy(i, q, p):
        return copy(slab(q, p), slab(q, p), w_send.at[i], w_recv.at[i], beside)

    def nth_piece(n):
        return (mine_first if n < 2 else theirs_first) + n % 2

    def z_copy(d, n, q=depth):
        piece = slab(q, nth_piece(n))
        return copy(piece, piece, z_send.at[d, n], z_recv.at[d, n], zs[d])

    def g_copy(d, q):
        piece = slab(q, mine_first + d)
        return copy(piece, piece, g_send.at[d], g_recv.at[d], zs[d])

    def o_copy(i, src, q, n, to):
        size = out_quarter // 2
        part = pl.ds(pl.multiple_of(q * out_quarter + n * size, size), size)
        return copy(src.at[part], wo_across_ref.at[part], o_send.at[i], o_recv.at[i], to)

    def table(ref, owner):
        start = pl.multiple_of((half * AROUND + owner) * 2 * rows, 2 * rows)
        return ref[pl.ds(start, 2 * rows), :]

    def turned(u, cosine, sine):
        return u * cosine + pltpu.roll(u, HEAD // 2, 1) * sine

    def own_heads(owner):
        source = normed[owner]
        cosine, sine = table(cos_ref, owner), table(sin_ref, owner)
        to = pl.ds(pl.multiple_of((half * AROUND + owner) * 2 * rows, 2 * rows), 2 * rows)
        q = jnp.dot(source, wq_ref[...], preferred_element_type=jnp.float32)
        heads_ref[0, to] = turned(q[:, :HEAD], cosine, sine).astype(jnp.bfloat16)
        heads_ref[1, to] = turned(q[:, HEAD:], cosine, sine).astype(jnp.bfloat16)
        k = jnp.dot(source, wk_ref[...], preferred_element_type=jnp.float32)
        heads_ref[2, to] = turned(k, cosine, sine).astype(jnp.bfloat16)
        v = jnp.dot(source, wv_ref[...], preferred_element_type=jnp.float32)
        heads_ref[3, to] = v.astype(jnp.bfloat16)

    def e_copy(i, b, owner, q):
        to = pl.ds(pl.multiple_of((half * AROUND + owner) * 2 * rows, 2 * rows), 2 * rows)
        return copy(ship.at[i, b], heads_ref.at[q, to], e_send.at[i, b], e_recv.at[i, b], across)

    def nth(base, i):
        return around(base + (i * (7 - i)) // 2)

    owners = [nth(spot, b) for b in range(4)]
    quarters = [nth(depth, i) for i in range(4)]

    def their_heads(i, b):
        owner, q = nth(spot, b), nth(depth, i)
        u = jnp.dot(normed[owner], weights[q], preferred_element_type=jnp.float32)
        plain = (q == 3).astype(jnp.float32)
        cosine, sine = table(cos_ref, owner), table(sin_ref, owner)
        cosine = cosine + plain * (1.0 - cosine)
        sine = sine * (1.0 - plain)
        ship[i, b] = turned(u, cosine, sine).astype(jnp.bfloat16)
        e_copy(i, b, owner, q).start()

    def own_blocks(first, last):
        def step(b, carry):
            own_heads(nth(spot, b))
            return carry

        lax.fori_loop(first, last, step, 0)

    def their_blocks(i0, i1, b0, b1):
        def step(n, carry):
            their_heads(i0 + n // (b1 - b0), b0 + lax.rem(n, b1 - b0))
            return carry

        lax.fori_loop(0, (i1 - i0) * (b1 - b0), step, 0)

    left, right, far = owners[1], owners[2], owners[3]
    below, above, beyond = quarters[1], quarters[2], quarters[3]
    y_start(0)
    y_start(1)
    wide = hid_ref[...].astype(jnp.float32)
    scale = lax.rsqrt(jnp.mean(wide * wide, axis=-1, keepdims=True) + EPSILON)
    normed[spot, pl.ds(mine, rows)] = (wide * scale * gain_ref[...]).astype(jnp.bfloat16)
    x_copy(0).start()
    x_copy(1).start()
    s_copy(0, spot).start()
    for n in range(2):
        y_done(n).wait_recv()
        w_copy(n, depth, mine_first + n).start()
        z_copy(0, n).start()
        z_copy(1, n).start()
    o_copy(0, wo_ref, depth, 1 - lows, near).start()
    s_copy(0, spot, twin).wait_recv()
    own_blocks(0, 1)
    for n in range(2):
        w_copy(n, depth, theirs_first + n).wait_recv()
        z_copy(0, n + 2).start()
        z_copy(1, n + 2).start()
    their_blocks(0, 1, 0, 1)
    z_copy(0, 0, below).wait_recv()
    g_copy(0, below).start()
    z_copy(1, 1, above).wait_recv()
    g_copy(1, above).start()
    o_copy(0, wo_ref, depth, lows, near).wait_recv()
    o_copy(1, wo_across_ref, depth, lows, beside).start()
    x_copy(0, left).wait_recv()
    f_copy(0, left).start()
    s_copy(1, left).start()
    x_copy(1, right).wait_recv()
    f_copy(1, right).start()
    s_copy(2, right).start()
    s_copy(1, left, twin).wait_recv()
    s_copy(2, right, twin).wait_recv()
    their_blocks(0, 1, 1, 3)
    for n in range(1, 4):
        z_copy(0, n, below).wait_recv()
    for n in (0, 2, 3):
        z_copy(1, n, above).wait_recv()
    g_copy(0, beyond).wait_recv()
    w_copy(2, beyond, mine_first).start()
    g_copy(1, beyond).wait_recv()
    w_copy(3, beyond, mine_first + 1).start()
    o_copy(1, wo_across_ref, depth, 1 - lows, beside).wait_recv()
    for n in range(2):
        o_copy(2 + n, wo_across_ref, depth, n, zs[0]).start()
        o_copy(4 + n, wo_across_ref, depth, n, zs[1]).start()
    their_blocks(1, 3, 0, 3)
    own_blocks(1, 3)
    w_copy(2, beyond, theirs_first).wait_recv()
    w_copy(3, beyond, theirs_first + 1).wait_recv()
    their_blocks(3, 4, 0, 3)
    f_copy(0, far).wait_recv()
    f_copy(1, far).wait_recv()
    s_copy(3, far).start()
    s_copy(3, far, twin).wait_recv()
    their_blocks(0, 4, 3, 4)
    o_copy(2, wo_across_ref, below, 0, zs[0]).wait_recv()
    o_copy(6, wo_across_ref, below, 0, zs[0]).start()
    o_copy(5, wo_across_ref, above, 1, zs[1]).wait_recv()
    o_copy(7, wo_across_ref, above, 1, zs[1]).start()
    own_blocks(3, 4)
    o_copy(3, wo_across_ref, below, 1, zs[0]).wait_recv()
    o_copy(4, wo_across_ref, above, 0, zs[1]).wait_recv()
    o_copy(6, wo_across_ref, beyond, 0, zs[0]).wait_recv()
    o_copy(7, wo_across_ref, beyond, 1, zs[1]).wait_recv()
    for i in range(4):
        for b in range(4):
            to = pl.ds(
                pl.multiple_of(((1 - half) * AROUND + owners[b]) * 2 * rows, 2 * rows), 2 * rows
            )
            copy(
                ship.at[i, b], heads_ref.at[quarters[i], to], e_send.at[i, b], e_recv.at[i, b], across
            ).wait()
    for d in range(2):
        x_copy(d).wait_send()
        f_copy(d, owners[1 + d]).wait_send()
        for n in range(4):
            z_copy(d, n).wait_send()
        g_copy(d, quarters[1 + d]).wait_send()
    for i in range(4):
        s_copy(i, owners[i]).wait_send()
        w_copy(i, (depth, depth, beyond, beyond)[i], mine_first + i % 2).wait_send()
    for n in range(2):
        y_done(n).wait_send()
    for i in range(8):
        o_copy(i, wo_across_ref, depth, 0, near).wait_send()


def project_in(own_rows, gain, w_query, w_key, w_value, cosine, sine, w_out):
    rows, features = own_rows.shape
    vmem = pl.BlockSpec(memory_space=pltpu.VMEM)
    hbm = pl.BlockSpec(memory_space=pl.ANY)
    dma = pltpu.SemaphoreType.DMA
    pairs = [(2,), (2,), (4,), (2,), (4,), (2, 4), (2,), (8,), (4, 4)]
    return pl.pallas_call(
        project_in_kernel,
        out_shape=(
            jax.ShapeDtypeStruct((4, cosine.shape[0], HEAD), jnp.bfloat16),
            jax.ShapeDtypeStruct(w_out.shape, jnp.bfloat16),
        ),
        in_specs=[vmem] * 7 + [hbm],
        out_specs=(vmem, hbm),
        scratch_shapes=[
            pltpu.VMEM((AROUND, 2 * rows, features), jnp.bfloat16),
            pltpu.VMEM((4, features, HEAD), jnp.bfloat16),
            pltpu.VMEM((4, 4, 2 * rows, HEAD), jnp.bfloat16),
        ] + [dma(shape) for shape in pairs for _ in range(2)],
        compiler_params=pltpu.CompilerParams(
            collective_id=2, has_side_effects=True, vmem_limit_bytes=48 << 20
        ),
        name="project_in",
    )(own_rows, gain[None, :], w_query, w_key, w_value, cosine, sine, w_out)


def on_device(
    hidden, input_gain, w_query, w_key, w_value, w_out, post_gain, cache_keys, cache_values,
    page_table, stretch_request, recompute_ids, query_counts,
):
    own_rows = hidden[0]
    tok_total = lax.axis_size("tok")
    groups = lax.axis_size("grp")
    new_rows = own_rows.shape[0] * tok_total
    pages, stretch_len = cache_keys.shape[:2]
    group = lax.axis_index("grp")
    mine = page_table // pages == group
    local = jnp.sum(jnp.where(mine, page_table % pages, 0), axis=1)
    picks = (local[:, None] == jnp.arange(pages, dtype=jnp.int32)[None, :]).astype(jnp.bfloat16)
    both = jnp.concatenate([cache_keys, cache_values], axis=-1)
    send = jnp.einsum("gp,pkh->gkh", picks, both, preferred_element_type=jnp.float32).astype(
        jnp.bfloat16
    )
    got = lax.all_to_all(send, "grp", 0, 0, tiled=True)
    got = got.reshape(groups * stretch_len, 2 * HEAD)
    table_row = lax.dynamic_index_in_dim(page_table, group, 0, keepdims=False)
    shift_of, row_req, row_pos, row_code, key_code, live = request_layout(
        stretch_request[0], query_counts[0], recompute_ids[0], table_row, (groups, pages),
        stretch_len, new_rows,
    )
    pcos, psin = angles_of(shift_of)
    cosine, sine = angles_of(row_pos)
    heads, w_across = project_in(own_rows, input_gain, w_query, w_key, w_value, cosine, sine, w_out)
    attended = attention(
        heads, got[:, :HEAD], got[:, HEAD:], pcos, psin, row_code, key_code, live
    )
    output = project(attended, w_out, w_across, own_rows, post_gain)
    return output[None]


def solution(mesh):
    return jax.shard_map(
        on_device,
        mesh=mesh,
        in_specs=(
            P("grp", "tok", None), P(), P(None, "tok"), P(None, "tok"), P(None, "tok"),
            P("tok", None), P(), P("grp", None, "tok"), P("grp", None, "tok"), P(),
            P("grp", None), P("grp", None), P("grp", None),
        ),
        out_specs=P("grp", "tok", None),
        check_vma=False,
    )
```

```python
import functools
import math

import jax
import jax.numpy as jnp
import numpy as np
from jax import lax
from jax.experimental import pallas as pl
from jax.experimental.pallas import tpu as pltpu
from jax.sharding import PartitionSpec as P

HEAD = 128
EPSILON = 1e-06
CAP_VALUE = 50.0
QUERY_SCALE = 1.0 / 12.0
ROPE_BASE = 10000.0
SPAN = 1 << 16
FAR = 1 << 30
BLOCK = 512


def frequencies():
    ladder = np.arange(HEAD // 2, dtype=np.float32)
    return np.exp(ladder * np.float32(-2.0 * math.log(ROPE_BASE) / HEAD)).astype(np.float32)


def turned(u, cosine, sine):
    return u * cosine + pltpu.roll(u, HEAD // 2, 1) * sine


def request_base(code):
    return jnp.where(code >= 2 * SPAN, 2 * SPAN, jnp.where(code >= SPAN, SPAN, 0))


class Layout:
    def __init__(self, owners, counts, stretch):
        slots = owners.shape[0]
        self.stretch = stretch
        self.owners = [owners[c] for c in range(slots)]
        held = [sum((o == r).astype(jnp.int32) for o in self.owners) for r in range(3)]
        first = [0, held[0], held[0] + held[1]]
        self.offsets = []
        self.slot_bases = []
        for c, o in enumerate(self.owners):
            start = jnp.where(o == 0, first[0], jnp.where(o == 1, first[1], first[2]))
            self.offsets.append(c - start)
            self.slot_bases.append(o * SPAN - start * stretch)
        self.starts = [0, counts[0], counts[0] + counts[1]]
        self.query_bases = [r * SPAN + held[r] * stretch - self.starts[r] for r in range(3)]

    def of_queries(self, m):
        base = jnp.where(
            m >= self.starts[2], self.query_bases[2],
            jnp.where(m >= self.starts[1], self.query_bases[1], self.query_bases[0]),
        )
        return m + base

    def of_cached(self, ids):
        base = self.slot_bases[0]
        for c in range(1, len(self.slot_bases)):
            base = jnp.where(ids >= c * self.stretch, self.slot_bases[c], base)
        return ids + base

    def request_of(self, m):
        return (m >= self.starts[1]).astype(jnp.int32) + (m >= self.starts[2]).astype(jnp.int32)


def attention_kernel(
    selected, owners_ref, counts_ref, table_ref, heads_ref, pages_ref, pcos_ref, psin_ref,
    ids_col_ref, ids_row_ref, out_ref, keys, values, key_codes, row_codes, row_bases, queries, total,
):
    rows = heads_ref.shape[1]
    groups, stretch = pages_ref.shape[:2]
    cached = groups * stretch
    group = lax.axis_index("grp")
    layout = Layout(owners_ref, counts_ref, stretch)
    lane = lax.broadcasted_iota(jnp.int32, (1, stretch), 1)
    below = lax.broadcasted_iota(jnp.int32, (stretch, 1), 0)
    ids_col = ids_col_ref[...]
    per = BLOCK // stretch

    def put_codes(i, codes):
        key_codes[i // per, :, pl.ds((i % per) * stretch, stretch)] = codes

    for c in range(groups):
        page = table_ref[group, c]
        source = page // (table_ref.shape[1])
        part = pl.ds(c * stretch, stretch)
        turn = layout.offsets[c]
        k = pages_ref[source, :, :HEAD].astype(jnp.float32)
        k = turned(k, pcos_ref[pl.ds(turn, 1), :], psin_ref[pl.ds(turn, 1), :])
        keys[part, :] = k.astype(jnp.bfloat16)
        values[part, :HEAD] = pages_ref[source, :, HEAD:]
        ids = lane + c * stretch
        dead = jnp.max((ids_col == ids).astype(jnp.int32), axis=0, keepdims=True)
        put_codes(c, jnp.where(dead > 0, FAR, ids + layout.slot_bases[c]))
    keys[pl.ds(cached, rows), :] = heads_ref[2]
    values[pl.ds(cached, rows), :HEAD] = heads_ref[3]
    values[:, HEAD:] = jnp.ones((cached + rows, HEAD), jnp.bfloat16)
    for i in range(rows // stretch):
        by_lane = layout.of_queries(lane + (i * stretch - selected))
        by_row = layout.of_queries(below + (i * stretch - selected))
        if i == 0:
            by_lane = jnp.where(lane < selected, layout.of_cached(ids_row_ref[...]), by_lane)
            by_row = jnp.where(below < selected, layout.of_cached(ids_col), by_row)
        put_codes(groups + i, by_lane)
        row_codes[pl.ds(i * stretch, stretch), :] = by_row
        row_bases[pl.ds(i * stretch, stretch), :] = request_base(by_row)

    ahead = cached // BLOCK

    def row_block(rb, carry):
        here = pl.ds(pl.multiple_of(rb * BLOCK, BLOCK), BLOCK)
        queries[:BLOCK, :] = heads_ref[0, here, :]
        queries[BLOCK:, :] = heads_ref[1, here, :]
        total[...] = jnp.zeros_like(total)
        code = row_codes[here, :]
        base = row_bases[here, :]
        low = jnp.where(rb == 0, 0, layout.request_of(rb * BLOCK - selected))
        high = jnp.where(rb == 0, 2, layout.request_of(rb * BLOCK - selected + BLOCK - 1))

        def attend(kb):
            there = pl.ds(pl.multiple_of(kb * BLOCK, BLOCK), BLOCK)
            scores = lax.dot_general(
                queries[...], keys[there, :], (((1,), (1,)), ((), ())),
                preferred_element_type=jnp.float32,
            )
            capped = jnp.tanh(scores * (QUERY_SCALE / CAP_VALUE))
            weights = jnp.exp2(capped * (CAP_VALUE * math.log2(math.e)))
            key_code = key_codes[kb]
            seen = (key_code <= code) & (key_code >= base)
            both = jnp.concatenate([seen, seen], axis=0)
            rounded = jnp.where(both, weights, 0.0).astype(jnp.bfloat16)
            total[...] += jnp.dot(rounded, values[there, :], preferred_element_type=jnp.float32)

        def key_block(kb, inner_carry):
            slot = jnp.minimum(kb * per, groups - per)
            from_cache = (owners_ref[slot] <= high) & (owners_ref[slot + per - 1] >= low)
            last = (kb - ahead + 1) * BLOCK - 1 - selected
            from_new = (kb == ahead) | (layout.request_of(last) >= low)

            @pl.when(((kb < ahead) & from_cache) | ((kb >= ahead) & from_new))
            def _():
                attend(kb)

            return inner_carry

        lax.fori_loop(0, ahead + rb + 1, key_block, 0)
        result = total[:, :HEAD] / total[:, HEAD:]
        out_ref[here, :HEAD] = result[:BLOCK].astype(jnp.bfloat16)
        out_ref[here, HEAD:] = result[BLOCK:].astype(jnp.bfloat16)
        return carry

    lax.fori_loop(0, rows // BLOCK, row_block, 0)


def attention(heads, pages, owners, counts, table, selected, ids_col, ids_row):
    rows = heads.shape[1]
    groups, stretch = pages.shape[:2]
    total_keys = groups * stretch + rows
    angles = (np.arange(groups, dtype=np.float32) * stretch)[:, None] * frequencies()[None, :]
    cosine, sine = np.cos(angles), np.sin(angles)
    vmem = pl.BlockSpec(memory_space=pltpu.VMEM)
    smem = pl.BlockSpec(memory_space=pltpu.SMEM)
    return pl.pallas_call(
        functools.partial(attention_kernel, selected),
        out_shape=jax.ShapeDtypeStruct((rows, 2 * HEAD), jnp.bfloat16),
        in_specs=[smem] * 3 + [vmem] * 6,
        out_specs=vmem,
        scratch_shapes=[
            pltpu.VMEM((total_keys, HEAD), jnp.bfloat16),
            pltpu.VMEM((total_keys, 2 * HEAD), jnp.bfloat16),
            pltpu.VMEM((total_keys // BLOCK, 1, BLOCK), jnp.int32),
            pltpu.VMEM((rows, 1), jnp.int32),
            pltpu.VMEM((rows, 1), jnp.int32),
            pltpu.VMEM((2 * BLOCK, HEAD), jnp.bfloat16),
            pltpu.VMEM((2 * BLOCK, 2 * HEAD), jnp.float32),
        ],
        compiler_params=pltpu.CompilerParams(vmem_limit_bytes=40 << 20),
        name="attention",
    )(
        owners, counts, table, heads, pages,
        np.concatenate([cosine, cosine], axis=1), np.concatenate([-sine, sine], axis=1),
        ids_col, ids_row,
    )


MESH = pl.DeviceIdType.MESH
RINGS = 4
AROUND = 4


def place():
    tok = lax.axis_index("tok")
    return lax.axis_index("grp"), tok // 8, (tok // 2) % AROUND, tok % 2


def device(group, half, spot, core):
    return (group, half * 8 + lax.rem(spot + 2 * AROUND, AROUND) * 2 + core)


def greet(partners):
    barrier = pltpu.get_barrier_semaphore()
    for partner in partners:
        pl.semaphore_signal(barrier, inc=1, device_id=partner, device_id_type=MESH)
    pl.semaphore_wait(barrier, len(partners))


def project_kernel(
    attn_ref, w0_ref, w1_ref, hid_ref, gain_ref, out_ref,
    other, product, own, pair_out, pair_in, ring_out, ring_in, result,
    other_send, other_recv, pair_send, pair_recv, ring_send, ring_recv,
):
    group, half, spot, core = place()
    rows = hid_ref.shape[0]
    width = hid_ref.shape[1] // RINGS
    chunk = 2 * rows
    across = device(group, 1 - half, spot, core)
    sibling = device(group, half, spot, 1 - core)
    greet([across, sibling, device(group, half, spot + 1, core), device(group, half, spot - 1, core)])

    def other_copy(j):
        owner = lax.rem(spot + (3, 1, 2, 0)[j], AROUND)
        start = pl.multiple_of(((1 - half) * AROUND + owner) * chunk, chunk)
        return pltpu.make_async_remote_copy(
            src_ref=attn_ref.at[pl.ds(start, chunk)], dst_ref=other.at[j],
            send_sem=other_send.at[j], recv_sem=other_recv.at[j],
            device_id=across, device_id_type=MESH,
        )

    def pair_copy(s, r):
        return pltpu.make_async_remote_copy(
            src_ref=pair_out.at[s, r], dst_ref=pair_in.at[s, r],
            send_sem=pair_send.at[s, r], recv_sem=pair_recv.at[s, r],
            device_id=sibling, device_id_type=MESH,
        )

    def ring_copy(s, r):
        return pltpu.make_async_remote_copy(
            src_ref=ring_out.at[s, r], dst_ref=ring_in.at[s, r],
            send_sem=ring_send.at[s, r], recv_sem=ring_recv.at[s, r],
            device_id=device(group, half, spot + 1 - 2 * (r // 2), core), device_id_type=MESH,
        )

    for j in range(4):
        other_copy(j).start()

    def partial(s, r):
        owner = lax.rem(spot + (2 * (r // 2) - 1) * (1 + s) + 2 * AROUND, AROUND)
        slot = (r // 2, 2, 1 - r // 2, 3)[s]
        start = pl.multiple_of((half * AROUND + owner) * chunk, chunk)
        columns = pl.ds(pl.multiple_of(r * width, width), width)
        product[...] = jnp.dot(
            attn_ref[pl.ds(start, chunk), :], w0_ref[:, columns], preferred_element_type=jnp.float32
        ) + jnp.dot(other[slot], w1_ref[:, columns], preferred_element_type=jnp.float32)
        theirs = pl.ds(pl.multiple_of((1 - core) * rows, rows), rows)
        pair_out[s, r] = product[theirs, :].astype(jnp.bfloat16)
        pair_copy(s, r).start()
        own[s, r] = product[pl.ds(pl.multiple_of(core * rows, rows), rows), :]

    def partials(s, first, last):
        def step(r, carry):
            partial(s, r)
            return carry

        lax.fori_loop(first, last, step, 0)

    def forward(s):
        def step(r, carry):
            pair_copy(s, r).wait_recv()
            running = own[s, r] + pair_in[s, r].astype(jnp.float32)
            if s > 0:
                ring_copy(s - 1, r).wait_recv()
                running = running + ring_in[s - 1, r].astype(jnp.float32)
            if s < 3:
                ring_out[s, r] = running.astype(jnp.bfloat16)
                ring_copy(s, r).start()
            else:
                result[:, pl.ds(pl.multiple_of(r * width, width), width)] = running
            return carry

        for r in (0, 2, 1, 3):
            step(r, 0)

    other_copy(0).wait_recv()
    partials(0, 0, 2)
    other_copy(1).wait_recv()
    partials(0, 2, 4)
    forward(0)
    other_copy(2).wait_recv()
    partials(1, 0, 4)
    partials(2, 0, 4)
    other_copy(3).wait_recv()
    partials(3, 0, 4)
    forward(1)
    forward(2)
    forward(3)
    for j in range(4):
        other_copy(j).wait_send()

    def drain(r, carry):
        for s in range(4):
            pair_copy(s, r).wait_send()
        for s in range(3):
            ring_copy(s, r).wait_send()
        return carry

    lax.fori_loop(0, RINGS, drain, 0)
    projected = result[...]
    scale = lax.rsqrt(jnp.mean(projected * projected, axis=-1, keepdims=True) + EPSILON)
    out_ref[...] = (
        hid_ref[...].astype(jnp.float32) + projected * scale * gain_ref[...]
    ).astype(jnp.bfloat16)


def project(attended, w_own, w_across, own_rows, post_gain):
    rows, features = own_rows.shape
    width = features // RINGS
    vmem = pl.BlockSpec(memory_space=pltpu.VMEM)
    dma = pltpu.SemaphoreType.DMA
    return pl.pallas_call(
        project_kernel,
        out_shape=jax.ShapeDtypeStruct((rows, features), jnp.bfloat16),
        in_specs=[vmem] * 5,
        out_specs=vmem,
        scratch_shapes=[
            pltpu.VMEM((4, 2 * rows, attended.shape[1]), jnp.bfloat16),
            pltpu.VMEM((2 * rows, width), jnp.float32),
            pltpu.VMEM((4, RINGS, rows, width), jnp.float32),
            pltpu.VMEM((4, RINGS, rows, width), jnp.bfloat16),
            pltpu.VMEM((4, RINGS, rows, width), jnp.bfloat16),
            pltpu.VMEM((3, RINGS, rows, width), jnp.bfloat16),
            pltpu.VMEM((3, RINGS, rows, width), jnp.bfloat16),
            pltpu.VMEM((rows, features), jnp.float32),
            dma((4,)), dma((4,)), dma((4, RINGS)), dma((4, RINGS)), dma((3, RINGS)), dma((3, RINGS)),
        ],
        compiler_params=pltpu.CompilerParams(
            collective_id=1, has_side_effects=True, vmem_limit_bytes=56 << 20
        ),
        name="project",
    )(attended, w_own, w_across, own_rows, post_gain[None, :])


def project_in_kernel(
    selected, owners_ref, counts_ref, table_ref, hid_ref, gain_ref, freq_ref, ids_ref,
    wq_hbm, wk_hbm, wv_hbm, ck_hbm, cv_hbm, wo_ref,
    heads_ref, wo_across_ref, pages_ref,
    normed, weights, ship, wq_ref, wk_ref, wv_ref, ck_ref, cv_ref, outgoing, cos_ref, sin_ref,
    l_sem, p_send, p_recv, x_send, x_recv, f_send, f_recv, s_send, s_recv, y_send, y_recv, w_send, w_recv, z_send, z_recv,
    g_send, g_recv, o_send, o_recv, e_send, e_recv,
):
    group, half, spot, core = place()
    rows, features = hid_ref.shape
    depth = group % AROUND
    lows = group // AROUND
    quarter = features // 4
    out_quarter = wo_ref.shape[0] // 4

    def around(value):
        return lax.rem(value + 2 * AROUND, AROUND)

    xs = [device(group, half, spot + 1, core), device(group, half, spot - 1, core)]
    zs = [
        device(lows * AROUND + around(depth + 1), half, spot, core),
        device(lows * AROUND + around(depth - 1), half, spot, core),
    ]
    near = device((1 - lows) * AROUND + depth, 1 - half, spot, core)
    across = device(group, 1 - half, spot, core)
    beside = device((1 - lows) * AROUND + depth, half, spot, core)
    sibling = device(group, half, spot, 1 - core)
    offsets = [(0, 1), (0, -1), (1, 0), (0, 2), (1, 1), (1, -1), (1, 2)]

    def group_at(low, deep):
        return lax.rem(lows + low, 2) * AROUND + around(depth + deep)

    local = [
        pltpu.make_async_copy(src, dst, l_sem.at[i])
        for i, (src, dst) in enumerate(
            [(ck_hbm, ck_ref), (cv_hbm, cv_ref), (wq_hbm, wq_ref), (wk_hbm, wk_ref), (wv_hbm, wv_ref)]
        )
    ]
    for each in local:
        each.start()
    greet(
        xs + zs + [near, across, beside, sibling]
        + [device(group_at(*o), half, spot, core) for o in offsets[3:]]
    )

    def copy(src, dst, send, recv, to):
        return pltpu.make_async_remote_copy(
            src_ref=src, dst_ref=dst, send_sem=send, recv_sem=recv, device_id=to, device_id_type=MESH
        )

    mine = pl.multiple_of(core * rows, rows)
    twin = pl.multiple_of((1 - core) * rows, rows)

    def block(owner, start=0, size=rows, base=mine):
        return normed.at[owner, pl.ds(pl.multiple_of(base + start, size), size)]

    def x_copy(d, owner=spot):
        return copy(block(owner), block(owner), x_send.at[d], x_recv.at[d], xs[d])

    def f_copy(d, owner):
        piece = block(owner, d * (rows // 2), rows // 2)
        return copy(piece, piece, f_send.at[d], f_recv.at[d], xs[d])

    def s_copy(i, owner, base=mine):
        piece = block(owner, base=base)
        return copy(piece, piece, s_send.at[i], s_recv.at[i], sibling)

    mine_first, theirs_first = 2 * lows, 2 * (1 - lows)

    def slab(q, p):
        return weights.at[q, pl.ds(pl.multiple_of(p * quarter, quarter), quarter)]

    def y_start(j):
        part = pl.ds(pl.multiple_of((theirs_first + j) * quarter, quarter), quarter)
        sources = [
            wq_hbm.at[part, pl.ds(0, HEAD)], wq_hbm.at[part, pl.ds(HEAD, HEAD)],
            wk_hbm.at[part], wv_hbm.at[part],
        ]
        for z, src in enumerate(sources):
            @pl.when(depth == z)
            def _(src=src):
                copy(src, slab(depth, theirs_first + j), y_send.at[j], y_recv.at[j], near).start()

    def y_done(j):
        piece = slab(depth, mine_first + j)
        return copy(piece, piece, y_send.at[j], y_recv.at[j], near)

    def w_copy(i, q, p):
        return copy(slab(q, p), slab(q, p), w_send.at[i], w_recv.at[i], beside)

    def nth_piece(n):
        return (mine_first if n < 2 else theirs_first) + n % 2

    def z_copy(d, n, q=depth):
        piece = slab(q, nth_piece(n))
        return copy(piece, piece, z_send.at[d, n], z_recv.at[d, n], zs[d])

    def g_copy(d, q):
        piece = slab(q, mine_first + d)
        return copy(piece, piece, g_send.at[d], g_recv.at[d], zs[d])

    def o_copy(i, src, q, n, to):
        size = out_quarter // 2
        part = pl.ds(pl.multiple_of(q * out_quarter + n * size, size), size)
        return copy(src.at[part], wo_across_ref.at[part], o_send.at[i], o_recv.at[i], to)

    pages, stretch = ck_ref.shape[:2]
    groups = table_ref.shape[0]

    def picked(target):
        index = 0
        for c in range(table_ref.shape[1]):
            page = table_ref[target, c]
            index = index + jnp.where(page // pages == group, page % pages, 0)
        return index

    def p_copy(j, source):
        return copy(
            outgoing.at[j], pages_ref.at[source], p_send.at[j], p_recv.at[j],
            device(group_at(*offsets[j]), half, spot, core),
        )

    def send_pages():
        for each in local[:2]:
            each.wait()
        for j, offset in enumerate(offsets):
            index = picked(group_at(*offset))
            outgoing[j, :, :HEAD] = ck_ref[index]
            outgoing[j, :, HEAD:] = cv_ref[index]
            p_copy(j, group).start()
        index = picked(group)
        pages_ref[group, :, :HEAD] = ck_ref[index]
        pages_ref[group, :, HEAD:] = cv_ref[index]

    def make_tables():
        layout = Layout(owners_ref, counts_ref, stretch)
        below = lax.broadcasted_iota(jnp.int32, (stretch, 1), 0)
        for i in range(cos_ref.shape[0] // stretch):
            row = below + (half * cos_ref.shape[0] + i * stretch)
            code = layout.of_queries(row - selected)
            if i == 0:
                code = jnp.where(row < selected, layout.of_cached(ids_ref[...]), code)
            angle = (code - request_base(code)).astype(jnp.float32) * freq_ref[...]
            sine = jnp.sin(angle)
            lane = lax.broadcasted_iota(jnp.int32, sine.shape, 1)
            cos_ref[pl.ds(i * stretch, stretch), :] = jnp.cos(angle)
            sin_ref[pl.ds(i * stretch, stretch), :] = jnp.where(lane < HEAD // 2, -sine, sine)

    def table(ref, owner):
        return ref[pl.ds(pl.multiple_of(owner * 2 * rows, 2 * rows), 2 * rows), :]

    def own_heads(owner):
        source = normed[owner]
        cosine, sine = table(cos_ref, owner), table(sin_ref, owner)
        to = pl.ds(pl.multiple_of((half * AROUND + owner) * 2 * rows, 2 * rows), 2 * rows)
        q = jnp.dot(source, wq_ref[...], preferred_element_type=jnp.float32)
        heads_ref[0, to] = turned(q[:, :HEAD], cosine, sine).astype(jnp.bfloat16)
        heads_ref[1, to] = turned(q[:, HEAD:], cosine, sine).astype(jnp.bfloat16)
        k = jnp.dot(source, wk_ref[...], preferred_element_type=jnp.float32)
        heads_ref[2, to] = turned(k, cosine, sine).astype(jnp.bfloat16)
        v = jnp.dot(source, wv_ref[...], preferred_element_type=jnp.float32)
        heads_ref[3, to] = v.astype(jnp.bfloat16)

    def e_copy(i, b, owner, q):
        to = pl.ds(pl.multiple_of((half * AROUND + owner) * 2 * rows, 2 * rows), 2 * rows)
        return copy(ship.at[i, b], heads_ref.at[q, to], e_send.at[i, b], e_recv.at[i, b], across)

    def nth(base, i):
        return around(base + (i * (7 - i)) // 2)

    owners = [nth(spot, b) for b in range(4)]
    quarters = [nth(depth, i) for i in range(4)]

    def their_heads(i, b):
        owner, q = nth(spot, b), nth(depth, i)
        u = jnp.dot(normed[owner], weights[q], preferred_element_type=jnp.float32)
        plain = (q == 3).astype(jnp.float32)
        cosine, sine = table(cos_ref, owner), table(sin_ref, owner)
        cosine = cosine + plain * (1.0 - cosine)
        sine = sine * (1.0 - plain)
        ship[i, b] = turned(u, cosine, sine).astype(jnp.bfloat16)
        e_copy(i, b, owner, q).start()

    def own_blocks(first, last):
        def step(b, carry):
            own_heads(nth(spot, b))
            return carry

        lax.fori_loop(first, last, step, 0)

    def their_blocks(i0, i1, b0, b1):
        def step(n, carry):
            their_heads(i0 + n // (b1 - b0), b0 + lax.rem(n, b1 - b0))
            return carry

        lax.fori_loop(0, (i1 - i0) * (b1 - b0), step, 0)

    left, right, far = owners[1], owners[2], owners[3]
    below, above, beyond = quarters[1], quarters[2], quarters[3]
    y_start(0)
    y_start(1)
    wide = hid_ref[...].astype(jnp.float32)
    scale = lax.rsqrt(jnp.mean(wide * wide, axis=-1, keepdims=True) + EPSILON)
    normed[spot, pl.ds(mine, rows)] = (wide * scale * gain_ref[...]).astype(jnp.bfloat16)
    x_copy(0).start()
    x_copy(1).start()
    s_copy(0, spot).start()
    send_pages()
    make_tables()
    for each in local[2:]:
        each.wait()
    for n in range(2):
        y_done(n).wait_recv()
        w_copy(n, depth, mine_first + n).start()
        z_copy(0, n).start()
        z_copy(1, n).start()
    o_copy(0, wo_ref, depth, 1 - lows, near).start()
    s_copy(0, spot, twin).wait_recv()
    own_blocks(0, 1)
    for n in range(2):
        w_copy(n, depth, theirs_first + n).wait_recv()
        z_copy(0, n + 2).start()
        z_copy(1, n + 2).start()
    their_blocks(0, 1, 0, 1)
    z_copy(0, 0, below).wait_recv()
    g_copy(0, below).start()
    z_copy(1, 1, above).wait_recv()
    g_copy(1, above).start()
    o_copy(0, wo_ref, depth, lows, near).wait_recv()
    o_copy(1, wo_across_ref, depth, lows, beside).start()
    x_copy(0, left).wait_recv()
    f_copy(0, left).start()
    s_copy(1, left).start()
    x_copy(1, right).wait_recv()
    f_copy(1, right).start()
    s_copy(2, right).start()
    s_copy(1, left, twin).wait_recv()
    s_copy(2, right, twin).wait_recv()
    their_blocks(0, 1, 1, 3)
    for n in range(1, 4):
        z_copy(0, n, below).wait_recv()
    for n in (0, 2, 3):
        z_copy(1, n, above).wait_recv()
    g_copy(0, beyond).wait_recv()
    w_copy(2, beyond, mine_first).start()
    g_copy(1, beyond).wait_recv()
    w_copy(3, beyond, mine_first + 1).start()
    o_copy(1, wo_across_ref, depth, 1 - lows, beside).wait_recv()
    for n in range(2):
        o_copy(2 + n, wo_across_ref, depth, n, zs[0]).start()
        o_copy(4 + n, wo_across_ref, depth, n, zs[1]).start()
    their_blocks(1, 3, 0, 3)
    own_blocks(1, 3)
    w_copy(2, beyond, theirs_first).wait_recv()
    w_copy(3, beyond, theirs_first + 1).wait_recv()
    their_blocks(3, 4, 0, 3)
    f_copy(0, far).wait_recv()
    f_copy(1, far).wait_recv()
    s_copy(3, far).start()
    s_copy(3, far, twin).wait_recv()
    their_blocks(0, 4, 3, 4)
    o_copy(2, wo_across_ref, below, 0, zs[0]).wait_recv()
    o_copy(6, wo_across_ref, below, 0, zs[0]).start()
    o_copy(5, wo_across_ref, above, 1, zs[1]).wait_recv()
    o_copy(7, wo_across_ref, above, 1, zs[1]).start()
    own_blocks(3, 4)
    o_copy(3, wo_across_ref, below, 1, zs[0]).wait_recv()
    o_copy(4, wo_across_ref, above, 0, zs[1]).wait_recv()
    o_copy(6, wo_across_ref, beyond, 0, zs[0]).wait_recv()
    o_copy(7, wo_across_ref, beyond, 1, zs[1]).wait_recv()
    for i in range(4):
        for b in range(4):
            to = pl.ds(
                pl.multiple_of(((1 - half) * AROUND + owners[b]) * 2 * rows, 2 * rows), 2 * rows
            )
            copy(
                ship.at[i, b], heads_ref.at[quarters[i], to], e_send.at[i, b], e_recv.at[i, b], across
            ).wait()
    for d in range(2):
        x_copy(d).wait_send()
        f_copy(d, owners[1 + d]).wait_send()
        for n in range(4):
            z_copy(d, n).wait_send()
        g_copy(d, quarters[1 + d]).wait_send()
    for i in range(4):
        s_copy(i, owners[i]).wait_send()
        w_copy(i, (depth, depth, beyond, beyond)[i], mine_first + i % 2).wait_send()
    for n in range(2):
        y_done(n).wait_send()
    for i in range(8):
        o_copy(i, wo_across_ref, depth, 0, near).wait_send()
    for j, (low, deep) in enumerate(offsets):
        p_copy(j, group_at(low, -deep)).wait()


def project_in(
    own_rows, gain, w_query, w_key, w_value, w_out, cache_keys, cache_values,
    owners, counts, table, selected, ids_col, new_rows,
):
    rows, features = own_rows.shape
    pages, stretch = cache_keys.shape[:2]
    vmem = pl.BlockSpec(memory_space=pltpu.VMEM)
    smem = pl.BlockSpec(memory_space=pltpu.SMEM)
    hbm = pl.BlockSpec(memory_space=pl.ANY)
    dma = pltpu.SemaphoreType.DMA
    pairs = [(7,), (2,), (2,), (4,), (2,), (4,), (2, 4), (2,), (8,), (4, 4)]
    bf16 = jnp.bfloat16
    return pl.pallas_call(
        functools.partial(project_in_kernel, selected),
        out_shape=(
            jax.ShapeDtypeStruct((4, new_rows, HEAD), bf16),
            jax.ShapeDtypeStruct(w_out.shape, bf16),
            jax.ShapeDtypeStruct((table.shape[0], stretch, 2 * HEAD), bf16),
        ),
        in_specs=[smem] * 3 + [vmem] * 4 + [hbm] * 6,
        out_specs=(vmem, hbm, vmem),
        scratch_shapes=[
            pltpu.VMEM((AROUND, 2 * rows, features), bf16),
            pltpu.VMEM((4, features, HEAD), bf16),
            pltpu.VMEM((4, 4, 2 * rows, HEAD), bf16),
            pltpu.VMEM(w_query.shape, bf16), pltpu.VMEM(w_key.shape, bf16),
            pltpu.VMEM(w_value.shape, bf16),
            pltpu.VMEM(cache_keys.shape, bf16), pltpu.VMEM(cache_values.shape, bf16),
            pltpu.VMEM((7, stretch, 2 * HEAD), bf16),
            pltpu.VMEM((new_rows // 2, HEAD), jnp.float32),
            pltpu.VMEM((new_rows // 2, HEAD), jnp.float32),
            dma((5,)),
        ] + [dma(shape) for shape in pairs for _ in range(2)],
        compiler_params=pltpu.CompilerParams(
            collective_id=2, has_side_effects=True, vmem_limit_bytes=52 << 20
        ),
        name="project_in",
    )(
        owners, counts, table, own_rows, gain[None, :],
        np.concatenate([frequencies()] * 2)[None, :], ids_col,
        w_query, w_key, w_value, cache_keys, cache_values, w_out,
    )


def on_device(
    hidden, input_gain, w_query, w_key, w_value, w_out, post_gain, cache_keys, cache_values,
    page_table, stretch_request, recompute_ids, query_counts,
):
    own_rows = hidden[0]
    new_rows = own_rows.shape[0] * lax.axis_size("tok")
    stretch = cache_keys.shape[1]
    owners, counts, ids = stretch_request[0], query_counts[0], recompute_ids[0]
    selected = ids.shape[0]
    padded = jnp.pad(ids, (0, stretch - selected), constant_values=-1)
    ids_col, ids_row = padded[:, None], padded[None, :]
    heads, w_across, pages = project_in(
        own_rows, input_gain, w_query, w_key, w_value, w_out, cache_keys, cache_values,
        owners, counts, page_table, selected, ids_col, new_rows,
    )
    attended = attention(heads, pages, owners, counts, page_table, selected, ids_col, ids_row)
    return project(attended, w_out, w_across, own_rows, post_gain)[None]


def solution(mesh):
    return jax.shard_map(
        on_device,
        mesh=mesh,
        in_specs=(
            P("grp", "tok", None), P(), P(None, "tok"), P(None, "tok"), P(None, "tok"),
            P("tok", None), P(), P("grp", None, "tok"), P("grp", None, "tok"), P(),
            P("grp", None), P("grp", None), P("grp", None),
        ),
        out_specs=P("grp", "tok", None),
        check_vma=False,
    )
```

```python
import functools
import math

import jax
import jax.numpy as jnp
import numpy as np
from jax import lax
from jax.experimental import pallas as pl
from jax.experimental.pallas import tpu as pltpu
from jax.sharding import PartitionSpec as P

HEAD = 128
EPSILON = 1e-06
CAP_VALUE = 50.0
QUERY_SCALE = 1.0 / 12.0
ROPE_BASE = 10000.0
SPAN = 1 << 16
FAR = 1 << 30
BLOCK = 512


def frequencies():
    ladder = np.arange(HEAD // 2, dtype=np.float32)
    return np.exp(ladder * np.float32(-2.0 * math.log(ROPE_BASE) / HEAD)).astype(np.float32)


def turned(u, cosine, sine):
    return u * cosine + pltpu.roll(u, HEAD // 2, 1) * sine


def request_base(code):
    return jnp.where(code >= 2 * SPAN, 2 * SPAN, jnp.where(code >= SPAN, SPAN, 0))


class Layout:
    def __init__(self, owners, counts, stretch):
        slots = owners.shape[0]
        self.stretch = stretch
        self.owners = [owners[c] for c in range(slots)]
        held = [sum((o == r).astype(jnp.int32) for o in self.owners) for r in range(3)]
        first = [0, held[0], held[0] + held[1]]
        self.offsets = []
        self.slot_bases = []
        for c, o in enumerate(self.owners):
            start = jnp.where(o == 0, first[0], jnp.where(o == 1, first[1], first[2]))
            self.offsets.append(c - start)
            self.slot_bases.append(o * SPAN - start * stretch)
        self.starts = [0, counts[0], counts[0] + counts[1]]
        self.query_bases = [r * SPAN + held[r] * stretch - self.starts[r] for r in range(3)]

    def of_queries(self, m):
        base = jnp.where(
            m >= self.starts[2], self.query_bases[2],
            jnp.where(m >= self.starts[1], self.query_bases[1], self.query_bases[0]),
        )
        return m + base

    def of_cached(self, ids):
        base = self.slot_bases[0]
        for c in range(1, len(self.slot_bases)):
            base = jnp.where(ids >= c * self.stretch, self.slot_bases[c], base)
        return ids + base

    def request_of(self, m):
        return (m >= self.starts[1]).astype(jnp.int32) + (m >= self.starts[2]).astype(jnp.int32)


MESH = pl.DeviceIdType.MESH
RINGS = 4
AROUND = 4


def place():
    tok = lax.axis_index("tok")
    return lax.axis_index("grp"), tok // 8, (tok // 2) % AROUND, tok % 2


def device(group, half, spot, core):
    return (group, half * 8 + lax.rem(spot + 2 * AROUND, AROUND) * 2 + core)


def greet(partners):
    barrier = pltpu.get_barrier_semaphore()
    for partner in partners:
        pl.semaphore_signal(barrier, inc=1, device_id=partner, device_id_type=MESH)
    pl.semaphore_wait(barrier, len(partners))


def make_attention(
    selected, owners_ref, counts_ref, table_ref, heads_ref, pages_ref, pcos_ref, psin_ref,
    ids_col_ref, ids_row_ref, attended, keys, values, key_codes, row_codes, row_bases, queries, total,
):
    rows = heads_ref.shape[1]
    groups, stretch = pages_ref.shape[:2]
    cached = groups * stretch
    group = lax.axis_index("grp")
    layout = Layout(owners_ref, counts_ref, stretch)
    lane = lax.broadcasted_iota(jnp.int32, (1, stretch), 1)
    below = lax.broadcasted_iota(jnp.int32, (stretch, 1), 0)
    ids_col = ids_col_ref[...]
    per = BLOCK // stretch

    def put_codes(i, codes):
        key_codes[i // per, :, pl.ds((i % per) * stretch, stretch)] = codes

    for c in range(groups):
        page = table_ref[group, c]
        source = page // (table_ref.shape[1])
        part = pl.ds(c * stretch, stretch)
        turn = layout.offsets[c]
        k = pages_ref[source, :, :HEAD].astype(jnp.float32)
        k = turned(k, pcos_ref[pl.ds(turn, 1), :], psin_ref[pl.ds(turn, 1), :])
        keys[part, :] = k.astype(jnp.bfloat16)
        values[part, :HEAD] = pages_ref[source, :, HEAD:]
        ids = lane + c * stretch
        dead = jnp.max((ids_col == ids).astype(jnp.int32), axis=0, keepdims=True)
        put_codes(c, jnp.where(dead > 0, FAR, ids + layout.slot_bases[c]))
    keys[pl.ds(cached, rows), :] = heads_ref[2]
    values[pl.ds(cached, rows), :HEAD] = heads_ref[3]
    values[:, HEAD:] = jnp.ones((cached + rows, HEAD), jnp.bfloat16)
    for i in range(rows // stretch):
        by_lane = layout.of_queries(lane + (i * stretch - selected))
        by_row = layout.of_queries(below + (i * stretch - selected))
        if i == 0:
            by_lane = jnp.where(lane < selected, layout.of_cached(ids_row_ref[...]), by_lane)
            by_row = jnp.where(below < selected, layout.of_cached(ids_col), by_row)
        put_codes(groups + i, by_lane)
        row_codes[pl.ds(i * stretch, stretch), :] = by_row
        row_bases[pl.ds(i * stretch, stretch), :] = request_base(by_row)

    ahead = cached // BLOCK

    def row_block(rb):
        here = pl.ds(pl.multiple_of(rb * BLOCK, BLOCK), BLOCK)
        queries[:BLOCK, :] = heads_ref[0, here, :]
        queries[BLOCK:, :] = heads_ref[1, here, :]
        total[...] = jnp.zeros_like(total)
        code = row_codes[here, :]
        base = row_bases[here, :]

        def key_block(kb, carry):
            there = pl.ds(pl.multiple_of(kb * BLOCK, BLOCK), BLOCK)
            scores = lax.dot_general(
                queries[...], keys[there, :], (((1,), (1,)), ((), ())),
                preferred_element_type=jnp.float32,
            )
            capped = jnp.tanh(scores * (QUERY_SCALE / CAP_VALUE))
            weights = jnp.exp2(capped * (CAP_VALUE * math.log2(math.e)))
            key_code = key_codes[kb]
            seen = (key_code <= code) & (key_code >= base)
            both = jnp.concatenate([seen, seen], axis=0)
            rounded = jnp.where(both, weights, 0.0).astype(jnp.bfloat16)
            total[...] += jnp.dot(rounded, values[there, :], preferred_element_type=jnp.float32)
            return carry

        lax.fori_loop(0, ahead + rb + 1, key_block, 0)
        quotient = total[:, :HEAD] / total[:, HEAD:]
        attended[here, :HEAD] = quotient[:BLOCK].astype(jnp.bfloat16)
        attended[here, HEAD:] = quotient[BLOCK:].astype(jnp.bfloat16)

    return row_block


def project_kernel(
    selected, owners_ref, counts_ref, table_ref, heads_ref, pages_ref, pcos_ref, psin_ref,
    ids_col_ref, ids_row_ref, w0_ref, hid_ref, gain_ref, out_ref,
    attn_ref, keys, values, key_codes, row_codes, row_bases, queries, total, w1_ref, other, product, own, pair_out, pair_in, ring_out, ring_in, result,
    other_send, other_recv, pair_send, pair_recv, ring_send, ring_recv, o_send, o_recv,
):
    group, half, spot, core = place()
    rows = hid_ref.shape[0]
    width = hid_ref.shape[1] // RINGS
    chunk = 2 * rows
    across = device(group, 1 - half, spot, core)
    sibling = device(group, half, spot, 1 - core)
    lows, depth = group // AROUND, group % AROUND
    zs = [
        device(lows * AROUND + lax.rem(depth + 1, AROUND), half, spot, core),
        device(lows * AROUND + lax.rem(depth + AROUND - 1, AROUND), half, spot, core),
    ]
    near = device((1 - lows) * AROUND + depth, 1 - half, spot, core)
    beside = device((1 - lows) * AROUND + depth, half, spot, core)
    greet(
        [across, sibling, device(group, half, spot + 1, core), device(group, half, spot - 1, core)]
        + zs + [near, beside]
    )

    def o_copy(i, src, step, n, to):
        size = w0_ref.shape[0] // (2 * AROUND)
        piece = lax.rem(depth + step + AROUND, AROUND) * 2 + n
        part = pl.ds(pl.multiple_of(piece * size, size), size)
        return pltpu.make_async_remote_copy(
            src_ref=src.at[part], dst_ref=w1_ref.at[part], send_sem=o_send.at[i],
            recv_sem=o_recv.at[i], device_id=to, device_id_type=MESH,
        )

    first, second = lows, 1 - lows
    o_copy(0, w0_ref, 0, second, near).start()
    row_block = make_attention(
        selected, owners_ref, counts_ref, table_ref, heads_ref, pages_ref, pcos_ref, psin_ref,
        ids_col_ref, ids_row_ref, attn_ref, keys, values, key_codes, row_codes, row_bases, queries,
        total,
    )

    def other_copy(j):
        owner = lax.rem(spot + (3, 1, 2, 0)[j], AROUND)
        start = pl.multiple_of(((1 - half) * AROUND + owner) * chunk, chunk)
        return pltpu.make_async_remote_copy(
            src_ref=attn_ref.at[pl.ds(start, chunk)], dst_ref=other.at[j],
            send_sem=other_send.at[j], recv_sem=other_recv.at[j],
            device_id=across, device_id_type=MESH,
        )

    def pair_copy(s, r):
        return pltpu.make_async_remote_copy(
            src_ref=pair_out.at[s, r], dst_ref=pair_in.at[s, r],
            send_sem=pair_send.at[s, r], recv_sem=pair_recv.at[s, r],
            device_id=sibling, device_id_type=MESH,
        )

    def ring_copy(s, r):
        return pltpu.make_async_remote_copy(
            src_ref=ring_out.at[s, r], dst_ref=ring_in.at[s, r],
            send_sem=ring_send.at[s, r], recv_sem=ring_recv.at[s, r],
            device_id=device(group, half, spot + 1 - 2 * (r // 2), core), device_id_type=MESH,
        )

    per_half = attn_ref.shape[0] // BLOCK // 2

    def attend(base_half, first_block):
        def step(i, carry):
            row_block(base_half * per_half + i)
            return carry

        lax.fori_loop(first_block, first_block + 1, step, 0)

    attend(1 - half, 0)
    o_copy(0, w1_ref, 0, first, near).wait_recv()
    o_copy(1, w1_ref, 0, first, beside).start()
    for d in range(2):
        o_copy(2 + d, w1_ref, 0, first, zs[d]).start()
    attend(1 - half, 1)
    for j in range(4):
        other_copy(j).start()
    o_copy(1, w1_ref, 0, second, beside).wait_recv()
    for d in range(2):
        o_copy(4 + d, w1_ref, 0, second, zs[d]).start()
    o_copy(2, w1_ref, -1, first, zs[0]).wait_recv()
    o_copy(6, w1_ref, -1, first, zs[0]).start()
    attend(half, 0)
    o_copy(5, w1_ref, 1, second, zs[1]).wait_recv()
    o_copy(7, w1_ref, 1, second, zs[1]).start()
    attend(half, 1)
    o_copy(3, w1_ref, 1, first, zs[1]).wait_recv()
    o_copy(4, w1_ref, -1, second, zs[0]).wait_recv()
    o_copy(6, w1_ref, 2, first, zs[0]).wait_recv()
    o_copy(7, w1_ref, 2, second, zs[1]).wait_recv()

    def partial(s, r):
        owner = lax.rem(spot + (2 * (r // 2) - 1) * (1 + s) + 2 * AROUND, AROUND)
        slot = (r // 2, 2, 1 - r // 2, 3)[s]
        start = pl.multiple_of((half * AROUND + owner) * chunk, chunk)
        columns = pl.ds(pl.multiple_of(r * width, width), width)
        product[...] = jnp.dot(
            attn_ref[pl.ds(start, chunk), :], w0_ref[:, columns], preferred_element_type=jnp.float32
        ) + jnp.dot(other[slot], w1_ref[:, columns], preferred_element_type=jnp.float32)
        theirs = pl.ds(pl.multiple_of((1 - core) * rows, rows), rows)
        pair_out[s, r] = product[theirs, :].astype(jnp.bfloat16)
        pair_copy(s, r).start()
        own[s, r] = product[pl.ds(pl.multiple_of(core * rows, rows), rows), :]

    def partials(s, first, last):
        def step(r, carry):
            partial(s, r)
            return carry

        lax.fori_loop(first, last, step, 0)

    def forward(s):
        def step(r, carry):
            pair_copy(s, r).wait_recv()
            running = own[s, r] + pair_in[s, r].astype(jnp.float32)
            if s > 0:
                ring_copy(s - 1, r).wait_recv()
                running = running + ring_in[s - 1, r].astype(jnp.float32)
            if s < 3:
                ring_out[s, r] = running.astype(jnp.bfloat16)
                ring_copy(s, r).start()
            else:
                result[:, pl.ds(pl.multiple_of(r * width, width), width)] = running
            return carry

        for r in (0, 2, 1, 3):
            step(r, 0)

    other_copy(0).wait_recv()
    partials(0, 0, 2)
    other_copy(1).wait_recv()
    partials(0, 2, 4)
    forward(0)
    other_copy(2).wait_recv()
    partials(1, 0, 4)
    partials(2, 0, 4)
    other_copy(3).wait_recv()
    partials(3, 0, 4)
    forward(1)
    forward(2)
    forward(3)
    for j in range(4):
        other_copy(j).wait_send()
    for i in range(8):
        o_copy(i, w1_ref, 0, first, near).wait_send()

    def drain(r, carry):
        for s in range(4):
            pair_copy(s, r).wait_send()
        for s in range(3):
            ring_copy(s, r).wait_send()
        return carry

    lax.fori_loop(0, RINGS, drain, 0)
    projected = result[...]
    scale = lax.rsqrt(jnp.mean(projected * projected, axis=-1, keepdims=True) + EPSILON)
    out_ref[...] = (
        hid_ref[...].astype(jnp.float32) + projected * scale * gain_ref[...]
    ).astype(jnp.bfloat16)


def project(heads, pages, owners, counts, table, selected, ids_col, ids_row, w_own, own_rows, post_gain):
    rows, features = own_rows.shape
    width = features // RINGS
    new_rows = heads.shape[1]
    groups, stretch = pages.shape[:2]
    total_keys = groups * stretch + new_rows
    angles = (np.arange(groups, dtype=np.float32) * stretch)[:, None] * frequencies()[None, :]
    cosine, sine = np.cos(angles), np.sin(angles)
    vmem = pl.BlockSpec(memory_space=pltpu.VMEM)
    smem = pl.BlockSpec(memory_space=pltpu.SMEM)
    dma = pltpu.SemaphoreType.DMA
    return pl.pallas_call(
        functools.partial(project_kernel, selected),
        out_shape=jax.ShapeDtypeStruct((rows, features), jnp.bfloat16),
        in_specs=[smem] * 3 + [vmem] * 9,
        out_specs=vmem,
        scratch_shapes=[
            pltpu.VMEM((new_rows, 2 * HEAD), jnp.bfloat16),
            pltpu.VMEM((total_keys, HEAD), jnp.bfloat16),
            pltpu.VMEM((total_keys, 2 * HEAD), jnp.bfloat16),
            pltpu.VMEM((total_keys // BLOCK, 1, BLOCK), jnp.int32),
            pltpu.VMEM((new_rows, 1), jnp.int32),
            pltpu.VMEM((new_rows, 1), jnp.int32),
            pltpu.VMEM((2 * BLOCK, HEAD), jnp.bfloat16),
            pltpu.VMEM((2 * BLOCK, 2 * HEAD), jnp.float32),
            pltpu.VMEM(w_own.shape, jnp.bfloat16),
            pltpu.VMEM((4, 2 * rows, 2 * HEAD), jnp.bfloat16),
            pltpu.VMEM((2 * rows, width), jnp.float32),
            pltpu.VMEM((4, RINGS, rows, width), jnp.float32),
            pltpu.VMEM((4, RINGS, rows, width), jnp.bfloat16),
            pltpu.VMEM((4, RINGS, rows, width), jnp.bfloat16),
            pltpu.VMEM((3, RINGS, rows, width), jnp.bfloat16),
            pltpu.VMEM((3, RINGS, rows, width), jnp.bfloat16),
            pltpu.VMEM((rows, features), jnp.float32),
            dma((4,)), dma((4,)), dma((4, RINGS)), dma((4, RINGS)), dma((3, RINGS)), dma((3, RINGS)),
            dma((8,)), dma((8,)),
        ],
        compiler_params=pltpu.CompilerParams(
            collective_id=1, has_side_effects=True, vmem_limit_bytes=60 << 20
        ),
        name="project",
    )(
        owners, counts, table, heads, pages,
        np.concatenate([cosine, cosine], axis=1), np.concatenate([-sine, sine], axis=1),
        ids_col, ids_row, w_own, own_rows, post_gain[None, :],
    )


def project_in_kernel(
    selected, owners_ref, counts_ref, table_ref, hid_ref, gain_ref, freq_ref, ids_ref,
    wq_hbm, wk_hbm, wv_hbm, ck_hbm, cv_hbm,
    heads_ref, pages_ref,
    normed, weights, ship, wq_ref, wk_ref, wv_ref, ck_ref, cv_ref, outgoing, cos_ref, sin_ref,
    l_sem, p_send, p_recv, x_send, x_recv, f_send, f_recv, s_send, s_recv, y_send, y_recv, w_send, w_recv, z_send, z_recv,
    g_send, g_recv, e_send, e_recv,
):
    group, half, spot, core = place()
    rows, features = hid_ref.shape
    depth = group % AROUND
    lows = group // AROUND
    quarter = features // 4

    def around(value):
        return lax.rem(value + 2 * AROUND, AROUND)

    xs = [device(group, half, spot + 1, core), device(group, half, spot - 1, core)]
    zs = [
        device(lows * AROUND + around(depth + 1), half, spot, core),
        device(lows * AROUND + around(depth - 1), half, spot, core),
    ]
    near = device((1 - lows) * AROUND + depth, 1 - half, spot, core)
    across = device(group, 1 - half, spot, core)
    beside = device((1 - lows) * AROUND + depth, half, spot, core)
    sibling = device(group, half, spot, 1 - core)
    offsets = [(0, 1), (0, -1), (1, 0), (0, 2), (1, 1), (1, -1), (1, 2)]

    def group_at(low, deep):
        return lax.rem(lows + low, 2) * AROUND + around(depth + deep)

    local = [
        pltpu.make_async_copy(src, dst, l_sem.at[i])
        for i, (src, dst) in enumerate(
            [(ck_hbm, ck_ref), (cv_hbm, cv_ref), (wq_hbm, wq_ref), (wk_hbm, wk_ref), (wv_hbm, wv_ref)]
        )
    ]
    for each in local:
        each.start()
    greet(
        xs + zs + [near, across, beside, sibling]
        + [device(group_at(*o), half, spot, core) for o in offsets[3:]]
    )

    def copy(src, dst, send, recv, to):
        return pltpu.make_async_remote_copy(
            src_ref=src, dst_ref=dst, send_sem=send, recv_sem=recv, device_id=to, device_id_type=MESH
        )

    mine = pl.multiple_of(core * rows, rows)
    twin = pl.multiple_of((1 - core) * rows, rows)

    def block(owner, start=0, size=rows, base=mine):
        return normed.at[owner, pl.ds(pl.multiple_of(base + start, size), size)]

    def x_copy(d, owner=spot):
        return copy(block(owner), block(owner), x_send.at[d], x_recv.at[d], xs[d])

    def f_copy(d, owner):
        piece = block(owner, d * (rows // 2), rows // 2)
        return copy(piece, piece, f_send.at[d], f_recv.at[d], xs[d])

    def s_copy(i, owner, base=mine):
        piece = block(owner, base=base)
        return copy(piece, piece, s_send.at[i], s_recv.at[i], sibling)

    mine_first, theirs_first = 2 * lows, 2 * (1 - lows)

    def slab(q, p):
        return weights.at[q, pl.ds(pl.multiple_of(p * quarter, quarter), quarter)]

    def y_start(j):
        piece = (theirs_first if j < 2 else mine_first) + j % 2
        part = pl.ds(pl.multiple_of(piece * quarter, quarter), quarter)
        sources = [
            wq_hbm.at[part, pl.ds(0, HEAD)], wq_hbm.at[part, pl.ds(HEAD, HEAD)],
            wk_hbm.at[part], wv_hbm.at[part],
        ]
        for z, src in enumerate(sources):
            @pl.when(depth == z)
            def _(src=src):
                copy(src, slab(depth, piece), y_send.at[j], y_recv.at[j], near).start()

    def y_done(j):
        piece = slab(depth, nth_piece(j))
        return copy(piece, piece, y_send.at[j], y_recv.at[j], near)

    def w_copy(i, q, p):
        return copy(slab(q, p), slab(q, p), w_send.at[i], w_recv.at[i], beside)

    def nth_piece(n):
        return (mine_first if n < 2 else theirs_first) + n % 2

    def z_copy(d, n, q=depth):
        piece = slab(q, nth_piece(n))
        return copy(piece, piece, z_send.at[d, n], z_recv.at[d, n], zs[d])

    def g_copy(d, q):
        piece = slab(q, mine_first + d)
        return copy(piece, piece, g_send.at[d], g_recv.at[d], zs[d])

    pages, stretch = ck_ref.shape[:2]
    groups = table_ref.shape[0]

    def picked(target):
        index = 0
        for c in range(table_ref.shape[1]):
            page = table_ref[target, c]
            index = index + jnp.where(page // pages == group, page % pages, 0)
        return index

    def p_copy(j, source):
        return copy(
            outgoing.at[j], pages_ref.at[source], p_send.at[j], p_recv.at[j],
            device(group_at(*offsets[j]), half, spot, core),
        )

    def send_pages():
        for each in local[:2]:
            each.wait()
        for j, offset in enumerate(offsets):
            index = picked(group_at(*offset))
            outgoing[j, :, :HEAD] = ck_ref[index]
            outgoing[j, :, HEAD:] = cv_ref[index]
            p_copy(j, group).start()
        index = picked(group)
        pages_ref[group, :, :HEAD] = ck_ref[index]
        pages_ref[group, :, HEAD:] = cv_ref[index]

    def make_tables():
        layout = Layout(owners_ref, counts_ref, stretch)
        below = lax.broadcasted_iota(jnp.int32, (stretch, 1), 0)
        for i in range(cos_ref.shape[0] // stretch):
            row = below + (half * cos_ref.shape[0] + i * stretch)
            code = layout.of_queries(row - selected)
            if i == 0:
                code = jnp.where(row < selected, layout.of_cached(ids_ref[...]), code)
            angle = (code - request_base(code)).astype(jnp.float32) * freq_ref[...]
            sine = jnp.sin(angle)
            lane = lax.broadcasted_iota(jnp.int32, sine.shape, 1)
            cos_ref[pl.ds(i * stretch, stretch), :] = jnp.cos(angle)
            sin_ref[pl.ds(i * stretch, stretch), :] = jnp.where(lane < HEAD // 2, -sine, sine)

    def table(ref, owner):
        return ref[pl.ds(pl.multiple_of(owner * 2 * rows, 2 * rows), 2 * rows), :]

    def own_heads(owner):
        source = normed[owner]
        cosine, sine = table(cos_ref, owner), table(sin_ref, owner)
        to = pl.ds(pl.multiple_of((half * AROUND + owner) * 2 * rows, 2 * rows), 2 * rows)
        q = jnp.dot(source, wq_ref[...], preferred_element_type=jnp.float32)
        heads_ref[0, to] = turned(q[:, :HEAD], cosine, sine).astype(jnp.bfloat16)
        heads_ref[1, to] = turned(q[:, HEAD:], cosine, sine).astype(jnp.bfloat16)
        k = jnp.dot(source, wk_ref[...], preferred_element_type=jnp.float32)
        heads_ref[2, to] = turned(k, cosine, sine).astype(jnp.bfloat16)
        v = jnp.dot(source, wv_ref[...], preferred_element_type=jnp.float32)
        heads_ref[3, to] = v.astype(jnp.bfloat16)

    def e_copy(i, b, owner, q):
        to = pl.ds(pl.multiple_of((half * AROUND + owner) * 2 * rows, 2 * rows), 2 * rows)
        return copy(ship.at[i, b], heads_ref.at[q, to], e_send.at[i, b], e_recv.at[i, b], across)

    def nth(base, i):
        return around(base + (i * (7 - i)) // 2)

    owners = [nth(spot, b) for b in range(4)]
    quarters = [nth(depth, i) for i in range(4)]

    def their_heads(i, b):
        owner, q = nth(spot, b), nth(depth, i)
        u = jnp.dot(normed[owner], weights[q], preferred_element_type=jnp.float32)
        plain = (q == 3).astype(jnp.float32)
        cosine, sine = table(cos_ref, owner), table(sin_ref, owner)
        cosine = cosine + plain * (1.0 - cosine)
        sine = sine * (1.0 - plain)
        ship[i, b] = turned(u, cosine, sine).astype(jnp.bfloat16)
        e_copy(i, b, owner, q).start()

    def own_blocks(first, last):
        def step(b, carry):
            own_heads(nth(spot, b))
            return carry

        lax.fori_loop(first, last, step, 0)

    def their_blocks(i0, i1, b0, b1):
        def step(n, carry):
            their_heads(i0 + n // (b1 - b0), b0 + lax.rem(n, b1 - b0))
            return carry

        lax.fori_loop(0, (i1 - i0) * (b1 - b0), step, 0)

    left, right, far = owners[1], owners[2], owners[3]
    below, above, beyond = quarters[1], quarters[2], quarters[3]
    y_start(0)
    y_start(1)
    wide = hid_ref[...].astype(jnp.float32)
    scale = lax.rsqrt(jnp.mean(wide * wide, axis=-1, keepdims=True) + EPSILON)
    normed[spot, pl.ds(mine, rows)] = (wide * scale * gain_ref[...]).astype(jnp.bfloat16)
    x_copy(0).start()
    x_copy(1).start()
    s_copy(0, spot).start()
    send_pages()
    make_tables()
    for each in local[2:]:
        each.wait()
    for n in range(2):
        y_done(n).wait_recv()
        z_copy(0, n).start()
        z_copy(1, n).start()
        y_start(n + 2)
    s_copy(0, spot, twin).wait_recv()
    own_blocks(0, 1)
    for n in range(2):
        y_done(n + 2).wait_recv()
        z_copy(0, n + 2).start()
        z_copy(1, n + 2).start()
    their_blocks(0, 1, 0, 1)
    z_copy(0, 0, below).wait_recv()
    g_copy(0, below).start()
    z_copy(1, 1, above).wait_recv()
    g_copy(1, above).start()
    x_copy(0, left).wait_recv()
    f_copy(0, left).start()
    s_copy(1, left).start()
    x_copy(1, right).wait_recv()
    f_copy(1, right).start()
    s_copy(2, right).start()
    s_copy(1, left, twin).wait_recv()
    s_copy(2, right, twin).wait_recv()
    their_blocks(0, 1, 1, 3)
    for n in range(1, 4):
        z_copy(0, n, below).wait_recv()
    for n in (0, 2, 3):
        z_copy(1, n, above).wait_recv()
    g_copy(0, beyond).wait_recv()
    w_copy(0, beyond, mine_first).start()
    g_copy(1, beyond).wait_recv()
    w_copy(1, beyond, mine_first + 1).start()
    their_blocks(1, 3, 0, 3)
    own_blocks(1, 3)
    w_copy(0, beyond, theirs_first).wait_recv()
    w_copy(1, beyond, theirs_first + 1).wait_recv()
    their_blocks(3, 4, 0, 3)
    f_copy(0, far).wait_recv()
    f_copy(1, far).wait_recv()
    s_copy(3, far).start()
    s_copy(3, far, twin).wait_recv()
    their_blocks(0, 4, 3, 4)
    own_blocks(3, 4)
    for i in range(4):
        for b in range(4):
            to = pl.ds(
                pl.multiple_of(((1 - half) * AROUND + owners[b]) * 2 * rows, 2 * rows), 2 * rows
            )
            copy(
                ship.at[i, b], heads_ref.at[quarters[i], to], e_send.at[i, b], e_recv.at[i, b], across
            ).wait()
    for d in range(2):
        x_copy(d).wait_send()
        f_copy(d, owners[1 + d]).wait_send()
        for n in range(4):
            z_copy(d, n).wait_send()
        g_copy(d, quarters[1 + d]).wait_send()
    for i in range(4):
        s_copy(i, owners[i]).wait_send()
    for n in range(2):
        w_copy(n, beyond, mine_first + n).wait_send()
    for n in range(4):
        y_done(n).wait_send()
    for j, (low, deep) in enumerate(offsets):
        p_copy(j, group_at(low, -deep)).wait()


def project_in(
    own_rows, gain, w_query, w_key, w_value, cache_keys, cache_values,
    owners, counts, table, selected, ids_col, new_rows,
):
    rows, features = own_rows.shape
    pages, stretch = cache_keys.shape[:2]
    vmem = pl.BlockSpec(memory_space=pltpu.VMEM)
    smem = pl.BlockSpec(memory_space=pltpu.SMEM)
    hbm = pl.BlockSpec(memory_space=pltpu.HBM)
    dma = pltpu.SemaphoreType.DMA
    pairs = [(7,), (2,), (2,), (4,), (4,), (2,), (2, 4), (2,), (4, 4)]
    bf16 = jnp.bfloat16
    return pl.pallas_call(
        functools.partial(project_in_kernel, selected),
        out_shape=(
            jax.ShapeDtypeStruct((4, new_rows, HEAD), bf16),
            jax.ShapeDtypeStruct((table.shape[0], stretch, 2 * HEAD), bf16),
        ),
        in_specs=[smem] * 3 + [vmem] * 4 + [hbm] * 5,
        out_specs=(vmem, vmem),
        scratch_shapes=[
            pltpu.VMEM((AROUND, 2 * rows, features), bf16),
            pltpu.VMEM((4, features, HEAD), bf16),
            pltpu.VMEM((4, 4, 2 * rows, HEAD), bf16),
            pltpu.VMEM(w_query.shape, bf16), pltpu.VMEM(w_key.shape, bf16),
            pltpu.VMEM(w_value.shape, bf16),
            pltpu.VMEM(cache_keys.shape, bf16), pltpu.VMEM(cache_values.shape, bf16),
            pltpu.VMEM((7, stretch, 2 * HEAD), bf16),
            pltpu.VMEM((new_rows // 2, HEAD), jnp.float32),
            pltpu.VMEM((new_rows // 2, HEAD), jnp.float32),
            dma((5,)),
        ] + [dma(shape) for shape in pairs for _ in range(2)],
        compiler_params=pltpu.CompilerParams(
            collective_id=2, has_side_effects=True, vmem_limit_bytes=52 << 20
        ),
        name="project_in",
    )(
        owners, counts, table, own_rows, gain[None, :],
        np.concatenate([frequencies()] * 2)[None, :], ids_col,
        w_query, w_key, w_value, cache_keys, cache_values,
    )


def on_device(
    hidden, input_gain, w_query, w_key, w_value, w_out, post_gain, cache_keys, cache_values,
    page_table, stretch_request, recompute_ids, query_counts,
):
    own_rows = hidden[0]
    new_rows = own_rows.shape[0] * lax.axis_size("tok")
    stretch = cache_keys.shape[1]
    owners, counts, ids = stretch_request[0], query_counts[0], recompute_ids[0]
    selected = ids.shape[0]
    padded = jnp.pad(ids, (0, stretch - selected), constant_values=-1)
    ids_col, ids_row = padded[:, None], padded[None, :]
    heads, pages = project_in(
        own_rows, input_gain, w_query, w_key, w_value, cache_keys, cache_values,
        owners, counts, page_table, selected, ids_col, new_rows,
    )
    output = project(
        heads, pages, owners, counts, page_table, selected, ids_col, ids_row, w_out, own_rows,
        post_gain,
    )
    return output[None]


def solution(mesh):
    return jax.shard_map(
        on_device,
        mesh=mesh,
        in_specs=(
            P("grp", "tok", None), P(), P(None, "tok"), P(None, "tok"), P(None, "tok"),
            P("tok", None), P(), P("grp", None, "tok"), P("grp", None, "tok"), P(),
            P("grp", None), P("grp", None), P("grp", None),
        ),
        out_specs=P("grp", "tok", None),
        check_vma=False,
    )
```

```python
import functools
import math

import jax
import jax.numpy as jnp
import numpy as np
from jax import lax
from jax.experimental import pallas as pl
from jax.experimental.pallas import tpu as pltpu
from jax.sharding import PartitionSpec as P

HEAD = 128
EPSILON = 1e-06
CAP_VALUE = 50.0
QUERY_SCALE = 1.0 / 12.0
ROPE_BASE = 10000.0
SPAN = 1 << 16
FAR = 1 << 30
BLOCK = 512


def frequencies():
    ladder = np.arange(HEAD // 2, dtype=np.float32)
    return np.exp(ladder * np.float32(-2.0 * math.log(ROPE_BASE) / HEAD)).astype(np.float32)


def turned(u, cosine, sine):
    return u * cosine + pltpu.roll(u, HEAD // 2, 1) * sine


def request_base(code):
    return jnp.where(code >= 2 * SPAN, 2 * SPAN, jnp.where(code >= SPAN, SPAN, 0))


class View:
    def __init__(self, ref, base, shape):
        self.ref, self.base, self.shape = ref, base, shape

    def __getitem__(self, index):
        if isinstance(index, tuple):
            index = index[0] * self.shape[1] + index[1]
        return self.ref[self.base + index]


def views(meta_ref, sizes):
    slots, requests, groups = sizes
    return (
        View(meta_ref, 0, (slots,)), View(meta_ref, slots, (requests,)),
        View(meta_ref, slots + requests, (groups, slots)),
    )


class Layout:
    def __init__(self, owners, counts, stretch):
        slots = owners.shape[0]
        self.stretch = stretch
        self.owners = [owners[c] for c in range(slots)]
        held = [sum((o == r).astype(jnp.int32) for o in self.owners) for r in range(3)]
        first = [0, held[0], held[0] + held[1]]
        self.offsets = []
        self.slot_bases = []
        for c, o in enumerate(self.owners):
            start = jnp.where(o == 0, first[0], jnp.where(o == 1, first[1], first[2]))
            self.offsets.append(c - start)
            self.slot_bases.append(o * SPAN - start * stretch)
        self.starts = [0, counts[0], counts[0] + counts[1]]
        self.query_bases = [r * SPAN + held[r] * stretch - self.starts[r] for r in range(3)]

    def of_queries(self, m):
        base = jnp.where(
            m >= self.starts[2], self.query_bases[2],
            jnp.where(m >= self.starts[1], self.query_bases[1], self.query_bases[0]),
        )
        return m + base

    def of_cached(self, ids):
        base = self.slot_bases[0]
        for c in range(1, len(self.slot_bases)):
            base = jnp.where(ids >= c * self.stretch, self.slot_bases[c], base)
        return ids + base

    def request_of(self, m):
        return (m >= self.starts[1]).astype(jnp.int32) + (m >= self.starts[2]).astype(jnp.int32)


MESH = pl.DeviceIdType.MESH
RINGS = 4
AROUND = 4


def place():
    tok = lax.axis_index("tok")
    return lax.axis_index("grp"), tok // 8, (tok // 2) % AROUND, tok % 2


def device(group, half, spot, core):
    return (group, half * 8 + lax.rem(spot + 2 * AROUND, AROUND) * 2 + core)


def greet(partners):
    barrier = pltpu.get_barrier_semaphore()
    for partner in partners:
        pl.semaphore_signal(barrier, inc=1, device_id=partner, device_id_type=MESH)
    pl.semaphore_wait(barrier, len(partners))


def make_attention(
    selected, layout, table_ref, heads_ref, pages_ref, pcos_ref, psin_ref,
    ids_col_ref, ids_row_ref, attended, keys, values, key_codes, row_codes, row_bases, queries, totals,
):
    rows = heads_ref.shape[1]
    groups, stretch = pages_ref.shape[:2]
    cached = groups * stretch
    group = lax.axis_index("grp")
    lane = lax.broadcasted_iota(jnp.int32, (1, stretch), 1)
    below = lax.broadcasted_iota(jnp.int32, (stretch, 1), 0)
    ids_col = ids_col_ref[...]
    per = BLOCK // stretch

    def put_codes(i, codes):
        key_codes[i // per, :, pl.ds((i % per) * stretch, stretch)] = codes

    def lay_cached():
        for c in range(groups):
            page = table_ref[group, c]
            source = page // (table_ref.shape[1])
            part = pl.ds(c * stretch, stretch)
            turn = layout.offsets[c]
            k = pages_ref[source, :, :HEAD].astype(jnp.float32)
            k = turned(k, pcos_ref[pl.ds(turn, 1), :], psin_ref[pl.ds(turn, 1), :])
            keys[part, :] = k.astype(jnp.bfloat16)
            values[part, :HEAD] = pages_ref[source, :, HEAD:]
            ids = lane + c * stretch
            dead = jnp.max((ids_col == ids).astype(jnp.int32), axis=0, keepdims=True)
            put_codes(c, jnp.where(dead > 0, FAR, ids + layout.slot_bases[c]))

    def lay_new():
        keys[pl.ds(cached, rows), :] = heads_ref[2]
        values[pl.ds(cached, rows), :HEAD] = heads_ref[3]
        values[:, HEAD:] = jnp.ones((cached + rows, HEAD), jnp.bfloat16)
        for i in range(rows // stretch):
            by_lane = layout.of_queries(lane + (i * stretch - selected))
            by_row = layout.of_queries(below + (i * stretch - selected))
            if i == 0:
                by_lane = jnp.where(lane < selected, layout.of_cached(ids_row_ref[...]), by_lane)
                by_row = jnp.where(below < selected, layout.of_cached(ids_col), by_row)
            put_codes(groups + i, by_lane)
            row_codes[pl.ds(i * stretch, stretch), :] = by_row
            row_bases[pl.ds(i * stretch, stretch), :] = request_base(by_row)

    ahead = cached // BLOCK

    def attend(rb, first, last):
        here = pl.ds(pl.multiple_of(rb * BLOCK, BLOCK), BLOCK)
        queries[:BLOCK, :] = heads_ref[0, here, :]
        queries[BLOCK:, :] = heads_ref[1, here, :]
        code = row_codes[here, :]
        base = row_bases[here, :]

        def key_block(kb, carry):
            there = pl.ds(pl.multiple_of(kb * BLOCK, BLOCK), BLOCK)
            scores = lax.dot_general(
                queries[...], keys[there, :], (((1,), (1,)), ((), ())),
                preferred_element_type=jnp.float32,
            )
            capped = jnp.tanh(scores * (QUERY_SCALE / CAP_VALUE))
            weights = jnp.exp2(capped * (CAP_VALUE * math.log2(math.e)))
            key_code = key_codes[kb]
            seen = (key_code <= code) & (key_code >= base)
            both = jnp.concatenate([seen, seen], axis=0)
            rounded = jnp.where(both, weights, 0.0).astype(jnp.bfloat16)
            totals[rb] += jnp.dot(rounded, values[there, :], preferred_element_type=jnp.float32)
            return carry

        lax.fori_loop(first, last, key_block, 0)

    def see_new(rb):
        totals[rb] = jnp.zeros(totals.shape[1:], jnp.float32)
        attend(rb, ahead, ahead + rb + 1)

    def see_cached(rb):
        attend(rb, 0, ahead)
        here = pl.ds(pl.multiple_of(rb * BLOCK, BLOCK), BLOCK)
        quotient = totals[rb, :, :HEAD] / totals[rb, :, HEAD:]
        attended[here, :HEAD] = quotient[:BLOCK].astype(jnp.bfloat16)
        attended[here, HEAD:] = quotient[BLOCK:].astype(jnp.bfloat16)

    return lay_new, lay_cached, see_new, see_cached


def project_kernel(
    selected, sizes, meta_ref, heads_ref, ck_ref, cv_ref, pcos_ref, psin_ref,
    ids_col_ref, ids_row_ref, w0_ref, hid_ref, gain_ref, out_ref,
    pages_ref, outgoing, attn_ref, keys, values, key_codes, row_codes, row_bases, queries, totals,
    w1_ref, other, product, own, pair_out, pair_in, ring_out, ring_in, result,
    other_send, other_recv, pair_send, pair_recv, ring_send, ring_recv, o_send, o_recv, p_send, p_recv,
):
    group, half, spot, core = place()
    rows = hid_ref.shape[0]
    width = hid_ref.shape[1] // RINGS
    chunk = 2 * rows
    across = device(group, 1 - half, spot, core)
    sibling = device(group, half, spot, 1 - core)
    lows, depth = group // AROUND, group % AROUND
    zs = [
        device(lows * AROUND + lax.rem(depth + 1, AROUND), half, spot, core),
        device(lows * AROUND + lax.rem(depth + AROUND - 1, AROUND), half, spot, core),
    ]
    near = device((1 - lows) * AROUND + depth, 1 - half, spot, core)
    beside = device((1 - lows) * AROUND + depth, half, spot, core)
    offsets = [(0, 1), (0, -1), (1, 0), (0, 2), (1, 1), (1, -1), (1, 2)]

    def group_at(low, deep):
        return lax.rem(lows + low, 2) * AROUND + lax.rem(depth + deep + AROUND, AROUND)

    greet(
        [across, sibling, device(group, half, spot + 1, core), device(group, half, spot - 1, core)]
        + zs + [near, beside] + [device(group_at(*o), half, spot, core) for o in offsets[3:]]
    )
    owners_ref, counts_ref, table_ref = views(meta_ref, sizes)
    pages, stretch = ck_ref.shape[:2]

    def o_copy(i, src, step, n, to):
        size = w0_ref.shape[0] // (2 * AROUND)
        piece = lax.rem(depth + step + AROUND, AROUND) * 2 + n
        part = pl.ds(pl.multiple_of(piece * size, size), size)
        return pltpu.make_async_remote_copy(
            src_ref=src.at[part], dst_ref=w1_ref.at[part], send_sem=o_send.at[i],
            recv_sem=o_recv.at[i], device_id=to, device_id_type=MESH,
        )

    first, second = lows, 1 - lows
    o_copy(0, w0_ref, 0, second, near).start()

    def picked(target):
        index = 0
        for c in range(table_ref.shape[1]):
            page = table_ref[target, c]
            index = index + jnp.where(page // pages == group, page % pages, 0)
        return index

    def p_copy(j, source):
        return pltpu.make_async_remote_copy(
            src_ref=outgoing.at[j], dst_ref=pages_ref.at[source], send_sem=p_send.at[j],
            recv_sem=p_recv.at[j], device_id=device(group_at(*offsets[j]), half, spot, core),
            device_id_type=MESH,
        )

    for j, offset in enumerate(offsets):
        index = picked(group_at(*offset))
        outgoing[j, :, :HEAD] = ck_ref[index]
        outgoing[j, :, HEAD:] = cv_ref[index]
        p_copy(j, group).start()
    index = picked(group)
    pages_ref[group, :, :HEAD] = ck_ref[index]
    pages_ref[group, :, HEAD:] = cv_ref[index]
    lay_new, lay_cached, see_new, see_cached = make_attention(
        selected, Layout(owners_ref, counts_ref, stretch), table_ref, heads_ref, pages_ref,
        pcos_ref, psin_ref, ids_col_ref, ids_row_ref, attn_ref, keys, values, key_codes, row_codes,
        row_bases, queries, totals,
    )

    def other_copy(j):
        owner = lax.rem(spot + (3, 1, 2, 0)[j], AROUND)
        start = pl.multiple_of(((1 - half) * AROUND + owner) * chunk, chunk)
        return pltpu.make_async_remote_copy(
            src_ref=attn_ref.at[pl.ds(start, chunk)], dst_ref=other.at[j],
            send_sem=other_send.at[j], recv_sem=other_recv.at[j],
            device_id=across, device_id_type=MESH,
        )

    def pair_copy(s, r):
        return pltpu.make_async_remote_copy(
            src_ref=pair_out.at[s, r], dst_ref=pair_in.at[s, r],
            send_sem=pair_send.at[s, r], recv_sem=pair_recv.at[s, r],
            device_id=sibling, device_id_type=MESH,
        )

    def ring_copy(s, r):
        return pltpu.make_async_remote_copy(
            src_ref=ring_out.at[s, r], dst_ref=ring_in.at[s, r],
            send_sem=ring_send.at[s, r], recv_sem=ring_recv.at[s, r],
            device_id=device(group, half, spot + 1 - 2 * (r // 2), core), device_id_type=MESH,
        )

    per_half = attn_ref.shape[0] // BLOCK // 2

    def blocks_of(one_half, see):
        def step(i, carry):
            see(one_half * per_half + i)
            return carry

        lax.fori_loop(0, per_half, step, 0)

    lay_new()
    blocks_of(half, see_new)
    o_copy(0, w1_ref, 0, first, near).wait_recv()
    o_copy(1, w1_ref, 0, first, beside).start()
    for d in range(2):
        o_copy(2 + d, w1_ref, 0, first, zs[d]).start()
    blocks_of(1 - half, see_new)
    o_copy(1, w1_ref, 0, second, beside).wait_recv()
    for d in range(2):
        o_copy(4 + d, w1_ref, 0, second, zs[d]).start()
    for j, (low, deep) in enumerate(offsets):
        p_copy(j, group_at(low, -deep)).wait()
    lay_cached()
    o_copy(2, w1_ref, -1, first, zs[0]).wait_recv()
    o_copy(6, w1_ref, -1, first, zs[0]).start()
    blocks_of(1 - half, see_cached)
    for j in range(4):
        other_copy(j).start()
    o_copy(5, w1_ref, 1, second, zs[1]).wait_recv()
    o_copy(7, w1_ref, 1, second, zs[1]).start()
    blocks_of(half, see_cached)
    o_copy(3, w1_ref, 1, first, zs[1]).wait_recv()
    o_copy(4, w1_ref, -1, second, zs[0]).wait_recv()
    o_copy(6, w1_ref, 2, first, zs[0]).wait_recv()
    o_copy(7, w1_ref, 2, second, zs[1]).wait_recv()

    def partial(s, r):
        owner = lax.rem(spot + (2 * (r // 2) - 1) * (1 + s) + 2 * AROUND, AROUND)
        slot = (r // 2, 2, 1 - r // 2, 3)[s]
        start = pl.multiple_of((half * AROUND + owner) * chunk, chunk)
        columns = pl.ds(pl.multiple_of(r * width, width), width)
        product[...] = jnp.dot(
            attn_ref[pl.ds(start, chunk), :], w0_ref[:, columns], preferred_element_type=jnp.float32
        ) + jnp.dot(other[slot], w1_ref[:, columns], preferred_element_type=jnp.float32)
        theirs = pl.ds(pl.multiple_of((1 - core) * rows, rows), rows)
        pair_out[s, r] = product[theirs, :].astype(jnp.bfloat16)
        pair_copy(s, r).start()
        own[s, r] = product[pl.ds(pl.multiple_of(core * rows, rows), rows), :]

    def partials(s, first, last):
        def step(r, carry):
            partial(s, r)
            return carry

        lax.fori_loop(first, last, step, 0)

    def forward(s):
        def step(r, carry):
            pair_copy(s, r).wait_recv()
            running = own[s, r] + pair_in[s, r].astype(jnp.float32)
            if s > 0:
                ring_copy(s - 1, r).wait_recv()
                running = running + ring_in[s - 1, r].astype(jnp.float32)
            if s < 3:
                ring_out[s, r] = running.astype(jnp.bfloat16)
                ring_copy(s, r).start()
            else:
                result[:, pl.ds(pl.multiple_of(r * width, width), width)] = running
            return carry

        for r in (0, 2, 1, 3):
            step(r, 0)

    other_copy(0).wait_recv()
    partials(0, 0, 2)
    other_copy(1).wait_recv()
    partials(0, 2, 4)
    forward(0)
    other_copy(2).wait_recv()
    partials(1, 0, 4)
    partials(2, 0, 4)
    other_copy(3).wait_recv()
    partials(3, 0, 4)
    forward(1)
    forward(2)
    forward(3)
    for j in range(4):
        other_copy(j).wait_send()
    for i in range(8):
        o_copy(i, w1_ref, 0, first, near).wait_send()

    def drain(r, carry):
        for s in range(4):
            pair_copy(s, r).wait_send()
        for s in range(3):
            ring_copy(s, r).wait_send()
        return carry

    lax.fori_loop(0, RINGS, drain, 0)
    projected = result[...]
    scale = lax.rsqrt(jnp.mean(projected * projected, axis=-1, keepdims=True) + EPSILON)
    out_ref[...] = (
        hid_ref[...].astype(jnp.float32) + projected * scale * gain_ref[...]
    ).astype(jnp.bfloat16)


def project(
    heads, cache_keys, cache_values, meta, sizes, selected, ids_col, ids_row, w_own, own_rows, post_gain
):
    rows, features = own_rows.shape
    width = features // RINGS
    new_rows = heads.shape[1]
    groups, stretch = sizes[2], cache_keys.shape[1]
    total_keys = groups * stretch + new_rows
    angles = (np.arange(groups, dtype=np.float32) * stretch)[:, None] * frequencies()[None, :]
    cosine, sine = np.cos(angles), np.sin(angles)
    vmem = pl.BlockSpec(memory_space=pltpu.VMEM)
    smem = pl.BlockSpec(memory_space=pltpu.SMEM)
    dma = pltpu.SemaphoreType.DMA
    return pl.pallas_call(
        functools.partial(project_kernel, selected, sizes),
        out_shape=jax.ShapeDtypeStruct((rows, features), jnp.bfloat16),
        in_specs=[smem] + [vmem] * 10,
        out_specs=vmem,
        scratch_shapes=[
            pltpu.VMEM((groups, stretch, 2 * HEAD), jnp.bfloat16),
            pltpu.VMEM((groups - 1, stretch, 2 * HEAD), jnp.bfloat16),
            pltpu.VMEM((new_rows, 2 * HEAD), jnp.bfloat16),
            pltpu.VMEM((total_keys, HEAD), jnp.bfloat16),
            pltpu.VMEM((total_keys, 2 * HEAD), jnp.bfloat16),
            pltpu.VMEM((total_keys // BLOCK, 1, BLOCK), jnp.int32),
            pltpu.VMEM((new_rows, 1), jnp.int32),
            pltpu.VMEM((new_rows, 1), jnp.int32),
            pltpu.VMEM((2 * BLOCK, HEAD), jnp.bfloat16),
            pltpu.VMEM((new_rows // BLOCK, 2 * BLOCK, 2 * HEAD), jnp.float32),
            pltpu.VMEM(w_own.shape, jnp.bfloat16),
            pltpu.VMEM((4, 2 * rows, 2 * HEAD), jnp.bfloat16),
            pltpu.VMEM((2 * rows, width), jnp.float32),
            pltpu.VMEM((4, RINGS, rows, width), jnp.float32),
            pltpu.VMEM((4, RINGS, rows, width), jnp.bfloat16),
            pltpu.VMEM((4, RINGS, rows, width), jnp.bfloat16),
            pltpu.VMEM((3, RINGS, rows, width), jnp.bfloat16),
            pltpu.VMEM((3, RINGS, rows, width), jnp.bfloat16),
            pltpu.VMEM((rows, features), jnp.float32),
            dma((4,)), dma((4,)), dma((4, RINGS)), dma((4, RINGS)), dma((3, RINGS)), dma((3, RINGS)),
            dma((8,)), dma((8,)), dma((7,)), dma((7,)),
        ],
        compiler_params=pltpu.CompilerParams(
            collective_id=1, has_side_effects=True, vmem_limit_bytes=60 << 20
        ),
        name="project",
    )(
        meta, heads, cache_keys, cache_values,
        np.concatenate([cosine, cosine], axis=1), np.concatenate([-sine, sine], axis=1),
        ids_col, ids_row, w_own, own_rows, post_gain[None, :],
    )


def project_in_kernel(
    selected, sizes, stretch, meta_ref, hid_ref, gain_ref, freq_ref, ids_ref,
    wq_hbm, wk_hbm, wv_hbm, heads_ref,
    normed, weights, ship, wq_ref, wk_ref, wv_ref, cos_ref, sin_ref,
    l_sem, x_send, x_recv, f_send, f_recv, s_send, s_recv, y_send, y_recv, w_send, w_recv, z_send, z_recv,
    g_send, g_recv, e_send, e_recv,
):
    group, half, spot, core = place()
    rows, features = hid_ref.shape
    depth = group % AROUND
    lows = group // AROUND
    quarter = features // 8

    def around(value):
        return lax.rem(value + 2 * AROUND, AROUND)

    xs = [device(group, half, spot + 1, core), device(group, half, spot - 1, core)]
    zs = [
        device(lows * AROUND + around(depth + 1), half, spot, core),
        device(lows * AROUND + around(depth - 1), half, spot, core),
    ]
    near = device((1 - lows) * AROUND + depth, 1 - half, spot, core)
    across = device(group, 1 - half, spot, core)
    beside = device((1 - lows) * AROUND + depth, half, spot, core)
    sibling = device(group, half, spot, 1 - core)
    local = [
        pltpu.make_async_copy(src, dst, l_sem.at[i])
        for i, (src, dst) in enumerate(
            [(wq_hbm, wq_ref), (wk_hbm, wk_ref), (wv_hbm, wv_ref)]
        )
    ]
    for each in local:
        each.start()
    greet(xs + zs + [near, across, beside, sibling])
    owners_ref, counts_ref, _ = views(meta_ref, sizes)

    def copy(src, dst, send, recv, to):
        return pltpu.make_async_remote_copy(
            src_ref=src, dst_ref=dst, send_sem=send, recv_sem=recv, device_id=to, device_id_type=MESH
        )

    mine = pl.multiple_of(core * rows, rows)
    twin = pl.multiple_of((1 - core) * rows, rows)

    def block(owner, start=0, size=rows, base=mine):
        return normed.at[owner, pl.ds(pl.multiple_of(base + start, size), size)]

    def x_copy(d, owner=spot):
        return copy(block(owner), block(owner), x_send.at[d], x_recv.at[d], xs[d])

    def f_copy(d, owner):
        piece = block(owner, d * (rows // 2), rows // 2)
        return copy(piece, piece, f_send.at[d], f_recv.at[d], xs[d])

    def s_copy(i, owner, base=mine):
        piece = block(owner, base=base)
        return copy(piece, piece, s_send.at[i], s_recv.at[i], sibling)

    mine_first, theirs_first = 4 * lows, 4 * (1 - lows)

    def slab(q, p):
        return weights.at[q, pl.ds(pl.multiple_of(p * quarter, quarter), quarter)]

    def y_start(j):
        piece = (theirs_first if j < 4 else mine_first) + j % 4
        part = pl.ds(pl.multiple_of(piece * quarter, quarter), quarter)
        sources = [
            wq_hbm.at[part, pl.ds(0, HEAD)], wq_hbm.at[part, pl.ds(HEAD, HEAD)],
            wk_hbm.at[part], wv_hbm.at[part],
        ]
        for z, src in enumerate(sources):
            @pl.when(depth == z)
            def _(src=src):
                copy(src, slab(depth, piece), y_send.at[j], y_recv.at[j], near).start()

    def y_done(j):
        piece = slab(depth, nth_piece(j))
        return copy(piece, piece, y_send.at[j], y_recv.at[j], near)

    def w_copy(i, q, p):
        return copy(slab(q, p), slab(q, p), w_send.at[i], w_recv.at[i], beside)

    def nth_piece(n):
        return (mine_first if n < 4 else theirs_first) + n % 4

    def z_copy(d, n, q=depth):
        piece = slab(q, nth_piece(n))
        return copy(piece, piece, z_send.at[d, n], z_recv.at[d, n], zs[d])

    def g_copy(d, j, q):
        piece = slab(q, mine_first + 2 * d + j)
        return copy(piece, piece, g_send.at[d, j], g_recv.at[d, j], zs[d])

    def make_tables():
        layout = Layout(owners_ref, counts_ref, stretch)
        below = lax.broadcasted_iota(jnp.int32, (stretch, 1), 0)
        for i in range(cos_ref.shape[0] // stretch):
            row = below + (half * cos_ref.shape[0] + i * stretch)
            code = layout.of_queries(row - selected)
            if i == 0:
                code = jnp.where(row < selected, layout.of_cached(ids_ref[...]), code)
            angle = (code - request_base(code)).astype(jnp.float32) * freq_ref[...]
            sine = jnp.sin(angle)
            lane = lax.broadcasted_iota(jnp.int32, sine.shape, 1)
            cos_ref[pl.ds(i * stretch, stretch), :] = jnp.cos(angle)
            sin_ref[pl.ds(i * stretch, stretch), :] = jnp.where(lane < HEAD // 2, -sine, sine)

    def table(ref, owner):
        return ref[pl.ds(pl.multiple_of(owner * 2 * rows, 2 * rows), 2 * rows), :]

    def own_heads(owner):
        source = normed[owner]
        cosine, sine = table(cos_ref, owner), table(sin_ref, owner)
        to = pl.ds(pl.multiple_of((half * AROUND + owner) * 2 * rows, 2 * rows), 2 * rows)
        q = jnp.dot(source, wq_ref[...], preferred_element_type=jnp.float32)
        heads_ref[0, to] = turned(q[:, :HEAD], cosine, sine).astype(jnp.bfloat16)
        heads_ref[1, to] = turned(q[:, HEAD:], cosine, sine).astype(jnp.bfloat16)
        k = jnp.dot(source, wk_ref[...], preferred_element_type=jnp.float32)
        heads_ref[2, to] = turned(k, cosine, sine).astype(jnp.bfloat16)
        v = jnp.dot(source, wv_ref[...], preferred_element_type=jnp.float32)
        heads_ref[3, to] = v.astype(jnp.bfloat16)

    def e_copy(i, b, owner, q):
        to = pl.ds(pl.multiple_of((half * AROUND + owner) * 2 * rows, 2 * rows), 2 * rows)
        return copy(ship.at[i, b], heads_ref.at[q, to], e_send.at[i, b], e_recv.at[i, b], across)

    def nth(base, i):
        return around(base + (i * (7 - i)) // 2)

    owners = [nth(spot, b) for b in range(4)]
    quarters = [nth(depth, i) for i in range(4)]

    def their_heads(i, b):
        owner, q = nth(spot, b), nth(depth, i)
        u = jnp.dot(normed[owner], weights[q], preferred_element_type=jnp.float32)
        plain = (q == 3).astype(jnp.float32)
        cosine, sine = table(cos_ref, owner), table(sin_ref, owner)
        cosine = cosine + plain * (1.0 - cosine)
        sine = sine * (1.0 - plain)
        ship[i, b] = turned(u, cosine, sine).astype(jnp.bfloat16)
        e_copy(i, b, owner, q).start()

    def own_blocks(first, last):
        def step(b, carry):
            own_heads(nth(spot, b))
            return carry

        lax.fori_loop(first, last, step, 0)

    def their_blocks(i0, i1, b0, b1):
        def step(n, carry):
            their_heads(i0 + n // (b1 - b0), b0 + lax.rem(n, b1 - b0))
            return carry

        lax.fori_loop(0, (i1 - i0) * (b1 - b0), step, 0)

    left, right, far = owners[1], owners[2], owners[3]
    below, above, beyond = quarters[1], quarters[2], quarters[3]
    def pass_on(n):
        y_done(n).wait_recv()
        z_copy(0, n).start()
        z_copy(1, n).start()
        if n + 2 < 8:
            y_start(n + 2)

    y_start(0)
    y_start(1)
    wide = hid_ref[...].astype(jnp.float32)
    scale = lax.rsqrt(jnp.mean(wide * wide, axis=-1, keepdims=True) + EPSILON)
    normed[spot, pl.ds(mine, rows)] = (wide * scale * gain_ref[...]).astype(jnp.bfloat16)
    x_copy(0).start()
    x_copy(1).start()
    s_copy(0, spot).start()
    pass_on(0)
    pass_on(1)
    make_tables()
    pass_on(2)
    pass_on(3)
    for each in local:
        each.wait()
    s_copy(0, spot, twin).wait_recv()
    own_blocks(0, 1)
    pass_on(4)
    for j in range(2):
        z_copy(0, j, below).wait_recv()
        g_copy(0, j, below).start()
    pass_on(5)
    for j in range(2):
        z_copy(1, 2 + j, above).wait_recv()
        g_copy(1, j, above).start()
    pass_on(6)
    pass_on(7)
    x_copy(0, left).wait_recv()
    f_copy(0, left).start()
    s_copy(1, left).start()
    x_copy(1, right).wait_recv()
    f_copy(1, right).start()
    s_copy(2, right).start()
    their_blocks(0, 1, 0, 1)
    s_copy(1, left, twin).wait_recv()
    s_copy(2, right, twin).wait_recv()
    their_blocks(0, 1, 1, 3)
    for d in range(2):
        for j in range(2):
            g_copy(d, j, beyond).wait_recv()
            w_copy(2 * d + j, beyond, mine_first + 2 * d + j).start()
    for n in range(2, 8):
        z_copy(0, n, below).wait_recv()
    for n in (0, 1, 4, 5, 6, 7):
        z_copy(1, n, above).wait_recv()
    f_copy(0, far).wait_recv()
    f_copy(1, far).wait_recv()
    s_copy(3, far).start()
    their_blocks(1, 3, 0, 3)
    s_copy(3, far, twin).wait_recv()
    their_blocks(0, 3, 3, 4)
    for n in range(4):
        w_copy(n, beyond, theirs_first + n).wait_recv()
    their_blocks(3, 4, 0, 4)
    own_blocks(1, 4)
    for i in range(4):
        for b in range(4):
            to = pl.ds(
                pl.multiple_of(((1 - half) * AROUND + owners[b]) * 2 * rows, 2 * rows), 2 * rows
            )
            copy(
                ship.at[i, b], heads_ref.at[quarters[i], to], e_send.at[i, b], e_recv.at[i, b], across
            ).wait()
    for d in range(2):
        x_copy(d).wait_send()
        f_copy(d, owners[1 + d]).wait_send()
        for n in range(8):
            z_copy(d, n).wait_send()
        for j in range(2):
            g_copy(d, j, quarters[1 + d]).wait_send()
    for i in range(4):
        s_copy(i, owners[i]).wait_send()
    for n in range(4):
        w_copy(n, beyond, mine_first + n).wait_send()
    for n in range(8):
        y_done(n).wait_send()


def project_in(
    own_rows, gain, w_query, w_key, w_value, meta, sizes, stretch, selected, ids_col, new_rows,
):
    rows, features = own_rows.shape
    vmem = pl.BlockSpec(memory_space=pltpu.VMEM)
    smem = pl.BlockSpec(memory_space=pltpu.SMEM)
    hbm = pl.BlockSpec(memory_space=pltpu.HBM)
    dma = pltpu.SemaphoreType.DMA
    pairs = [(2,), (2,), (4,), (8,), (4,), (2, 8), (2, 2), (4, 4)]
    bf16 = jnp.bfloat16
    return pl.pallas_call(
        functools.partial(project_in_kernel, selected, sizes, stretch),
        out_shape=jax.ShapeDtypeStruct((4, new_rows, HEAD), bf16),
        in_specs=[smem] + [vmem] * 4 + [hbm] * 3,
        out_specs=vmem,
        scratch_shapes=[
            pltpu.VMEM((AROUND, 2 * rows, features), bf16),
            pltpu.VMEM((4, features, HEAD), bf16),
            pltpu.VMEM((4, 4, 2 * rows, HEAD), bf16),
            pltpu.VMEM(w_query.shape, bf16), pltpu.VMEM(w_key.shape, bf16),
            pltpu.VMEM(w_value.shape, bf16),
            pltpu.VMEM((new_rows // 2, HEAD), jnp.float32),
            pltpu.VMEM((new_rows // 2, HEAD), jnp.float32),
            dma((3,)),
        ] + [dma(shape) for shape in pairs for _ in range(2)],
        compiler_params=pltpu.CompilerParams(
            collective_id=2, has_side_effects=True, vmem_limit_bytes=52 << 20
        ),
        name="project_in",
    )(
        meta, own_rows, gain[None, :], np.concatenate([frequencies()] * 2)[None, :], ids_col,
        w_query, w_key, w_value,
    )


def on_device(
    hidden, input_gain, w_query, w_key, w_value, w_out, post_gain, cache_keys, cache_values,
    page_table, stretch_request, recompute_ids, query_counts,
):
    own_rows = hidden[0]
    new_rows = own_rows.shape[0] * lax.axis_size("tok")
    stretch = cache_keys.shape[1]
    owners, counts, ids = stretch_request[0], query_counts[0], recompute_ids[0]
    selected = ids.shape[0]
    padded = jnp.pad(ids, (0, stretch - selected), constant_values=-1)
    ids_col, ids_row = padded[:, None], padded[None, :]
    sizes = (owners.shape[0], counts.shape[0], page_table.shape[0])
    meta = jnp.concatenate([owners, counts, page_table.reshape(-1)])
    heads = project_in(
        own_rows, input_gain, w_query, w_key, w_value, meta, sizes, stretch, selected, ids_col, new_rows
    )
    output = project(
        heads, cache_keys, cache_values, meta, sizes, selected, ids_col, ids_row, w_out, own_rows,
        post_gain,
    )
    return output[None]


def solution(mesh):
    return jax.shard_map(
        on_device,
        mesh=mesh,
        in_specs=(
            P("grp", "tok", None), P(), P(None, "tok"), P(None, "tok"), P(None, "tok"),
            P("tok", None), P(), P("grp", None, "tok"), P("grp", None, "tok"), P(),
            P("grp", None), P("grp", None), P("grp", None),
        ),
        out_specs=P("grp", "tok", None),
        check_vma=False,
    )
```

```python
import functools
import math

import jax
import jax.numpy as jnp
import numpy as np
from jax import lax
from jax.experimental import pallas as pl
from jax.experimental.pallas import tpu as pltpu
from jax.sharding import PartitionSpec as P

HEAD = 128
EPSILON = 1e-06
CAP_VALUE = 50.0
QUERY_SCALE = 1.0 / 12.0
ROPE_BASE = 10000.0
SPAN = 1 << 16
FAR = 1 << 30
BLOCK = 512


def frequencies():
    ladder = np.arange(HEAD // 2, dtype=np.float32)
    return np.exp(ladder * np.float32(-2.0 * math.log(ROPE_BASE) / HEAD)).astype(np.float32)


def turned(u, cosine, sine):
    return u * cosine + pltpu.roll(u, HEAD // 2, 1) * sine


def request_base(code):
    return jnp.where(code >= 2 * SPAN, 2 * SPAN, jnp.where(code >= SPAN, SPAN, 0))


class View:
    def __init__(self, ref, base, shape):
        self.ref, self.base, self.shape = ref, base, shape

    def __getitem__(self, index):
        if isinstance(index, tuple):
            index = index[0] * self.shape[1] + index[1]
        return self.ref[self.base + index]


def views(meta_ref, sizes):
    slots, requests, groups = sizes
    return (
        View(meta_ref, 0, (slots,)), View(meta_ref, slots, (requests,)),
        View(meta_ref, slots + requests, (groups, slots)),
    )


class Layout:
    def __init__(self, owners, counts, stretch):
        slots = owners.shape[0]
        self.stretch = stretch
        self.owners = [owners[c] for c in range(slots)]
        held = [sum((o == r).astype(jnp.int32) for o in self.owners) for r in range(3)]
        first = [0, held[0], held[0] + held[1]]
        self.offsets = []
        self.slot_bases = []
        for c, o in enumerate(self.owners):
            start = jnp.where(o == 0, first[0], jnp.where(o == 1, first[1], first[2]))
            self.offsets.append(c - start)
            self.slot_bases.append(o * SPAN - start * stretch)
        self.starts = [0, counts[0], counts[0] + counts[1]]
        self.query_bases = [r * SPAN + held[r] * stretch - self.starts[r] for r in range(3)]

    def of_queries(self, m):
        base = jnp.where(
            m >= self.starts[2], self.query_bases[2],
            jnp.where(m >= self.starts[1], self.query_bases[1], self.query_bases[0]),
        )
        return m + base

    def of_cached(self, ids):
        base = self.slot_bases[0]
        for c in range(1, len(self.slot_bases)):
            base = jnp.where(ids >= c * self.stretch, self.slot_bases[c], base)
        return ids + base

    def request_of(self, m):
        return (m >= self.starts[1]).astype(jnp.int32) + (m >= self.starts[2]).astype(jnp.int32)


MESH = pl.DeviceIdType.MESH
RINGS = 4
AROUND = 4


def place():
    tok = lax.axis_index("tok")
    return lax.axis_index("grp"), tok // 8, (tok // 2) % AROUND, tok % 2


def device(group, half, spot, core):
    return (group, half * 8 + lax.rem(spot + 2 * AROUND, AROUND) * 2 + core)


def greet(partners):
    barrier = pltpu.get_barrier_semaphore()
    for partner in partners:
        pl.semaphore_signal(barrier, inc=1, device_id=partner, device_id_type=MESH)
    pl.semaphore_wait(barrier, len(partners))


def make_attention(
    selected, layout, table_ref, heads_ref, pages_ref, pcos_ref, psin_ref,
    ids_col_ref, ids_row_ref, attended, keys, values, cached_codes, key_codes, row_codes, row_bases, queries, totals,
):
    rows = heads_ref.shape[1]
    groups, stretch = pages_ref.shape[:2]
    cached = groups * stretch
    group = lax.axis_index("grp")
    lane = lax.broadcasted_iota(jnp.int32, (1, stretch), 1)
    below = lax.broadcasted_iota(jnp.int32, (stretch, 1), 0)
    ids_col = ids_col_ref[...]
    wide = cached_codes.shape[2]

    def put_codes(codes_ref, i, codes):
        per = codes_ref.shape[2] // stretch
        codes_ref[i // per, :, pl.ds((i % per) * stretch, stretch)] = codes

    def lay_cached():
        for c in range(groups):
            page = table_ref[group, c]
            source = page // (table_ref.shape[1])
            part = pl.ds(c * stretch, stretch)
            turn = layout.offsets[c]
            k = pages_ref[source, :, :HEAD].astype(jnp.float32)
            k = turned(k, pcos_ref[pl.ds(turn, 1), :], psin_ref[pl.ds(turn, 1), :])
            keys[part, :] = k.astype(jnp.bfloat16)
            values[part, :HEAD] = pages_ref[source, :, HEAD:]
            ids = lane + c * stretch
            dead = jnp.max((ids_col == ids).astype(jnp.int32), axis=0, keepdims=True)
            put_codes(cached_codes, c, jnp.where(dead > 0, FAR, ids + layout.slot_bases[c]))

    def lay_new():
        keys[pl.ds(cached, rows), :] = heads_ref[2]
        values[pl.ds(cached, rows), :HEAD] = heads_ref[3]
        values[:, HEAD:] = jnp.ones((cached + rows, HEAD), jnp.bfloat16)
        for i in range(rows // stretch):
            by_lane = layout.of_queries(lane + (i * stretch - selected))
            by_row = layout.of_queries(below + (i * stretch - selected))
            if i == 0:
                by_lane = jnp.where(lane < selected, layout.of_cached(ids_row_ref[...]), by_lane)
                by_row = jnp.where(below < selected, layout.of_cached(ids_col), by_row)
            put_codes(key_codes, i, by_lane)
            row_codes[pl.ds(i * stretch, stretch), :] = by_row
            row_bases[pl.ds(i * stretch, stretch), :] = request_base(by_row)

    def weigh(asked, there, key_code, code, base):
        scores = lax.dot_general(
            asked, keys[there, :], (((1,), (1,)), ((), ())), preferred_element_type=jnp.float32
        )
        capped = jnp.tanh(scores * (QUERY_SCALE / CAP_VALUE))
        weights = jnp.exp2(capped * (CAP_VALUE * math.log2(math.e)))
        seen = (key_code <= code) & (key_code >= base)
        both = jnp.concatenate([seen, seen], axis=0)
        rounded = jnp.where(both, weights, 0.0).astype(jnp.bfloat16)
        return jnp.dot(rounded, values[there, :], preferred_element_type=jnp.float32)

    def see_new(rb):
        here = pl.ds(pl.multiple_of(rb * BLOCK, BLOCK), BLOCK)
        queries[:BLOCK, :] = heads_ref[0, here, :]
        queries[BLOCK:, :] = heads_ref[1, here, :]
        code, base = row_codes[here, :], row_bases[here, :]
        totals[rb] = jnp.zeros(totals.shape[1:], jnp.float32)

        def key_block(kb, carry):
            there = pl.ds(pl.multiple_of(cached + kb * BLOCK, BLOCK), BLOCK)
            totals[rb] += weigh(queries[...], there, key_codes[kb], code, base)
            return carry

        lax.fori_loop(0, rb + 1, key_block, 0)

    def see_cached(qb):
        few = BLOCK // 2
        here = pl.ds(pl.multiple_of(qb * few, few), few)
        queries[:few, :] = heads_ref[0, here, :]
        queries[few:BLOCK, :] = heads_ref[1, here, :]
        code, base = row_codes[here, :], row_bases[here, :]
        rb = qb // 2
        low = pl.ds(pl.multiple_of(lax.rem(qb, 2) * few, few), few)
        high = pl.ds(pl.multiple_of(BLOCK + lax.rem(qb, 2) * few, few), few)

        def key_block(kb, carry):
            there = pl.ds(pl.multiple_of(kb * wide, wide), wide)
            more = weigh(queries[:BLOCK, :], there, cached_codes[kb], code, base)
            totals[rb, low, :] += more[:few]
            totals[rb, high, :] += more[few:]
            return carry

        lax.fori_loop(0, cached // wide, key_block, 0)
        for head, part in enumerate((low, high)):
            quotient = totals[rb, part, :HEAD] / totals[rb, part, HEAD:]
            attended[here, head * HEAD : (head + 1) * HEAD] = quotient.astype(jnp.bfloat16)

    return lay_new, lay_cached, see_new, see_cached


def project_kernel(
    selected, sizes, meta_ref, heads_ref, ck_ref, cv_ref, pcos_ref, psin_ref,
    ids_col_ref, ids_row_ref, w0_ref, w1_ref, hid_ref, gain_ref, out_ref,
    pages_ref, outgoing, attn_ref, keys, values, cached_codes, key_codes, row_codes, row_bases,
    queries, totals, other, product, own, pair_out, pair_in, ring_out, ring_in, result,
    other_send, other_recv, pair_send, pair_recv, ring_send, ring_recv, p_send, p_recv,
):
    group, half, spot, core = place()
    rows = hid_ref.shape[0]
    width = hid_ref.shape[1] // RINGS
    chunk = 2 * rows
    across = device(group, 1 - half, spot, core)
    sibling = device(group, half, spot, 1 - core)
    lows, depth = group // AROUND, group % AROUND
    zs = [
        device(lows * AROUND + lax.rem(depth + 1, AROUND), half, spot, core),
        device(lows * AROUND + lax.rem(depth + AROUND - 1, AROUND), half, spot, core),
    ]
    beside = device((1 - lows) * AROUND + depth, half, spot, core)
    offsets = [(0, 1), (0, -1), (1, 0), (0, 2), (1, 1), (1, -1), (1, 2)]

    def group_at(low, deep):
        return lax.rem(lows + low, 2) * AROUND + lax.rem(depth + deep + AROUND, AROUND)

    greet(
        [across, sibling, device(group, half, spot + 1, core), device(group, half, spot - 1, core)]
        + zs + [beside] + [device(group_at(*o), half, spot, core) for o in offsets[3:]]
    )
    owners_ref, counts_ref, table_ref = views(meta_ref, sizes)
    pages, stretch = ck_ref.shape[:2]

    def picked(target):
        index = 0
        for c in range(table_ref.shape[1]):
            page = table_ref[target, c]
            index = index + jnp.where(page // pages == group, page % pages, 0)
        return index

    def p_copy(j, source):
        return pltpu.make_async_remote_copy(
            src_ref=outgoing.at[j], dst_ref=pages_ref.at[source], send_sem=p_send.at[j],
            recv_sem=p_recv.at[j], device_id=device(group_at(*offsets[j]), half, spot, core),
            device_id_type=MESH,
        )

    for j, offset in enumerate(offsets):
        index = picked(group_at(*offset))
        outgoing[j, :, :HEAD] = ck_ref[index]
        outgoing[j, :, HEAD:] = cv_ref[index]
        p_copy(j, group).start()
    index = picked(group)
    pages_ref[group, :, :HEAD] = ck_ref[index]
    pages_ref[group, :, HEAD:] = cv_ref[index]
    lay_new, lay_cached, see_new, see_cached = make_attention(
        selected, Layout(owners_ref, counts_ref, stretch), table_ref, heads_ref, pages_ref,
        pcos_ref, psin_ref, ids_col_ref, ids_row_ref, attn_ref, keys, values, cached_codes, key_codes,
        row_codes, row_bases, queries, totals,
    )

    def other_copy(j):
        owner = lax.rem(spot + 3 - 2 * j + 3 * (j // 2) + AROUND, AROUND)
        start = pl.multiple_of(((1 - half) * AROUND + owner) * chunk, chunk)
        return pltpu.make_async_remote_copy(
            src_ref=attn_ref.at[pl.ds(start, chunk)], dst_ref=other.at[j],
            send_sem=other_send.at[j], recv_sem=other_recv.at[j],
            device_id=across, device_id_type=MESH,
        )

    def pair_copy(s, r):
        return pltpu.make_async_remote_copy(
            src_ref=pair_out.at[s, r], dst_ref=pair_in.at[s, r],
            send_sem=pair_send.at[s, r], recv_sem=pair_recv.at[s, r],
            device_id=sibling, device_id_type=MESH,
        )

    def ring_copy(s, r):
        return pltpu.make_async_remote_copy(
            src_ref=ring_out.at[s, r], dst_ref=ring_in.at[s, r],
            send_sem=ring_send.at[s, r], recv_sem=ring_recv.at[s, r],
            device_id=device(group, half, spot + 1 - 2 * (r // 2), core), device_id_type=MESH,
        )

    per_half = attn_ref.shape[0] // BLOCK // 2

    def blocks_of(one_half, see):
        def step(i, carry):
            see(one_half * per_half + i)
            return carry

        lax.fori_loop(0, per_half, step, 0)

    lay_new()
    blocks_of(half, see_new)
    blocks_of(1 - half, see_new)
    for j, (low, deep) in enumerate(offsets):
        p_copy(j, group_at(low, -deep)).wait()
    lay_cached()

    def finish_rows(first, last):
        count = last - first

        def step(n, carry):
            theirs = n < count
            j = first + lax.rem(n, count)
            owner = lax.rem(spot + 3 - 2 * j + 3 * (j // 2) + AROUND, AROUND)
            see_cached(jnp.where(theirs, 1 - half, half) * AROUND + owner)

            @pl.when(theirs)
            def _():
                other_copy(j).start()

            return carry

        lax.fori_loop(0, 2 * count, step, 0)

    def partial(s, r):
        owner = lax.rem(spot + (2 * (r // 2) - 1) * (1 + s) + 2 * AROUND, AROUND)
        slot = (r // 2, 2, 1 - r // 2, 3)[s]
        start = pl.multiple_of((half * AROUND + owner) * chunk, chunk)
        columns = pl.ds(pl.multiple_of(r * width, width), width)
        product[...] = jnp.dot(
            attn_ref[pl.ds(start, chunk), :], w0_ref[:, columns], preferred_element_type=jnp.float32
        ) + jnp.dot(other[slot], w1_ref[:, columns], preferred_element_type=jnp.float32)
        theirs = pl.ds(pl.multiple_of((1 - core) * rows, rows), rows)
        pair_out[s, r] = product[theirs, :].astype(jnp.bfloat16)
        pair_copy(s, r).start()
        own[s, r] = product[pl.ds(pl.multiple_of(core * rows, rows), rows), :]

    def partials(s, first, last):
        def step(r, carry):
            partial(s, r)
            return carry

        lax.fori_loop(first, last, step, 0)

    def forward(s):
        def step(r, carry):
            pair_copy(s, r).wait_recv()
            running = own[s, r] + pair_in[s, r].astype(jnp.float32)
            if s > 0:
                ring_copy(s - 1, r).wait_recv()
                running = running + ring_in[s - 1, r].astype(jnp.float32)
            if s < 3:
                ring_out[s, r] = running.astype(jnp.bfloat16)
                ring_copy(s, r).start()
            else:
                result[:, pl.ds(pl.multiple_of(r * width, width), width)] = running
            return carry

        for r in (0, 2, 1, 3):
            step(r, 0)

    finish_rows(0, 2)
    other_copy(0).wait_recv()
    partials(0, 0, 2)
    other_copy(1).wait_recv()
    partials(0, 2, 4)
    forward(0)
    finish_rows(2, 3)
    other_copy(2).wait_recv()
    partials(1, 0, 4)
    forward(1)
    finish_rows(3, 4)
    partials(2, 0, 4)
    forward(2)
    other_copy(3).wait_recv()
    partials(3, 0, 4)
    forward(3)
    for j in range(4):
        other_copy(j).wait_send()

    def drain(r, carry):
        for s in range(4):
            pair_copy(s, r).wait_send()
        for s in range(3):
            ring_copy(s, r).wait_send()
        return carry

    lax.fori_loop(0, RINGS, drain, 0)
    projected = result[...]
    scale = lax.rsqrt(jnp.mean(projected * projected, axis=-1, keepdims=True) + EPSILON)
    out_ref[...] = (
        hid_ref[...].astype(jnp.float32) + projected * scale * gain_ref[...]
    ).astype(jnp.bfloat16)


def project(
    heads, cache_keys, cache_values, meta, sizes, selected, ids_col, ids_row, w_own, w_across, own_rows,
    post_gain,
):
    rows, features = own_rows.shape
    width = features // RINGS
    new_rows = heads.shape[1]
    groups, stretch = sizes[2], cache_keys.shape[1]
    total_keys = groups * stretch + new_rows
    angles = (np.arange(groups, dtype=np.float32) * stretch)[:, None] * frequencies()[None, :]
    cosine, sine = np.cos(angles), np.sin(angles)
    vmem = pl.BlockSpec(memory_space=pltpu.VMEM)
    smem = pl.BlockSpec(memory_space=pltpu.SMEM)
    dma = pltpu.SemaphoreType.DMA
    return pl.pallas_call(
        functools.partial(project_kernel, selected, sizes),
        out_shape=jax.ShapeDtypeStruct((rows, features), jnp.bfloat16),
        in_specs=[smem] + [vmem] * 11,
        out_specs=vmem,
        scratch_shapes=[
            pltpu.VMEM((groups, stretch, 2 * HEAD), jnp.bfloat16),
            pltpu.VMEM((groups - 1, stretch, 2 * HEAD), jnp.bfloat16),
            pltpu.VMEM((new_rows, 2 * HEAD), jnp.bfloat16),
            pltpu.VMEM((total_keys, HEAD), jnp.bfloat16),
            pltpu.VMEM((total_keys, 2 * HEAD), jnp.bfloat16),
            pltpu.VMEM((groups * stretch // (2 * BLOCK), 1, 2 * BLOCK), jnp.int32),
            pltpu.VMEM((new_rows // BLOCK, 1, BLOCK), jnp.int32),
            pltpu.VMEM((new_rows, 1), jnp.int32),
            pltpu.VMEM((new_rows, 1), jnp.int32),
            pltpu.VMEM((2 * BLOCK, HEAD), jnp.bfloat16),
            pltpu.VMEM((new_rows // BLOCK, 2 * BLOCK, 2 * HEAD), jnp.float32),
            pltpu.VMEM((4, 2 * rows, 2 * HEAD), jnp.bfloat16),
            pltpu.VMEM((2 * rows, width), jnp.float32),
            pltpu.VMEM((4, RINGS, rows, width), jnp.float32),
            pltpu.VMEM((4, RINGS, rows, width), jnp.bfloat16),
            pltpu.VMEM((4, RINGS, rows, width), jnp.bfloat16),
            pltpu.VMEM((3, RINGS, rows, width), jnp.bfloat16),
            pltpu.VMEM((3, RINGS, rows, width), jnp.bfloat16),
            pltpu.VMEM((rows, features), jnp.float32),
            dma((4,)), dma((4,)), dma((4, RINGS)), dma((4, RINGS)), dma((3, RINGS)), dma((3, RINGS)),
            dma((7,)), dma((7,)),
        ],
        compiler_params=pltpu.CompilerParams(
            collective_id=1, has_side_effects=True, vmem_limit_bytes=60 << 20
        ),
        name="project",
    )(
        meta, heads, cache_keys, cache_values,
        np.concatenate([cosine, cosine], axis=1), np.concatenate([-sine, sine], axis=1),
        ids_col, ids_row, w_own, w_across, own_rows, post_gain[None, :],
    )


def project_in_kernel(
    selected, sizes, stretch, meta_ref, hid_ref, gain_ref, freq_ref, ids_ref,
    wq_hbm, wk_hbm, wv_hbm, wo_ref, heads_ref, wo_across_ref,
    normed, weights, ship, wq_ref, wk_ref, wv_ref, cos_ref, sin_ref,
    l_sem, x_send, x_recv, f_send, f_recv, s_send, s_recv, y_send, y_recv, w_send, w_recv, z_send, z_recv,
    g_send, g_recv, o_send, o_recv, e_send, e_recv,
):
    group, half, spot, core = place()
    rows, features = hid_ref.shape
    depth = group % AROUND
    lows = group // AROUND
    quarter = features // 8

    def around(value):
        return lax.rem(value + 2 * AROUND, AROUND)

    xs = [device(group, half, spot + 1, core), device(group, half, spot - 1, core)]
    zs = [
        device(lows * AROUND + around(depth + 1), half, spot, core),
        device(lows * AROUND + around(depth - 1), half, spot, core),
    ]
    near = device((1 - lows) * AROUND + depth, 1 - half, spot, core)
    across = device(group, 1 - half, spot, core)
    beside = device((1 - lows) * AROUND + depth, half, spot, core)
    sibling = device(group, half, spot, 1 - core)
    local = [
        pltpu.make_async_copy(src, dst, l_sem.at[i])
        for i, (src, dst) in enumerate(
            [(wq_hbm, wq_ref), (wk_hbm, wk_ref), (wv_hbm, wv_ref)]
        )
    ]
    for each in local:
        each.start()
    greet(xs + zs + [near, across, beside, sibling])
    owners_ref, counts_ref, _ = views(meta_ref, sizes)

    def copy(src, dst, send, recv, to):
        return pltpu.make_async_remote_copy(
            src_ref=src, dst_ref=dst, send_sem=send, recv_sem=recv, device_id=to, device_id_type=MESH
        )

    mine = pl.multiple_of(core * rows, rows)
    twin = pl.multiple_of((1 - core) * rows, rows)

    def block(owner, start=0, size=rows, base=mine):
        return normed.at[owner, pl.ds(pl.multiple_of(base + start, size), size)]

    def x_copy(d, owner=spot):
        return copy(block(owner), block(owner), x_send.at[d], x_recv.at[d], xs[d])

    def f_copy(d, owner):
        piece = block(owner, d * (rows // 2), rows // 2)
        return copy(piece, piece, f_send.at[d], f_recv.at[d], xs[d])

    def s_copy(i, owner, base=mine):
        piece = block(owner, base=base)
        return copy(piece, piece, s_send.at[i], s_recv.at[i], sibling)

    mine_first, theirs_first = 4 * lows, 4 * (1 - lows)

    def slab(q, p):
        return weights.at[q, pl.ds(pl.multiple_of(p * quarter, quarter), quarter)]

    def y_start(j):
        piece = (theirs_first if j < 4 else mine_first) + j % 4
        part = pl.ds(pl.multiple_of(piece * quarter, quarter), quarter)
        sources = [
            wq_hbm.at[part, pl.ds(0, HEAD)], wq_hbm.at[part, pl.ds(HEAD, HEAD)],
            wk_hbm.at[part], wv_hbm.at[part],
        ]
        for z, src in enumerate(sources):
            @pl.when(depth == z)
            def _(src=src):
                copy(src, slab(depth, piece), y_send.at[j], y_recv.at[j], near).start()

    def y_done(j):
        piece = slab(depth, nth_piece(j))
        return copy(piece, piece, y_send.at[j], y_recv.at[j], near)

    def w_copy(i, q, p):
        return copy(slab(q, p), slab(q, p), w_send.at[i], w_recv.at[i], beside)

    def nth_piece(n):
        return (mine_first if n < 4 else theirs_first) + n % 4

    def z_copy(d, n, q=depth):
        piece = slab(q, nth_piece(n))
        return copy(piece, piece, z_send.at[d, n], z_recv.at[d, n], zs[d])

    def g_copy(d, j, q):
        piece = slab(q, mine_first + 2 * d + j)
        return copy(piece, piece, g_send.at[d, j], g_recv.at[d, j], zs[d])

    def o_copy(i, src, q, part, to):
        size = wo_ref.shape[0] // (4 if part is None else 8)
        start = q * (wo_ref.shape[0] // 4) + (part or 0) * size
        piece = pl.ds(pl.multiple_of(start, size), size)
        return copy(src.at[piece], wo_across_ref.at[piece], o_send.at[i], o_recv.at[i], to)

    def make_tables():
        layout = Layout(owners_ref, counts_ref, stretch)
        below = lax.broadcasted_iota(jnp.int32, (stretch, 1), 0)
        for i in range(cos_ref.shape[0] // stretch):
            row = below + (half * cos_ref.shape[0] + i * stretch)
            code = layout.of_queries(row - selected)
            if i == 0:
                code = jnp.where(row < selected, layout.of_cached(ids_ref[...]), code)
            angle = (code - request_base(code)).astype(jnp.float32) * freq_ref[...]
            sine = jnp.sin(angle)
            lane = lax.broadcasted_iota(jnp.int32, sine.shape, 1)
            cos_ref[pl.ds(i * stretch, stretch), :] = jnp.cos(angle)
            sin_ref[pl.ds(i * stretch, stretch), :] = jnp.where(lane < HEAD // 2, -sine, sine)

    def table(ref, owner):
        return ref[pl.ds(pl.multiple_of(owner * 2 * rows, 2 * rows), 2 * rows), :]

    def own_heads(owner):
        source = normed[owner]
        cosine, sine = table(cos_ref, owner), table(sin_ref, owner)
        to = pl.ds(pl.multiple_of((half * AROUND + owner) * 2 * rows, 2 * rows), 2 * rows)
        q = jnp.dot(source, wq_ref[...], preferred_element_type=jnp.float32)
        heads_ref[0, to] = turned(q[:, :HEAD], cosine, sine).astype(jnp.bfloat16)
        heads_ref[1, to] = turned(q[:, HEAD:], cosine, sine).astype(jnp.bfloat16)
        k = jnp.dot(source, wk_ref[...], preferred_element_type=jnp.float32)
        heads_ref[2, to] = turned(k, cosine, sine).astype(jnp.bfloat16)
        v = jnp.dot(source, wv_ref[...], preferred_element_type=jnp.float32)
        heads_ref[3, to] = v.astype(jnp.bfloat16)

    def e_copy(i, b, owner, q):
        to = pl.ds(pl.multiple_of((half * AROUND + owner) * 2 * rows, 2 * rows), 2 * rows)
        return copy(ship.at[i, b], heads_ref.at[q, to], e_send.at[i, b], e_recv.at[i, b], across)

    def nth(base, i):
        return around(base + (i * (7 - i)) // 2)

    owners = [nth(spot, b) for b in range(4)]
    quarters = [nth(depth, i) for i in range(4)]

    def their_heads(i, b):
        owner, q = nth(spot, b), nth(depth, i)
        u = jnp.dot(normed[owner], weights[q], preferred_element_type=jnp.float32)
        plain = (q == 3).astype(jnp.float32)
        cosine, sine = table(cos_ref, owner), table(sin_ref, owner)
        cosine = cosine + plain * (1.0 - cosine)
        sine = sine * (1.0 - plain)
        ship[i, b] = turned(u, cosine, sine).astype(jnp.bfloat16)
        e_copy(i, b, owner, q).start()

    def own_blocks(first, last):
        def step(b, carry):
            own_heads(nth(spot, b))
            return carry

        lax.fori_loop(first, last, step, 0)

    def their_blocks(i0, i1, b0, b1):
        def step(n, carry):
            their_heads(i0 + n // (b1 - b0), b0 + lax.rem(n, b1 - b0))
            return carry

        lax.fori_loop(0, (i1 - i0) * (b1 - b0), step, 0)

    left, right, far = owners[1], owners[2], owners[3]
    below, above, beyond = quarters[1], quarters[2], quarters[3]
    def pass_on(n):
        y_done(n).wait_recv()
        z_copy(0, n).start()
        z_copy(1, n).start()
        if n + 2 < 8:
            y_start(n + 2)

    y_start(0)
    y_start(1)
    wide = hid_ref[...].astype(jnp.float32)
    scale = lax.rsqrt(jnp.mean(wide * wide, axis=-1, keepdims=True) + EPSILON)
    normed[spot, pl.ds(mine, rows)] = (wide * scale * gain_ref[...]).astype(jnp.bfloat16)
    x_copy(0).start()
    x_copy(1).start()
    s_copy(0, spot).start()
    pass_on(0)
    pass_on(1)
    make_tables()
    pass_on(2)
    pass_on(3)
    for each in local:
        each.wait()
    s_copy(0, spot, twin).wait_recv()
    own_blocks(0, 1)
    pass_on(4)
    for j in range(2):
        z_copy(0, j, below).wait_recv()
        g_copy(0, j, below).start()
    pass_on(5)
    for j in range(2):
        z_copy(1, 2 + j, above).wait_recv()
        g_copy(1, j, above).start()
    pass_on(6)
    pass_on(7)
    o_copy(0, wo_ref, depth, None, near).start()
    x_copy(0, left).wait_recv()
    f_copy(0, left).start()
    s_copy(1, left).start()
    x_copy(1, right).wait_recv()
    f_copy(1, right).start()
    s_copy(2, right).start()
    their_blocks(0, 1, 0, 1)
    s_copy(1, left, twin).wait_recv()
    s_copy(2, right, twin).wait_recv()
    their_blocks(0, 1, 1, 3)
    for d in range(2):
        for j in range(2):
            g_copy(d, j, beyond).wait_recv()
            w_copy(2 * d + j, beyond, mine_first + 2 * d + j).start()
    o_copy(0, wo_ref, depth, None, near).wait_recv()
    o_copy(1, wo_across_ref, depth, None, zs[0]).start()
    o_copy(2, wo_across_ref, depth, None, zs[1]).start()
    for n in range(2, 8):
        z_copy(0, n, below).wait_recv()
    for n in (0, 1, 4, 5, 6, 7):
        z_copy(1, n, above).wait_recv()
    f_copy(0, far).wait_recv()
    f_copy(1, far).wait_recv()
    s_copy(3, far).start()
    their_blocks(1, 3, 0, 3)
    s_copy(3, far, twin).wait_recv()
    their_blocks(0, 3, 3, 4)
    for n in range(4):
        w_copy(n, beyond, theirs_first + n).wait_recv()
    their_blocks(3, 4, 0, 4)
    own_blocks(1, 2)
    o_copy(1, wo_across_ref, below, None, zs[0]).wait_recv()
    o_copy(3, wo_across_ref, below, 0, zs[0]).start()
    o_copy(2, wo_across_ref, above, None, zs[1]).wait_recv()
    o_copy(4, wo_across_ref, above, 1, zs[1]).start()
    own_blocks(2, 4)
    o_copy(3, wo_across_ref, beyond, 0, zs[0]).wait_recv()
    o_copy(4, wo_across_ref, beyond, 1, zs[1]).wait_recv()
    for i in range(4):
        for b in range(4):
            to = pl.ds(
                pl.multiple_of(((1 - half) * AROUND + owners[b]) * 2 * rows, 2 * rows), 2 * rows
            )
            copy(
                ship.at[i, b], heads_ref.at[quarters[i], to], e_send.at[i, b], e_recv.at[i, b], across
            ).wait()
    for d in range(2):
        x_copy(d).wait_send()
        f_copy(d, owners[1 + d]).wait_send()
        for n in range(8):
            z_copy(d, n).wait_send()
        for j in range(2):
            g_copy(d, j, quarters[1 + d]).wait_send()
    for i in range(4):
        s_copy(i, owners[i]).wait_send()
    for n in range(4):
        w_copy(n, beyond, mine_first + n).wait_send()
    for n in range(8):
        y_done(n).wait_send()
    o_copy(0, wo_ref, depth, None, near).wait_send()
    o_copy(1, wo_across_ref, depth, None, zs[0]).wait_send()
    o_copy(2, wo_across_ref, depth, None, zs[1]).wait_send()
    o_copy(3, wo_across_ref, below, 0, zs[0]).wait_send()
    o_copy(4, wo_across_ref, above, 1, zs[1]).wait_send()


def project_in(
    own_rows, gain, w_query, w_key, w_value, w_out, meta, sizes, stretch, selected, ids_col, new_rows,
):
    rows, features = own_rows.shape
    vmem = pl.BlockSpec(memory_space=pltpu.VMEM)
    smem = pl.BlockSpec(memory_space=pltpu.SMEM)
    hbm = pl.BlockSpec(memory_space=pltpu.HBM)
    dma = pltpu.SemaphoreType.DMA
    pairs = [(2,), (2,), (4,), (8,), (4,), (2, 8), (2, 2), (5,), (4, 4)]
    bf16 = jnp.bfloat16
    return pl.pallas_call(
        functools.partial(project_in_kernel, selected, sizes, stretch),
        out_shape=(
            jax.ShapeDtypeStruct((4, new_rows, HEAD), bf16), jax.ShapeDtypeStruct(w_out.shape, bf16)
        ),
        in_specs=[smem] + [vmem] * 4 + [hbm] * 4,
        out_specs=(vmem, hbm),
        scratch_shapes=[
            pltpu.VMEM((AROUND, 2 * rows, features), bf16),
            pltpu.VMEM((4, features, HEAD), bf16),
            pltpu.VMEM((4, 4, 2 * rows, HEAD), bf16),
            pltpu.VMEM(w_query.shape, bf16), pltpu.VMEM(w_key.shape, bf16),
            pltpu.VMEM(w_value.shape, bf16),
            pltpu.VMEM((new_rows // 2, HEAD), jnp.float32),
            pltpu.VMEM((new_rows // 2, HEAD), jnp.float32),
            dma((3,)),
        ] + [dma(shape) for shape in pairs for _ in range(2)],
        compiler_params=pltpu.CompilerParams(
            collective_id=2, has_side_effects=True, vmem_limit_bytes=52 << 20
        ),
        name="project_in",
    )(
        meta, own_rows, gain[None, :], np.concatenate([frequencies()] * 2)[None, :], ids_col,
        w_query, w_key, w_value, w_out,
    )


def on_device(
    hidden, input_gain, w_query, w_key, w_value, w_out, post_gain, cache_keys, cache_values,
    page_table, stretch_request, recompute_ids, query_counts,
):
    own_rows = hidden[0]
    new_rows = own_rows.shape[0] * lax.axis_size("tok")
    stretch = cache_keys.shape[1]
    owners, counts, ids = stretch_request[0], query_counts[0], recompute_ids[0]
    selected = ids.shape[0]
    padded = jnp.pad(ids, (0, stretch - selected), constant_values=-1)
    ids_col, ids_row = padded[:, None], padded[None, :]
    sizes = (owners.shape[0], counts.shape[0], page_table.shape[0])
    meta = jnp.concatenate([owners, counts, page_table.reshape(-1)])
    heads, w_across = project_in(
        own_rows, input_gain, w_query, w_key, w_value, w_out, meta, sizes, stretch, selected, ids_col,
        new_rows,
    )
    output = project(
        heads, cache_keys, cache_values, meta, sizes, selected, ids_col, ids_row, w_out, w_across, own_rows,
        post_gain,
    )
    return output[None]


def solution(mesh):
    return jax.shard_map(
        on_device,
        mesh=mesh,
        in_specs=(
            P("grp", "tok", None), P(), P(None, "tok"), P(None, "tok"), P(None, "tok"),
            P("tok", None), P(), P("grp", None, "tok"), P("grp", None, "tok"), P(),
            P("grp", None), P("grp", None), P("grp", None),
        ),
        out_specs=P("grp", "tok", None),
        check_vma=False,
    )
```

```python
import functools
import math

import jax
import jax.numpy as jnp
import numpy as np
from jax import lax
from jax.experimental import pallas as pl
from jax.experimental.pallas import tpu as pltpu
from jax.sharding import PartitionSpec as P

HEAD = 128
EPSILON = 1e-06
CAP_VALUE = 50.0
QUERY_SCALE = 1.0 / 12.0
ROPE_BASE = 10000.0
SPAN = 1 << 16
FAR = 1 << 30
BLOCK = 512


def frequencies():
    ladder = np.arange(HEAD // 2, dtype=np.float32)
    return np.exp(ladder * np.float32(-2.0 * math.log(ROPE_BASE) / HEAD)).astype(np.float32)


def turned(u, cosine, sine):
    return u * cosine + pltpu.roll(u, HEAD // 2, 1) * sine


def request_base(code):
    return jnp.where(code >= 2 * SPAN, 2 * SPAN, jnp.where(code >= SPAN, SPAN, 0))


class View:
    def __init__(self, ref, base, shape):
        self.ref, self.base, self.shape = ref, base, shape

    def __getitem__(self, index):
        if isinstance(index, tuple):
            index = index[0] * self.shape[1] + index[1]
        return self.ref[self.base + index]


def views(meta_ref, sizes):
    slots, requests, groups = sizes
    return (
        View(meta_ref, 0, (slots,)), View(meta_ref, slots, (requests,)),
        View(meta_ref, slots + requests, (groups, slots)),
    )


class Layout:
    def __init__(self, owners, counts, stretch):
        slots = owners.shape[0]
        self.stretch = stretch
        self.owners = [owners[c] for c in range(slots)]
        held = [sum((o == r).astype(jnp.int32) for o in self.owners) for r in range(3)]
        first = [0, held[0], held[0] + held[1]]
        self.offsets = []
        self.slot_bases = []
        for c, o in enumerate(self.owners):
            start = jnp.where(o == 0, first[0], jnp.where(o == 1, first[1], first[2]))
            self.offsets.append(c - start)
            self.slot_bases.append(o * SPAN - start * stretch)
        self.starts = [0, counts[0], counts[0] + counts[1]]
        self.query_bases = [r * SPAN + held[r] * stretch - self.starts[r] for r in range(3)]

    def of_queries(self, m):
        base = jnp.where(
            m >= self.starts[2], self.query_bases[2],
            jnp.where(m >= self.starts[1], self.query_bases[1], self.query_bases[0]),
        )
        return m + base

    def of_cached(self, ids):
        base = self.slot_bases[0]
        for c in range(1, len(self.slot_bases)):
            base = jnp.where(ids >= c * self.stretch, self.slot_bases[c], base)
        return ids + base

    def request_of(self, m):
        return (m >= self.starts[1]).astype(jnp.int32) + (m >= self.starts[2]).astype(jnp.int32)


MESH = pl.DeviceIdType.MESH
RINGS = 4
AROUND = 4


def place():
    tok = lax.axis_index("tok")
    return lax.axis_index("grp"), tok // 8, (tok // 2) % AROUND, tok % 2


def device(group, half, spot, core):
    return (group, half * 8 + lax.rem(spot + 2 * AROUND, AROUND) * 2 + core)


def greet(partners):
    barrier = pltpu.get_barrier_semaphore()
    for partner in partners:
        pl.semaphore_signal(barrier, inc=1, device_id=partner, device_id_type=MESH)
    pl.semaphore_wait(barrier, len(partners))


def make_attention(
    selected, layout, table_ref, heads_ref, pages_ref, pcos_ref, psin_ref,
    ids_col_ref, ids_row_ref, attended, keys, values, cached_codes, key_codes, row_codes, row_bases, queries, totals,
):
    rows = heads_ref.shape[1]
    groups, stretch = pages_ref.shape[:2]
    cached = groups * stretch
    group = lax.axis_index("grp")
    lane = lax.broadcasted_iota(jnp.int32, (1, stretch), 1)
    below = lax.broadcasted_iota(jnp.int32, (stretch, 1), 0)
    ids_col = ids_col_ref[...]
    wide = cached_codes.shape[2]

    def put_codes(codes_ref, i, codes):
        per = codes_ref.shape[2] // stretch
        codes_ref[i // per, :, pl.ds((i % per) * stretch, stretch)] = codes

    def lay_cached():
        for c in range(groups):
            page = table_ref[group, c]
            source = page // (table_ref.shape[1])
            part = pl.ds(c * stretch, stretch)
            turn = layout.offsets[c]
            k = pages_ref[source, :, :HEAD].astype(jnp.float32)
            k = turned(k, pcos_ref[pl.ds(turn, 1), :], psin_ref[pl.ds(turn, 1), :])
            keys[part, :] = k.astype(jnp.bfloat16)
            values[part, :HEAD] = pages_ref[source, :, HEAD:]
            ids = lane + c * stretch
            dead = jnp.max((ids_col == ids).astype(jnp.int32), axis=0, keepdims=True)
            put_codes(cached_codes, c, jnp.where(dead > 0, FAR, ids + layout.slot_bases[c]))

    def lay_new():
        keys[pl.ds(cached, rows), :] = heads_ref[2]
        values[pl.ds(cached, rows), :HEAD] = heads_ref[3]
        values[:, HEAD:] = jnp.ones((cached + rows, HEAD), jnp.bfloat16)
        for i in range(rows // stretch):
            by_lane = layout.of_queries(lane + (i * stretch - selected))
            by_row = layout.of_queries(below + (i * stretch - selected))
            if i == 0:
                by_lane = jnp.where(lane < selected, layout.of_cached(ids_row_ref[...]), by_lane)
                by_row = jnp.where(below < selected, layout.of_cached(ids_col), by_row)
            put_codes(key_codes, i, by_lane)
            row_codes[pl.ds(i * stretch, stretch), :] = by_row
            row_bases[pl.ds(i * stretch, stretch), :] = request_base(by_row)

    def weigh(asked, there, key_code, code, base):
        scores = lax.dot_general(
            asked, keys[there, :], (((1,), (1,)), ((), ())), preferred_element_type=jnp.float32
        )
        capped = jnp.tanh(scores * (QUERY_SCALE / CAP_VALUE))
        weights = jnp.exp2(capped * (CAP_VALUE * math.log2(math.e)))
        seen = (key_code <= code) & (key_code >= base)
        both = jnp.concatenate([seen, seen], axis=0)
        rounded = jnp.where(both, weights, 0.0).astype(jnp.bfloat16)
        return jnp.dot(rounded, values[there, :], preferred_element_type=jnp.float32)

    def see_new(rb):
        here = pl.ds(pl.multiple_of(rb * BLOCK, BLOCK), BLOCK)
        queries[:BLOCK, :] = heads_ref[0, here, :]
        queries[BLOCK:, :] = heads_ref[1, here, :]
        code, base = row_codes[here, :], row_bases[here, :]
        totals[rb] = jnp.zeros(totals.shape[1:], jnp.float32)

        def key_block(kb, carry):
            there = pl.ds(pl.multiple_of(cached + kb * BLOCK, BLOCK), BLOCK)
            totals[rb] += weigh(queries[...], there, key_codes[kb], code, base)
            return carry

        lax.fori_loop(0, rb + 1, key_block, 0)

    def see_cached(qb):
        few = BLOCK // 2
        here = pl.ds(pl.multiple_of(qb * few, few), few)
        queries[:few, :] = heads_ref[0, here, :]
        queries[few:BLOCK, :] = heads_ref[1, here, :]
        code, base = row_codes[here, :], row_bases[here, :]
        rb = qb // 2
        low = pl.ds(pl.multiple_of(lax.rem(qb, 2) * few, few), few)
        high = pl.ds(pl.multiple_of(BLOCK + lax.rem(qb, 2) * few, few), few)

        def key_block(kb, carry):
            there = pl.ds(pl.multiple_of(kb * wide, wide), wide)
            more = weigh(queries[:BLOCK, :], there, cached_codes[kb], code, base)
            totals[rb, low, :] += more[:few]
            totals[rb, high, :] += more[few:]
            return carry

        lax.fori_loop(0, cached // wide, key_block, 0)
        for head, part in enumerate((low, high)):
            quotient = totals[rb, part, :HEAD] / totals[rb, part, HEAD:]
            attended[here, head * HEAD : (head + 1) * HEAD] = quotient.astype(jnp.bfloat16)

    return lay_new, lay_cached, see_new, see_cached


def project_kernel(
    selected, sizes, meta_ref, heads_ref, ck_ref, cv_ref, pcos_ref, psin_ref,
    ids_col_ref, ids_row_ref, w0_ref, w1_ref, hid_ref, gain_ref, out_ref,
    pages_ref, outgoing, attn_ref, keys, values, cached_codes, key_codes, row_codes, row_bases,
    queries, totals, other, product, own, pair_out, pair_in, ring_out, ring_in, result,
    other_send, other_recv, pair_send, pair_recv, ring_send, ring_recv, p_send, p_recv,
):
    group, half, spot, core = place()
    rows = hid_ref.shape[0]
    width = hid_ref.shape[1] // RINGS
    chunk = 2 * rows
    across = device(group, 1 - half, spot, core)
    sibling = device(group, half, spot, 1 - core)
    lows, depth = group // AROUND, group % AROUND
    zs = [
        device(lows * AROUND + lax.rem(depth + 1, AROUND), half, spot, core),
        device(lows * AROUND + lax.rem(depth + AROUND - 1, AROUND), half, spot, core),
    ]
    beside = device((1 - lows) * AROUND + depth, half, spot, core)
    offsets = [(0, 1), (0, -1), (1, 0), (0, 2), (1, 1), (1, -1), (1, 2)]

    def group_at(low, deep):
        return lax.rem(lows + low, 2) * AROUND + lax.rem(depth + deep + AROUND, AROUND)

    greet(
        [across, sibling, device(group, half, spot + 1, core), device(group, half, spot - 1, core)]
        + zs + [beside] + [device(group_at(*o), half, spot, core) for o in offsets[3:]]
    )
    owners_ref, counts_ref, table_ref = views(meta_ref, sizes)
    pages, stretch = ck_ref.shape[:2]

    def picked(target):
        index = 0
        for c in range(table_ref.shape[1]):
            page = table_ref[target, c]
            index = index + jnp.where(page // pages == group, page % pages, 0)
        return index

    def p_copy(j, source):
        return pltpu.make_async_remote_copy(
            src_ref=outgoing.at[j], dst_ref=pages_ref.at[source], send_sem=p_send.at[j],
            recv_sem=p_recv.at[j], device_id=device(group_at(*offsets[j]), half, spot, core),
            device_id_type=MESH,
        )

    for j, offset in enumerate(offsets):
        index = picked(group_at(*offset))
        outgoing[j, :, :HEAD] = ck_ref[index]
        outgoing[j, :, HEAD:] = cv_ref[index]
        p_copy(j, group).start()
    index = picked(group)
    pages_ref[group, :, :HEAD] = ck_ref[index]
    pages_ref[group, :, HEAD:] = cv_ref[index]
    lay_new, lay_cached, see_new, see_cached = make_attention(
        selected, Layout(owners_ref, counts_ref, stretch), table_ref, heads_ref, pages_ref,
        pcos_ref, psin_ref, ids_col_ref, ids_row_ref, attn_ref, keys, values, cached_codes, key_codes,
        row_codes, row_bases, queries, totals,
    )

    def other_copy(j):
        owner = lax.rem(spot + 3 - 2 * j + 3 * (j // 2) + AROUND, AROUND)
        start = pl.multiple_of(((1 - half) * AROUND + owner) * chunk, chunk)
        return pltpu.make_async_remote_copy(
            src_ref=attn_ref.at[pl.ds(start, chunk)], dst_ref=other.at[j],
            send_sem=other_send.at[j], recv_sem=other_recv.at[j],
            device_id=across, device_id_type=MESH,
        )

    def pair_copy(s, r):
        return pltpu.make_async_remote_copy(
            src_ref=pair_out.at[s, r], dst_ref=pair_in.at[s, r],
            send_sem=pair_send.at[s, r], recv_sem=pair_recv.at[s, r],
            device_id=sibling, device_id_type=MESH,
        )

    def ring_copy(s, r):
        return pltpu.make_async_remote_copy(
            src_ref=ring_out.at[s, r], dst_ref=ring_in.at[s, r],
            send_sem=ring_send.at[s, r], recv_sem=ring_recv.at[s, r],
            device_id=device(group, half, spot + 1 - 2 * (r // 2), core), device_id_type=MESH,
        )

    per_half = attn_ref.shape[0] // BLOCK // 2

    def blocks_of(one_half, see):
        def step(i, carry):
            see(one_half * per_half + i)
            return carry

        lax.fori_loop(0, per_half, step, 0)

    lay_new()
    blocks_of(half, see_new)
    blocks_of(1 - half, see_new)
    for j, (low, deep) in enumerate(offsets):
        p_copy(j, group_at(low, -deep)).wait()
    lay_cached()

    def finish_rows(first, last):
        count = last - first

        def step(n, carry):
            theirs = n < count
            j = first + lax.rem(n, count)
            owner = lax.rem(spot + 3 - 2 * j + 3 * (j // 2) + AROUND, AROUND)
            see_cached(jnp.where(theirs, 1 - half, half) * AROUND + owner)

            @pl.when(theirs)
            def _():
                other_copy(j).start()

            return carry

        lax.fori_loop(0, 2 * count, step, 0)

    def partial(s, r):
        owner = lax.rem(spot + (2 * (r // 2) - 1) * (1 + s) + 2 * AROUND, AROUND)
        slot = (r // 2, 2, 1 - r // 2, 3)[s]
        start = pl.multiple_of((half * AROUND + owner) * chunk, chunk)
        columns = pl.ds(pl.multiple_of(r * width, width), width)
        product[...] = jnp.dot(
            attn_ref[pl.ds(start, chunk), :], w0_ref[:, columns], preferred_element_type=jnp.float32
        ) + jnp.dot(other[slot], w1_ref[:, columns], preferred_element_type=jnp.float32)
        theirs = pl.ds(pl.multiple_of((1 - core) * rows, rows), rows)
        pair_out[s, r] = product[theirs, :].astype(jnp.bfloat16)
        pair_copy(s, r).start()
        own[s, r] = product[pl.ds(pl.multiple_of(core * rows, rows), rows), :]

    def partials(s, first, last):
        def step(r, carry):
            partial(s, r)
            return carry

        lax.fori_loop(first, last, step, 0)

    def forward(s):
        def step(r, carry):
            pair_copy(s, r).wait_recv()
            running = own[s, r] + pair_in[s, r].astype(jnp.float32)
            if s > 0:
                ring_copy(s - 1, r).wait_recv()
                running = running + ring_in[s - 1, r].astype(jnp.float32)
            if s < 3:
                ring_out[s, r] = running.astype(jnp.bfloat16)
                ring_copy(s, r).start()
            else:
                result[:, pl.ds(pl.multiple_of(r * width, width), width)] = running
            return carry

        for r in (0, 2, 1, 3):
            step(r, 0)

    finish_rows(0, 2)
    other_copy(0).wait_recv()
    partials(0, 0, 2)
    other_copy(1).wait_recv()
    partials(0, 2, 4)
    forward(0)
    finish_rows(2, 3)
    other_copy(2).wait_recv()
    partials(1, 0, 4)
    forward(1)
    finish_rows(3, 4)
    partials(2, 0, 4)
    forward(2)
    other_copy(3).wait_recv()
    partials(3, 0, 4)
    forward(3)
    for j in range(4):
        other_copy(j).wait_send()

    def drain(r, carry):
        for s in range(4):
            pair_copy(s, r).wait_send()
        for s in range(3):
            ring_copy(s, r).wait_send()
        return carry

    lax.fori_loop(0, RINGS, drain, 0)
    projected = result[...]
    scale = lax.rsqrt(jnp.mean(projected * projected, axis=-1, keepdims=True) + EPSILON)
    out_ref[...] = (
        hid_ref[...].astype(jnp.float32) + projected * scale * gain_ref[...][None, :]
    ).astype(jnp.bfloat16)


def project(
    heads, cache_keys, cache_values, meta, sizes, selected, ids_col, ids_row, w_own, w_across, own_rows,
    post_gain,
):
    rows, features = own_rows.shape
    width = features // RINGS
    new_rows = heads.shape[1]
    groups, stretch = sizes[2], cache_keys.shape[1]
    total_keys = groups * stretch + new_rows
    angles = (np.arange(groups, dtype=np.float32) * stretch)[:, None] * frequencies()[None, :]
    cosine, sine = np.cos(angles), np.sin(angles)
    vmem = pl.BlockSpec(memory_space=pltpu.VMEM)
    smem = pl.BlockSpec(memory_space=pltpu.SMEM)
    dma = pltpu.SemaphoreType.DMA
    return pl.pallas_call(
        functools.partial(project_kernel, selected, sizes),
        out_shape=jax.ShapeDtypeStruct((rows, features), jnp.bfloat16),
        in_specs=[smem] + [vmem] * 11,
        out_specs=vmem,
        scratch_shapes=[
            pltpu.VMEM((groups, stretch, 2 * HEAD), jnp.bfloat16),
            pltpu.VMEM((groups - 1, stretch, 2 * HEAD), jnp.bfloat16),
            pltpu.VMEM((new_rows, 2 * HEAD), jnp.bfloat16),
            pltpu.VMEM((total_keys, HEAD), jnp.bfloat16),
            pltpu.VMEM((total_keys, 2 * HEAD), jnp.bfloat16),
            pltpu.VMEM((groups * stretch // (2 * BLOCK), 1, 2 * BLOCK), jnp.int32),
            pltpu.VMEM((new_rows // BLOCK, 1, BLOCK), jnp.int32),
            pltpu.VMEM((new_rows, 1), jnp.int32),
            pltpu.VMEM((new_rows, 1), jnp.int32),
            pltpu.VMEM((2 * BLOCK, HEAD), jnp.bfloat16),
            pltpu.VMEM((new_rows // BLOCK, 2 * BLOCK, 2 * HEAD), jnp.float32),
            pltpu.VMEM((4, 2 * rows, 2 * HEAD), jnp.bfloat16),
            pltpu.VMEM((2 * rows, width), jnp.float32),
            pltpu.VMEM((4, RINGS, rows, width), jnp.float32),
            pltpu.VMEM((4, RINGS, rows, width), jnp.bfloat16),
            pltpu.VMEM((4, RINGS, rows, width), jnp.bfloat16),
            pltpu.VMEM((3, RINGS, rows, width), jnp.bfloat16),
            pltpu.VMEM((3, RINGS, rows, width), jnp.bfloat16),
            pltpu.VMEM((rows, features), jnp.float32),
            dma((4,)), dma((4,)), dma((4, RINGS)), dma((4, RINGS)), dma((3, RINGS)), dma((3, RINGS)),
            dma((7,)), dma((7,)),
        ],
        compiler_params=pltpu.CompilerParams(
            collective_id=1, has_side_effects=True, vmem_limit_bytes=60 << 20
        ),
        name="project",
    )(
        meta, heads, cache_keys, cache_values,
        np.concatenate([cosine, cosine], axis=1), np.concatenate([-sine, sine], axis=1),
        ids_col, ids_row, w_own, w_across, own_rows, post_gain,
    )


def project_in_kernel(
    selected, sizes, stretch, meta_ref, hid_ref, gain_ref, ids_ref,
    wq_hbm, wk_hbm, wv_hbm, wo_ref, heads_ref, wo_across_ref,
    normed, weights, ship, wq_ref, wk_ref, wv_ref, cos_ref, sin_ref,
    l_sem, x_send, x_recv, f_send, f_recv, s_send, s_recv, y_send, y_recv, w_send, w_recv, z_send, z_recv,
    g_send, g_recv, o_send, o_recv, e_send, e_recv,
):
    group, half, spot, core = place()
    rows, features = hid_ref.shape
    depth = group % AROUND
    lows = group // AROUND
    quarter = features // 8

    def around(value):
        return lax.rem(value + 2 * AROUND, AROUND)

    xs = [device(group, half, spot + 1, core), device(group, half, spot - 1, core)]
    zs = [
        device(lows * AROUND + around(depth + 1), half, spot, core),
        device(lows * AROUND + around(depth - 1), half, spot, core),
    ]
    near = device((1 - lows) * AROUND + depth, 1 - half, spot, core)
    across = device(group, 1 - half, spot, core)
    beside = device((1 - lows) * AROUND + depth, half, spot, core)
    sibling = device(group, half, spot, 1 - core)
    local = [
        pltpu.make_async_copy(src, dst, l_sem.at[i])
        for i, (src, dst) in enumerate(
            [(wq_hbm, wq_ref), (wk_hbm, wk_ref), (wv_hbm, wv_ref)]
        )
    ]
    for each in local:
        each.start()
    greet(xs + zs + [near, across, beside, sibling])
    owners_ref, counts_ref, _ = views(meta_ref, sizes)

    def copy(src, dst, send, recv, to):
        return pltpu.make_async_remote_copy(
            src_ref=src, dst_ref=dst, send_sem=send, recv_sem=recv, device_id=to, device_id_type=MESH
        )

    mine = pl.multiple_of(core * rows, rows)
    twin = pl.multiple_of((1 - core) * rows, rows)

    def block(owner, start=0, size=rows, base=mine):
        return normed.at[owner, pl.ds(pl.multiple_of(base + start, size), size)]

    def x_copy(d, owner=spot):
        return copy(block(owner), block(owner), x_send.at[d], x_recv.at[d], xs[d])

    def f_copy(d, owner):
        piece = block(owner, d * (rows // 2), rows // 2)
        return copy(piece, piece, f_send.at[d], f_recv.at[d], xs[d])

    def s_copy(i, owner, base=mine):
        piece = block(owner, base=base)
        return copy(piece, piece, s_send.at[i], s_recv.at[i], sibling)

    mine_first, theirs_first = 4 * lows, 4 * (1 - lows)

    def slab(q, p):
        return weights.at[q, pl.ds(pl.multiple_of(p * quarter, quarter), quarter)]

    def y_start(j):
        piece = (theirs_first if j < 4 else mine_first) + j % 4
        part = pl.ds(pl.multiple_of(piece * quarter, quarter), quarter)
        sources = [
            wq_hbm.at[part, pl.ds(0, HEAD)], wq_hbm.at[part, pl.ds(HEAD, HEAD)],
            wk_hbm.at[part], wv_hbm.at[part],
        ]
        for z, src in enumerate(sources):
            @pl.when(depth == z)
            def _(src=src):
                copy(src, slab(depth, piece), y_send.at[j], y_recv.at[j], near).start()

    def y_done(j):
        piece = slab(depth, nth_piece(j))
        return copy(piece, piece, y_send.at[j], y_recv.at[j], near)

    def w_copy(i, q, p):
        return copy(slab(q, p), slab(q, p), w_send.at[i], w_recv.at[i], beside)

    def nth_piece(n):
        return (mine_first if n < 4 else theirs_first) + n % 4

    def z_copy(d, n, q=depth):
        piece = slab(q, nth_piece(n))
        return copy(piece, piece, z_send.at[d, n], z_recv.at[d, n], zs[d])

    def g_copy(d, j, q):
        piece = slab(q, mine_first + 2 * d + j)
        return copy(piece, piece, g_send.at[d, j], g_recv.at[d, j], zs[d])

    def o_copy(i, src, q, part, to):
        size = wo_ref.shape[0] // (4 if part is None else 8)
        start = q * (wo_ref.shape[0] // 4) + (part or 0) * size
        piece = pl.ds(pl.multiple_of(start, size), size)
        return copy(src.at[piece], wo_across_ref.at[piece], o_send.at[i], o_recv.at[i], to)

    def make_tables():
        layout = Layout(owners_ref, counts_ref, stretch)
        below = lax.broadcasted_iota(jnp.int32, (stretch, 1), 0)
        step = lax.broadcasted_iota(jnp.int32, (1, HEAD), 1)
        step = jnp.where(step < HEAD // 2, step, step - HEAD // 2).astype(jnp.float32)
        frequency = jnp.exp(step * (-2.0 * math.log(ROPE_BASE) / HEAD))
        for i in range(cos_ref.shape[0] // stretch):
            row = below + (half * cos_ref.shape[0] + i * stretch)
            code = layout.of_queries(row - selected)
            if i == 0:
                code = jnp.where(row < selected, layout.of_cached(ids_ref[...]), code)
            angle = (code - request_base(code)).astype(jnp.float32) * frequency
            sine = jnp.sin(angle)
            lane = lax.broadcasted_iota(jnp.int32, sine.shape, 1)
            cos_ref[pl.ds(i * stretch, stretch), :] = jnp.cos(angle)
            sin_ref[pl.ds(i * stretch, stretch), :] = jnp.where(lane < HEAD // 2, -sine, sine)

    def table(ref, owner):
        return ref[pl.ds(pl.multiple_of(owner * 2 * rows, 2 * rows), 2 * rows), :]

    def own_heads(owner):
        source = normed[owner]
        cosine, sine = table(cos_ref, owner), table(sin_ref, owner)
        to = pl.ds(pl.multiple_of((half * AROUND + owner) * 2 * rows, 2 * rows), 2 * rows)
        q = jnp.dot(source, wq_ref[...], preferred_element_type=jnp.float32)
        heads_ref[0, to] = turned(q[:, :HEAD], cosine, sine).astype(jnp.bfloat16)
        heads_ref[1, to] = turned(q[:, HEAD:], cosine, sine).astype(jnp.bfloat16)
        k = jnp.dot(source, wk_ref[...], preferred_element_type=jnp.float32)
        heads_ref[2, to] = turned(k, cosine, sine).astype(jnp.bfloat16)
        v = jnp.dot(source, wv_ref[...], preferred_element_type=jnp.float32)
        heads_ref[3, to] = v.astype(jnp.bfloat16)

    def e_copy(i, b, owner, q):
        to = pl.ds(pl.multiple_of((half * AROUND + owner) * 2 * rows, 2 * rows), 2 * rows)
        return copy(ship.at[i, b], heads_ref.at[q, to], e_send.at[i, b], e_recv.at[i, b], across)

    def nth(base, i):
        return around(base + (i * (7 - i)) // 2)

    owners = [nth(spot, b) for b in range(4)]
    quarters = [nth(depth, i) for i in range(4)]

    def their_heads(i, b):
        owner, q = nth(spot, b), nth(depth, i)
        u = jnp.dot(normed[owner], weights[q], preferred_element_type=jnp.float32)
        plain = (q == 3).astype(jnp.float32)
        cosine, sine = table(cos_ref, owner), table(sin_ref, owner)
        cosine = cosine + plain * (1.0 - cosine)
        sine = sine * (1.0 - plain)
        ship[i, b] = turned(u, cosine, sine).astype(jnp.bfloat16)
        e_copy(i, b, owner, q).start()

    def own_blocks(first, last):
        def step(b, carry):
            own_heads(nth(spot, b))
            return carry

        lax.fori_loop(first, last, step, 0)

    def their_blocks(i0, i1, b0, b1):
        def step(n, carry):
            their_heads(i0 + n // (b1 - b0), b0 + lax.rem(n, b1 - b0))
            return carry

        lax.fori_loop(0, (i1 - i0) * (b1 - b0), step, 0)

    left, right, far = owners[1], owners[2], owners[3]
    below, above, beyond = quarters[1], quarters[2], quarters[3]
    def pass_on(n):
        y_done(n).wait_recv()
        z_copy(0, n).start()
        z_copy(1, n).start()
        if n + 2 < 8:
            y_start(n + 2)

    y_start(0)
    y_start(1)
    wide = hid_ref[...].astype(jnp.float32)
    scale = lax.rsqrt(jnp.mean(wide * wide, axis=-1, keepdims=True) + EPSILON)
    normed[spot, pl.ds(mine, rows)] = (wide * scale * gain_ref[...][None, :]).astype(jnp.bfloat16)
    x_copy(0).start()
    x_copy(1).start()
    s_copy(0, spot).start()
    pass_on(0)
    pass_on(1)
    make_tables()
    pass_on(2)
    pass_on(3)
    for each in local:
        each.wait()
    s_copy(0, spot, twin).wait_recv()
    own_blocks(0, 1)
    pass_on(4)
    for j in range(2):
        z_copy(0, j, below).wait_recv()
        g_copy(0, j, below).start()
    pass_on(5)
    for j in range(2):
        z_copy(1, 2 + j, above).wait_recv()
        g_copy(1, j, above).start()
    pass_on(6)
    pass_on(7)
    o_copy(0, wo_ref, depth, None, near).start()
    x_copy(0, left).wait_recv()
    f_copy(0, left).start()
    s_copy(1, left).start()
    x_copy(1, right).wait_recv()
    f_copy(1, right).start()
    s_copy(2, right).start()
    their_blocks(0, 1, 0, 1)
    s_copy(1, left, twin).wait_recv()
    s_copy(2, right, twin).wait_recv()
    their_blocks(0, 1, 1, 3)
    own_blocks(1, 2)
    for d in range(2):
        for j in range(2):
            g_copy(d, j, beyond).wait_recv()
            w_copy(2 * d + j, beyond, mine_first + 2 * d + j).start()
    o_copy(0, wo_ref, depth, None, near).wait_recv()
    o_copy(1, wo_across_ref, depth, None, zs[0]).start()
    o_copy(2, wo_across_ref, depth, None, zs[1]).start()
    for n in range(2, 8):
        z_copy(0, n, below).wait_recv()
    for n in (0, 1, 4, 5, 6, 7):
        z_copy(1, n, above).wait_recv()
    f_copy(0, far).wait_recv()
    f_copy(1, far).wait_recv()
    s_copy(3, far).start()
    their_blocks(1, 3, 0, 3)
    s_copy(3, far, twin).wait_recv()
    their_blocks(0, 3, 3, 4)
    for n in range(4):
        w_copy(n, beyond, theirs_first + n).wait_recv()
    their_blocks(3, 4, 0, 4)
    o_copy(1, wo_across_ref, below, None, zs[0]).wait_recv()
    o_copy(3, wo_across_ref, below, 0, zs[0]).start()
    o_copy(2, wo_across_ref, above, None, zs[1]).wait_recv()
    o_copy(4, wo_across_ref, above, 1, zs[1]).start()
    own_blocks(2, 4)
    o_copy(3, wo_across_ref, beyond, 0, zs[0]).wait_recv()
    o_copy(4, wo_across_ref, beyond, 1, zs[1]).wait_recv()
    for i in range(4):
        for b in range(4):
            to = pl.ds(
                pl.multiple_of(((1 - half) * AROUND + owners[b]) * 2 * rows, 2 * rows), 2 * rows
            )
            copy(
                ship.at[i, b], heads_ref.at[quarters[i], to], e_send.at[i, b], e_recv.at[i, b], across
            ).wait()
    for d in range(2):
        x_copy(d).wait_send()
        f_copy(d, owners[1 + d]).wait_send()
        for n in range(8):
            z_copy(d, n).wait_send()
        for j in range(2):
            g_copy(d, j, quarters[1 + d]).wait_send()
    for i in range(4):
        s_copy(i, owners[i]).wait_send()
    for n in range(4):
        w_copy(n, beyond, mine_first + n).wait_send()
    for n in range(8):
        y_done(n).wait_send()
    o_copy(0, wo_ref, depth, None, near).wait_send()
    o_copy(1, wo_across_ref, depth, None, zs[0]).wait_send()
    o_copy(2, wo_across_ref, depth, None, zs[1]).wait_send()
    o_copy(3, wo_across_ref, below, 0, zs[0]).wait_send()
    o_copy(4, wo_across_ref, above, 1, zs[1]).wait_send()


def project_in(
    own_rows, gain, w_query, w_key, w_value, w_out, meta, sizes, stretch, selected, ids_col, new_rows,
):
    rows, features = own_rows.shape
    vmem = pl.BlockSpec(memory_space=pltpu.VMEM)
    smem = pl.BlockSpec(memory_space=pltpu.SMEM)
    hbm = pl.BlockSpec(memory_space=pltpu.HBM)
    dma = pltpu.SemaphoreType.DMA
    pairs = [(2,), (2,), (4,), (8,), (4,), (2, 8), (2, 2), (5,), (4, 4)]
    bf16 = jnp.bfloat16
    return pl.pallas_call(
        functools.partial(project_in_kernel, selected, sizes, stretch),
        out_shape=(
            jax.ShapeDtypeStruct((4, new_rows, HEAD), bf16), jax.ShapeDtypeStruct(w_out.shape, bf16)
        ),
        in_specs=[smem] + [vmem] * 3 + [hbm] * 4,
        out_specs=(vmem, hbm),
        scratch_shapes=[
            pltpu.VMEM((AROUND, 2 * rows, features), bf16),
            pltpu.VMEM((4, features, HEAD), bf16),
            pltpu.VMEM((4, 4, 2 * rows, HEAD), bf16),
            pltpu.VMEM(w_query.shape, bf16), pltpu.VMEM(w_key.shape, bf16),
            pltpu.VMEM(w_value.shape, bf16),
            pltpu.VMEM((new_rows // 2, HEAD), jnp.float32),
            pltpu.VMEM((new_rows // 2, HEAD), jnp.float32),
            dma((3,)),
        ] + [dma(shape) for shape in pairs for _ in range(2)],
        compiler_params=pltpu.CompilerParams(
            collective_id=2, has_side_effects=True, vmem_limit_bytes=52 << 20
        ),
        name="project_in",
    )(
        meta, own_rows, gain, ids_col,
        w_query, w_key, w_value, w_out,
    )


def on_device(
    hidden, input_gain, w_query, w_key, w_value, w_out, post_gain, cache_keys, cache_values,
    page_table, stretch_request, recompute_ids, query_counts,
):
    own_rows = hidden[0]
    new_rows = own_rows.shape[0] * lax.axis_size("tok")
    stretch = cache_keys.shape[1]
    owners, counts, ids = stretch_request[0], query_counts[0], recompute_ids[0]
    selected = ids.shape[0]
    padded = jnp.pad(ids, (0, stretch - selected), constant_values=-1)
    ids_col, ids_row = padded[:, None], padded[None, :]
    sizes = (owners.shape[0], counts.shape[0], page_table.shape[0])
    meta = jnp.concatenate([owners, counts, page_table.reshape(-1)])
    heads, w_across = project_in(
        own_rows, input_gain, w_query, w_key, w_value, w_out, meta, sizes, stretch, selected, ids_col,
        new_rows,
    )
    output = project(
        heads, cache_keys, cache_values, meta, sizes, selected, ids_col, ids_row, w_out, w_across, own_rows,
        post_gain,
    )
    return output[None]


def solution(mesh):
    return jax.shard_map(
        on_device,
        mesh=mesh,
        in_specs=(
            P("grp", "tok", None), P(), P(None, "tok"), P(None, "tok"), P(None, "tok"),
            P("tok", None), P(), P("grp", None, "tok"), P("grp", None, "tok"), P(),
            P("grp", None), P("grp", None), P("grp", None),
        ),
        out_specs=P("grp", "tok", None),
        check_vma=False,
    )
```
